32 devices in a mesh: seq: 4 (over y, x), mp: 8 (over z, core).
Axes of the slice: x: 2, y: 2, z: 4, core: 2. Of those that a mesh axis runs over, the one named last changes fastest.
Arguments:
- incoming: bfloat16 [2048, 4096], P('seq', 'mp'), may hold values from -12 to 12
- queries: bfloat16 [2048, 4096], P('seq', 'mp'), may hold values from -5 to 5
- key_vecs: bfloat16 [2048, 4096], P('seq', 'mp'), may hold values from -5 to 5
- value_vecs: bfloat16 [2048, 4096], P('seq', 'mp'), may hold values from -6 to 6
- w_out: bfloat16 [4096, 4096], P(None, 'mp'), may hold values from -0.09375 to 0.09375
- norm_gain: float32 [4096], P('mp'), may hold values from 0.25 to 1.75
- filters: bfloat16 [4096, 256], P('mp'), may hold values from -0.375 to 0.375
- filter_len: int32 [4096], P('mp'), may hold values from 128 to 256, as said below
- skip_gain: float32 [4096], P('mp'), may hold values from 0.5 to 1.5
- slot_map: int32 [8], replicated, may hold values from 0 to 7, as said below
Outputs:
- layer_out: bfloat16 [2048, 4096], P('seq', 'mp')
The draws below stay inside these ranges and needn't reach their ends.
Inputs may be any that keep to these rules, and one draw needn't show every extreme that they name: `slot_map`: slots 2 * i and 2 * i + 1, the rows of index i of seq, hold blocks i and 7 - i, in either order. `filter_len`: some channel uses all 256 taps.
All inputs are finite; a program needn't handle non-finite values.
Results may differ from the reference program's by a relative error of at most 0.0055.
Values may be sent and summed in bfloat16 or wider, within the bound.
No kernel may reach another device: no remote copies, remote signals or barrier semaphores. Data moves between devices by JAX's collectives and lax.ppermute only.
A program may use at most 64 MiB of HBM per device.

```python
import jax
import jax.numpy as jnp
from jax import lax

D = 4096
HD = 128
SPAN = 256
FILT = 256
SPANS = 8
TOKENS = 2048


def draw_slot_map(key, part):
    flips = jax.random.randint(jax.random.fold_in(key, 11), (SPANS // 2,), 0, 2).astype(jnp.int32)
    lower_ids = jnp.arange(SPANS // 2, dtype=jnp.int32)
    upper_ids = SPANS - 1 - lower_ids
    first_ids = jnp.where(flips == 1, upper_ids, lower_ids)
    second_ids = jnp.where(flips == 1, lower_ids, upper_ids)
    return jnp.stack([first_ids, second_ids], axis=1).reshape(SPANS).astype(jnp.int32)


def draw_filter_len(key, part):
    first_key, second_key = jax.random.split(jax.random.fold_in(key, 23))
    lengths = jax.random.randint(first_key, (D,), FILT // 2, FILT + 1)
    chosen = jax.random.randint(second_key, (), 0, D)
    return jnp.where(jnp.arange(D) == chosen, FILT, lengths).astype(jnp.int32)


def draw_incoming(key, part):
    channel = jnp.arange(D, dtype=jnp.float32) / D
    raw_values = jnp.clip(jax.random.normal(jax.random.fold_in(key, 31), (TOKENS, D), jnp.float32), -6.0, 6.0)
    amplitude = 1.0 + channel
    return (raw_values * amplitude[None, :]).astype(jnp.bfloat16)


def query_key_pair(key):
    first_key, second_key = jax.random.split(jax.random.fold_in(key, 47), 2)
    shape = (TOKENS, D)
    query_rows = jnp.clip(1.5 * jax.random.normal(first_key, shape, jnp.float32), -5.0, 5.0)
    key_rows = jnp.clip(1.5 * jax.random.normal(second_key, shape, jnp.float32), -5.0, 5.0)
    return (query_rows, key_rows)


def draw_queries(key, part):
    return query_key_pair(key)[0].astype(jnp.bfloat16)


def draw_key_vecs(key, part):
    return query_key_pair(key)[1].astype(jnp.bfloat16)


def shard_levels(stream_key, extent, cuts, low, high):
    loudness, own = 1.0, jax.random.fold_in(stream_key, 6)
    for dim, shards_of in cuts:
        draws = jnp.exp(jax.random.uniform(jax.random.fold_in(own, dim), (shards_of,), jnp.float32, low / len(cuts), high / len(cuts)))
        loudness = loudness * jnp.repeat(draws, extent[dim] // shards_of).reshape([-1 if axis == dim else 1 for axis in range(len(extent))])
    return loudness


def scatter_about(key, dims, width, limit, cuts=(), kind=jnp.bfloat16):
    drawn = jax.random.normal(key, dims, jnp.float32) * width
    if len(cuts) > 0:
        drawn = shard_levels(key, dims, cuts, -0.22, 0.18) * drawn
    return jnp.clip(drawn, min=-limit, max=limit).astype(kind)


def setup_inputs(seed: int = 0) -> dict:
    key_list = jax.random.split(jax.random.key(seed), 11)
    return {
        "incoming": draw_incoming(jax.random.fold_in(key_list[10], 71), 0),
        "queries": draw_queries(jax.random.fold_in(key_list[10], 71), 0),
        "key_vecs": draw_key_vecs(jax.random.fold_in(key_list[10], 71), 0),
        "value_vecs": scatter_about(key_list[3], (TOKENS, D), 1.0, 6.0, ((0, 4), (1, 8))),
        "w_out": scatter_about(key_list[4], (D, D), D ** -0.5, 0.09375, ((1, 8),)),
        "norm_gain": jnp.clip(1.0 + 0.15 * jax.random.normal(key_list[5], (D,), jnp.float32), 0.25, 1.75),
        "filters": scatter_about(key_list[6], (D, FILT), FILT ** -0.5, 0.375, ((0, 8),)),
        "filter_len": draw_filter_len(jax.random.fold_in(key_list[10], 71), 0),
        "skip_gain": jnp.clip(0.5 + 1.0 * jax.random.uniform(key_list[8], (D,), jnp.float32) ** shard_levels(key_list[8], (D,), ((0, 8),), -0.2, 0.2), 0.5, 1.5),
        "slot_map": draw_slot_map(jax.random.fold_in(key_list[10], 71), 0),
    }


EPS = 1e-05

def toeplitz_table(group_taps, lag_table):
    tap_count = group_taps.shape[1]
    inside = (lag_table >= 0) & (lag_table < tap_count)
    picked = jnp.take(group_taps, jnp.clip(lag_table, 0, tap_count - 1).astype(jnp.int32), axis=1)
    return jnp.where(inside[None, :, :], picked, jnp.zeros((), group_taps.dtype))

def reference(incoming, queries, key_vecs, value_vecs, w_out, norm_gain, filters, filter_len, skip_gain, slot_map):
    row_ids = jnp.arange(TOKENS, dtype=jnp.int32)
    position = (slot_map[row_ids // SPAN] * SPAN + row_ids % SPAN).astype(jnp.int32)
    head_count = D // HD
    block_count = TOKENS // SPAN
    query_split = queries.reshape(TOKENS, head_count, HD).transpose(1, 0, 2)
    key_split = key_vecs.reshape(TOKENS, head_count, HD).transpose(1, 0, 2)
    value_split = value_vecs.reshape(TOKENS, head_count, HD).transpose(1, 0, 2)

    def one_head(operands):
        head_query, head_key, head_value = operands

        def one_block(block):
            block_query, block_pos = block
            scores = jnp.dot(block_query, head_key.T, preferred_element_type=jnp.float32) * HD ** (-0.5)
            allowed = position[None, :] <= block_pos[:, None]
            row_peak = lax.optimization_barrier(jnp.max(jnp.where(allowed, scores, -jnp.inf), axis=1, keepdims=True))
            weights = jnp.where(allowed, jnp.exp(scores - row_peak), 0.0)
            totals = lax.optimization_barrier(jnp.sum(weights, axis=1, keepdims=True))
            numerator = jnp.dot(weights.astype(jnp.bfloat16), head_value, preferred_element_type=jnp.float32)
            return (numerator / totals).astype(jnp.bfloat16)
        blocks_out = lax.map(one_block, (head_query.reshape(block_count, SPAN, HD), position.reshape(block_count, SPAN)))
        return blocks_out.reshape(TOKENS, HD)
    attention = lax.map(one_head, (query_split, key_split, value_split)).transpose(1, 0, 2).reshape(TOKENS, D)
    residual = incoming.astype(jnp.float32) + jnp.dot(attention, w_out, preferred_element_type=jnp.float32)
    mean_square = lax.optimization_barrier(jnp.mean(residual * residual, axis=1, keepdims=True))
    normed = (residual * lax.rsqrt(mean_square + EPS) * norm_gain[None, :]).astype(jnp.bfloat16)
    tap_ids = jnp.arange(FILT, dtype=jnp.int32)
    taps = jnp.where(tap_ids[None, :] < filter_len[:, None], filters, jnp.zeros((), filters.dtype))
    inverse = jnp.zeros((TOKENS,), jnp.int32).at[position].set(row_ids)
    ordered = normed[inverse].reshape(SPANS, SPAN, D)
    before = jnp.concatenate([jnp.zeros((1, SPAN, D), ordered.dtype), ordered[:-1]], axis=0)
    group_count = D // HD
    now_groups = ordered.reshape(SPANS, SPAN, group_count, HD).transpose(2, 0, 1, 3)
    before_groups = before.reshape(SPANS, SPAN, group_count, HD).transpose(2, 0, 1, 3)
    taps_groups = taps.reshape(group_count, HD, FILT)
    lag_now = (jnp.arange(SPAN, dtype=jnp.int32)[:, None] - jnp.arange(SPAN, dtype=jnp.int32)[None, :]).astype(jnp.int32)

    def one_group(operands):
        group_taps, group_now, group_before = operands
        near_matrix = toeplitz_table(group_taps, lag_now).astype(jnp.float32)
        far_matrix = toeplitz_table(group_taps, lag_now + SPAN).astype(jnp.float32)
        near_part = jnp.einsum('cts,nsc->ntc', near_matrix, group_now.astype(jnp.float32), precision=lax.Precision.HIGHEST)
        far_part = jnp.einsum('cts,nsc->ntc', far_matrix, group_before.astype(jnp.float32), precision=lax.Precision.HIGHEST)
        return near_part + far_part
    conv_groups = lax.map(one_group, (taps_groups, now_groups, before_groups))
    conv_natural = conv_groups.transpose(1, 2, 0, 3).reshape(TOKENS, D)
    conv_stored = conv_natural[position]
    layer_out = residual + conv_stored + skip_gain[None, :] * normed.astype(jnp.float32)
    return layer_out.astype(jnp.bfloat16)
```

```python
import functools

import jax
import jax.numpy as jnp
import numpy as np
from jax import lax
from jax.experimental import pallas as pl
from jax.experimental.pallas import tpu as pltpu
from jax.sharding import PartitionSpec as P

HD = 128
EPS = 1e-05
NEG = -1e30
LOG2E = 1.4426950408889634
BF = jnp.bfloat16
F32 = jnp.float32
VMEM = pltpu.VMEM
SMEM = pltpu.SMEM


def shifted(block, axis, distance):
    devices = range(lax.axis_size(axis))
    route = [(i - distance, i) for i in devices if i - distance in devices]
    return lax.ppermute(block, axis, route)


def block_update(running, query_heads, query_pos, key_part, value_part, key_pos):
    peak_now, total_now, accum_now = running
    key_count = key_part.shape[0]
    head_count = query_heads.shape[1]
    key_heads = key_part.reshape(key_count, head_count, HD)
    value_heads = value_part.reshape(key_count, head_count, HD)
    scores = jnp.einsum(
        "thd,shd->ths", query_heads, key_heads, preferred_element_type=F32
    ) * HD ** (-0.5)
    allowed = key_pos[None, None, :] <= query_pos[:, None, None]
    masked = jnp.where(allowed, scores, NEG)
    peak_next = jnp.maximum(peak_now, jnp.max(masked, axis=2))
    weights = jnp.where(allowed, jnp.exp(masked - peak_next[:, :, None]), 0.0)
    factor = jnp.exp(peak_now - peak_next)
    total_next = total_now * factor + jnp.sum(weights, axis=2)
    summed = jnp.einsum(
        "ths,shd->thd", weights.astype(BF), value_heads, preferred_element_type=F32
    )
    return (peak_next, total_next, accum_now * factor[:, :, None] + summed)


def attend_keys(running, query_heads, query_pos, key_part, value_part, key_pos, block_rows):
    block_count = key_part.shape[0] // block_rows

    def attend_advance(state, item):
        return block_update(state, query_heads, query_pos, *item), None

    stacked = (
        key_part.reshape(block_count, block_rows, -1),
        value_part.reshape(block_count, block_rows, -1),
        key_pos.reshape(block_count, block_rows),
    )
    running, _ = lax.scan(attend_advance, running, stacked)
    return running


def causal_window(extended, taps_lag):
    pair_count, twice, width = extended.shape
    length = twice // 2
    tap_count = taps_lag.shape[0]
    inner = int(np.gcd(tap_count, 16))

    def causal_advance(block, accum):
        base = block * inner
        window = lax.dynamic_slice_in_dim(
            extended, length - base - inner + 1, length + inner - 1, 1
        ).astype(F32)
        tap_block = lax.dynamic_slice_in_dim(taps_lag, base, inner, 0).astype(F32)
        for lag in range(inner):
            offset = inner - 1 - lag
            accum = accum + tap_block[lag][None, None, :] * window[:, offset : offset + length]
        return accum

    start = jnp.zeros((pair_count, length, width), F32)
    return lax.fori_loop(0, tap_count // inner, causal_advance, start)


def general_device(
    incoming, queries, key_vecs, value_vecs, w_out, norm_gain, filters, filter_len, skip_gain, slot_map
):
    tok_rows, local_width = queries.shape
    span_rows = tok_rows // 2
    head_count = local_width // HD
    model_width = w_out.shape[0]
    all_rows = slot_map.shape[0] * span_rows
    row_ids = jnp.arange(all_rows, dtype=jnp.int32)
    position = (
        jnp.repeat(slot_map, span_rows, total_repeat_length=all_rows) * span_rows
        + row_ids % span_rows
    )
    seq_rank = lax.axis_index("seq")
    seq_size = lax.axis_size("seq")
    own_pos = lax.dynamic_slice_in_dim(position, seq_rank * tok_rows, tok_rows)
    query_heads = queries.reshape(tok_rows, head_count, HD)
    keys_all = lax.all_gather(key_vecs, "seq", axis=0, tiled=True)
    values_all = lax.all_gather(value_vecs, "seq", axis=0, tiled=True)
    running = attend_keys(
        (
            jnp.full((tok_rows, head_count), NEG, F32),
            jnp.zeros((tok_rows, head_count), F32),
            jnp.zeros((tok_rows, head_count, HD), F32),
        ),
        query_heads,
        own_pos,
        keys_all,
        values_all,
        position,
        2 * tok_rows,
    )
    attention = (running[2] / running[1][:, :, None]).reshape(-1, local_width).astype(BF)
    projected = jnp.dot(
        lax.all_gather(attention, "mp", axis=1, tiled=True), w_out, preferred_element_type=F32
    )
    residual = incoming.astype(F32) + projected
    square_total = lax.psum(jnp.sum(residual * residual, axis=1), "mp")
    scale = lax.rsqrt(square_total / model_width + EPS)
    normed = (residual * scale[:, None] * norm_gain[None, :]).astype(BF)
    tap_count = filters.shape[1]
    taps = jnp.where(
        jnp.arange(tap_count, dtype=jnp.int32)[None, :] < filter_len[:, None],
        filters,
        jnp.zeros((), filters.dtype),
    )
    pair_ids = lax.dynamic_slice_in_dim(slot_map, 2 * seq_rank, 2)
    low_first = pair_ids[0] < pair_ids[1]
    slots = normed.reshape(2, span_rows, local_width)
    low_rows = jnp.where(low_first, slots[0], slots[1])
    high_rows = jnp.where(low_first, slots[1], slots[0])
    own_pair = jnp.stack([low_rows, high_rows])
    low_before = shifted(low_rows, "seq", 1)
    high_before = shifted(high_rows, "seq", -1)
    high_before = jnp.where(seq_rank == seq_size - 1, low_rows, high_before)
    before_pair = jnp.stack([low_before, high_before])
    conv_pair = causal_window(jnp.concatenate([before_pair, own_pair], axis=1), taps.T)
    conv_slots = jnp.where(low_first, conv_pair, conv_pair[::-1])
    conv_rows = conv_slots.reshape(tok_rows, local_width)
    layer_out = residual + conv_rows + skip_gain[None, :] * normed.astype(F32)
    return layer_out.astype(BF)


def params(megabytes=20):
    return pltpu.CompilerParams(vmem_limit_bytes=megabytes << 20)


def cost(flops, moved, exps=0):
    return pl.CostEstimate(flops=int(flops), bytes_accessed=int(moved), transcendentals=int(exps))


def vm():
    return pl.BlockSpec(memory_space=VMEM)


def sm():
    return pl.BlockSpec(memory_space=SMEM)


def xor_route(count, k):
    return [(i, i ^ k) for i in range(count)]


def half_index(slots_ref, ids_ref, high):
    rank = ids_ref[0]
    first_is_high = slots_ref[2 * rank] > slots_ref[2 * rank + 1]
    return jnp.where(first_is_high, 1 - high, high).astype(jnp.int32)


def pack_kernel(n, slots_ref, ids_ref, q_ref, k_ref, v_ref, *outs):
    rank = ids_ref[0]
    rows, width = q_ref.shape
    wide = width // n
    for k in range(n):
        cols = pl.ds(pl.multiple_of((rank ^ k) * wide, wide), wide)
        for a, ref in enumerate((q_ref, k_ref, v_ref)):
            outs[k][a * rows : (a + 1) * rows, :] = ref[:, cols]


def pack(n, high, slots, ids, q, k, v):
    rows, width = q.shape[0] // 2, q.shape[1]
    spec = pl.BlockSpec((rows, width), lambda i, s, d: (half_index(s, d, high), 0))
    piece = jax.ShapeDtypeStruct((3 * rows, width // n), BF)
    return pl.pallas_call(
        functools.partial(pack_kernel, n),
        out_shape=[piece] * n,
        grid_spec=pltpu.PrefetchScalarGridSpec(
            num_scalar_prefetch=2,
            grid=(1,),
            in_specs=[spec] * 3,
            out_specs=[pl.BlockSpec((3 * rows, width // n), lambda i, s, d: (0, 0))] * n,
        ),
        compiler_params=params(),
        cost_estimate=cost(0, 12 * rows * width),
        name="pack_high" if high else "pack_low",
    )(slots, ids, q, k, v)


def attend_kernel(n, high, rows, ids_ref, *refs):
    chunks = 2 if high else 1
    ins = refs[: chunks * n]
    outs = refs[chunks * n : chunks * n + n]
    q_all, k_all, v_all, o_all = refs[chunks * n + n :]
    rank = ids_ref[0]
    wide = outs[0].shape[1]

    def place(block):
        return pl.ds(pl.multiple_of(block * rows, rows), rows)

    for c in range(chunks):
        for k in range(n):
            source = rank ^ k
            block = source if c == 0 else 2 * n - 1 - source
            piece = ins[c * n + k]
            if c == chunks - 1:
                q_all[place(block - c * n), :] = piece[0:rows, :]
            k_all[place(block), :] = piece[rows : 2 * rows, :]
            v_all[place(block), :] = piece[2 * rows : 3 * rows, :]
    base = n if high else 0
    row_id = lax.broadcasted_iota(jnp.int32, (rows, rows), 0)
    col_id = lax.broadcasted_iota(jnp.int32, (rows, rows), 1)
    causal = col_id <= row_id
    factor = HD ** (-0.5) * LOG2E
    nt = (((1,), (1,)), ((), ()))
    for b in range(n):
        past = (base + b) * rows
        for h in range(wide // HD):
            cols = slice(h * HD, (h + 1) * HD)
            q = q_all[b * rows : (b + 1) * rows, cols]
            near = lax.dot_general(
                q, k_all[past : past + rows, cols], nt, preferred_element_type=F32
            )
            near = jnp.where(causal, near, NEG)
            peak = jnp.max(near, axis=1, keepdims=True)
            if past:
                far = lax.dot_general(q, k_all[0:past, cols], nt, preferred_element_type=F32)
                peak = jnp.maximum(peak, jnp.max(far, axis=1, keepdims=True))
            w_near = jnp.exp2((near - peak) * factor)
            total = jnp.sum(w_near, axis=1, keepdims=True)
            summed = jnp.dot(
                w_near.astype(BF), v_all[past : past + rows, cols], preferred_element_type=F32
            )
            if past:
                w_far = jnp.exp2((far - peak) * factor)
                total = total + jnp.sum(w_far, axis=1, keepdims=True)
                summed = summed + jnp.dot(
                    w_far.astype(BF), v_all[0:past, cols], preferred_element_type=F32
                )
            owner = n - 1 - b if high else b
            o_all[owner * rows : (owner + 1) * rows, cols] = (summed / total).astype(BF)
    for k in range(n):
        outs[k][...] = o_all[place(rank ^ k), :]


def attend(n, high, rows, ids, pieces):
    wide = pieces[0].shape[1]
    chunks = 2 if high else 1
    pairs = n * (n + 1) // 2 + (n * n if high else 0)
    area = pairs * rows * rows * (wide // HD)
    return pl.pallas_call(
        functools.partial(attend_kernel, n, high, rows),
        out_shape=[jax.ShapeDtypeStruct((rows, wide), BF)] * n,
        in_specs=[sm()] + [vm()] * len(pieces),
        out_specs=[vm()] * n,
        scratch_shapes=[
            VMEM((n * rows, wide), BF),
            VMEM((chunks * n * rows, wide), BF),
            VMEM((chunks * n * rows, wide), BF),
            VMEM((n * rows, wide), BF),
        ],
        compiler_params=params(32),
        cost_estimate=cost(4 * area * HD, 8 * n * rows * wide * chunks, area),
        name="attend_high" if high else "attend_low",
    )(ids, *pieces)


def project_kernel(n, high, slots_ref, ids_ref, inc_ref, w_ref, *refs):
    parts = refs[:-3]
    res_ref, sq_ref, lhs = refs[-3:]
    rank = ids_ref[0]
    me = ids_ref[1]
    rows = res_ref.shape[0]
    width = lhs.shape[1]
    wide = width // n
    half = half_index(slots_ref, ids_ref, high)
    total = inc_ref[pl.ds(pl.multiple_of(half * rows, rows), rows), :].astype(F32)
    for index, part in enumerate(parts):
        for k in range(n):
            cols = pl.ds(pl.multiple_of((rank ^ k) * wide, wide), wide)
            lhs[:, cols] = part[k * rows : (k + 1) * rows, :]
        depth = pl.ds(pl.multiple_of((me ^ index) * width, width), width)
        total = total + jnp.dot(lhs[...], w_ref[depth, :], preferred_element_type=F32)
    res_ref[...] = total
    squares = total * total
    lanes = squares[:, 0:HD]
    for g in range(1, squares.shape[1] // HD):
        lanes = lanes + squares[:, g * HD : (g + 1) * HD]
    sq_ref[...] = jnp.sum(lanes.T, axis=0, keepdims=True)


def project(n, high, slots, ids, incoming, w_out, parts):
    rows, width = incoming.shape[0] // 2, incoming.shape[1]
    return pl.pallas_call(
        functools.partial(project_kernel, n, high),
        out_shape=[
            jax.ShapeDtypeStruct((rows, width), F32),
            jax.ShapeDtypeStruct((1, rows), F32),
        ],
        in_specs=[sm(), sm()] + [vm()] * (2 + len(parts)),
        out_specs=[vm(), vm()],
        scratch_shapes=[VMEM((rows, width), BF)],
        compiler_params=params(20),
        cost_estimate=cost(2 * rows * width * w_out.shape[0], 2 * w_out.size * 1.5),
        name="project_high" if high else "project_low",
    )(slots, ids, incoming, w_out, *parts)


def normed_rows(res, sq_row, gain, model_width):
    rows, width = res.shape
    scale = lax.rsqrt(sq_row / model_width + EPS)
    column = jnp.broadcast_to(scale, (HD, rows)).T
    parts = [
        (res[:, g * HD : (g + 1) * HD] * column * gain[:, g * HD : (g + 1) * HD]).astype(BF)
        for g in range(width // HD)
    ]
    return jnp.concatenate(parts, axis=1)


def norm_kernel(model_width, res_ref, sq_ref, gain_ref, out_ref):
    out_ref[...] = normed_rows(res_ref[...], sq_ref[...], gain_ref[...], model_width)


def norm(model_width, res, sq, gain, name):
    return pl.pallas_call(
        functools.partial(norm_kernel, model_width),
        out_shape=jax.ShapeDtypeStruct(res.shape, BF),
        in_specs=[vm()] * 3,
        out_specs=vm(),
        compiler_params=params(8),
        cost_estimate=cost(4 * res.size, 6 * res.size),
        name=name,
    )(res, sq, gain)


def split(array):
    high = array.astype(jnp.bfloat16)
    low = (array - high.astype(np.float64)).astype(jnp.bfloat16)
    return high, low


def transform_tables(rows):
    size = 2 * rows
    freq = np.arange(rows)[:, None].astype(np.float64)
    time = np.arange(rows)[None, :].astype(np.float64)
    angle = 2 * np.pi * ((freq * time) % size) / size
    cosine = np.cos(angle)
    sine = -np.sin(angle)
    nyquist = np.where(np.arange(rows) % 2 == 0, 1.0, -1.0)
    sine[0] = nyquist
    forward = np.concatenate([cosine, sine], axis=0)
    late = 2 * np.pi * ((freq * (time + rows)) % size) / size
    back_cos = 2 * np.cos(late)
    back_cos[0] = 1.0
    back_sin = -2 * np.sin(late)
    back_sin[0] = np.where((np.arange(rows) + rows) % 2 == 0, 1.0, -1.0)
    backward = np.concatenate([back_cos, back_sin], axis=0).T / size
    return split(forward), split(backward)


def spectrum_kernel(filters_ref, len_ref, fh_ref, fl_ref, out_ref):
    taps = filters_ref.shape[1]
    lag = lax.broadcasted_iota(jnp.int32, filters_ref.shape, 1)
    used = jnp.where(lag < len_ref[...], filters_ref[...].astype(F32), 0.0).astype(BF)
    nt = (((1,), (1,)), ((), ()))
    fh = fh_ref[:, 0:taps]
    fl = fl_ref[:, 0:taps]
    out_ref[...] = lax.dot_general(fh, used, nt, preferred_element_type=F32) + lax.dot_general(
        fl, used, nt, preferred_element_type=F32
    )


def spectrum(filters, filter_len, forward):
    return pl.pallas_call(
        spectrum_kernel,
        out_shape=jax.ShapeDtypeStruct((forward[0].shape[0], filters.shape[0]), F32),
        in_specs=[vm()] * 4,
        out_specs=vm(),
        compiler_params=params(12),
        cost_estimate=cost(4 * forward[0].size * filters.shape[0], 8 * filters.size),
        name="spectrum",
    )(filters, filter_len.reshape(-1, 1), *forward)


def conv_rows(before, own, fh, fl, gh, gl, spec):
    rows = own.shape[0]

    def two(a_high, a_low, b):
        return jnp.dot(a_high, b, preferred_element_type=F32) + jnp.dot(
            a_low, b, preferred_element_type=F32
        )

    row_id = lax.broadcasted_iota(jnp.int32, (rows, 1), 0)
    sign = jnp.where(row_id % 2 == 0, 1.0, -1.0)
    first = row_id == 0
    spec_b = two(fh, fl, before)
    spec_o = two(fh, fl, own)
    x_re = spec_b[:rows] + sign * spec_o[:rows]
    x_im = spec_b[rows:] + jnp.where(first, 1.0, sign) * spec_o[rows:]
    h_re, h_im = spec[:rows], spec[rows:]
    h_cross = jnp.where(first, 0.0, h_im)
    h_own = jnp.where(first, h_im, h_re)
    y_re = x_re * h_re - x_im * h_cross
    y_im = x_re * h_cross + x_im * h_own
    y = jnp.concatenate([y_re, y_im], axis=0)
    y_high = y.astype(BF)
    y_low = (y - y_high.astype(F32)).astype(BF)
    return two(gh, gl, y_high) + jnp.dot(gh, y_low, preferred_element_type=F32)


def finish(res, normed, conv, skip):
    return (res + conv + skip * normed.astype(F32)).astype(BF)


def conv_low_kernel(res_ref, own_ref, before_ref, spec_ref, skip_ref, fh, fl, gh, gl, out_ref):
    conv = conv_rows(
        before_ref[...], own_ref[...], fh[...], fl[...], gh[...], gl[...], spec_ref[...]
    )
    out_ref[...] = finish(res_ref[...], own_ref[...], conv, skip_ref[...])


def conv_high_kernel(
    n, slots_ref, ids_ref, res_ref, own_ref, before_ref, low_ref, done_ref, spec_ref, skip_ref,
    fh, fl, gh, gl, out_ref,
):
    rows = res_ref.shape[0]
    last = ids_ref[0] == n - 1
    before = jnp.where(last, low_ref[...].astype(F32), before_ref[...].astype(F32)).astype(BF)
    conv = conv_rows(before, own_ref[...], fh[...], fl[...], gh[...], gl[...], spec_ref[...])
    half = half_index(slots_ref, ids_ref, 1)
    out_ref[pl.ds(pl.multiple_of((1 - half) * rows, rows), rows), :] = done_ref[...]
    out_ref[pl.ds(pl.multiple_of(half * rows, rows), rows), :] = finish(
        res_ref[...], own_ref[...], conv, skip_ref[...]
    )


def gather_mp(own, size):
    chips = size // 2
    pieces = [own]
    for k in range(1, chips - 1):
        pieces.append(lax.ppermute(own, "mp", xor_route(size, 2 * k)))
    inner = [(i, i ^ (size - 2)) for i in range(2, size - 2)]
    direct = lax.ppermute(own, "mp", inner)
    ends = [(2, 0), (3, 1), (size - 4, size - 2), (size - 3, size - 1)]
    relayed = lax.ppermute(pieces[chips - 2], "mp", ends)
    pieces.append(direct + relayed)
    parts = []
    for piece in pieces:
        parts.append(piece)
        parts.append(lax.ppermute(piece, "mp", xor_route(size, 1)))
    return parts


def total_mp(part, size):
    k = 1
    while k < size:
        part = part + lax.ppermute(part, "mp", xor_route(size, k))
        k *= 2
    return part


def fast_device(
    incoming, queries, key_vecs, value_vecs, w_out, norm_gain, filters, filter_len, skip_gain, slot_map
):
    n = lax.axis_size("seq")
    mp_size = lax.axis_size("mp")
    rows, width = queries.shape[0] // 2, queries.shape[1]
    model_width = w_out.shape[0]
    ids = jnp.stack([lax.axis_index("seq"), lax.axis_index("mp")]).astype(jnp.int32)
    gain = norm_gain.reshape(1, -1)
    skip = skip_gain.reshape(1, -1)
    forward, backward = transform_tables(rows)
    forward = tuple(jnp.asarray(t) for t in forward)
    backward = tuple(jnp.asarray(t) for t in backward)

    def exchange(pieces):
        return [pieces[0]] + [
            lax.ppermute(pieces[k], "seq", xor_route(n, k)) for k in range(1, n)
        ]

    low = exchange(pack(n, 0, slot_map, ids, queries, key_vecs, value_vecs))
    high = exchange(pack(n, 1, slot_map, ids, queries, key_vecs, value_vecs))
    spec = spectrum(filters, filter_len, forward)

    att_low = exchange(attend(n, 0, rows, ids, low))
    parts_low = gather_mp(jnp.concatenate(att_low, axis=0), mp_size)
    att_high = exchange(attend(n, 1, rows, ids, low + high))
    parts_high = gather_mp(jnp.concatenate(att_high, axis=0), mp_size)

    res_low, sq_low = project(n, 0, slot_map, ids, incoming, w_out, parts_low)
    norm_low = norm(model_width, res_low, total_mp(sq_low, mp_size), gain, "norm_low")
    before_low = shifted(norm_low, "seq", 1)
    done_low = pl.pallas_call(
        conv_low_kernel,
        out_shape=jax.ShapeDtypeStruct((rows, width), BF),
        in_specs=[vm()] * 9,
        out_specs=vm(),
        compiler_params=params(20),
        cost_estimate=cost(14 * rows * rows * width, 12 * rows * width),
        name="conv_low",
    )(res_low, norm_low, before_low, spec, skip, *forward, *backward)

    res_high, sq_high = project(n, 1, slot_map, ids, incoming, w_out, parts_high)
    norm_high = norm(model_width, res_high, total_mp(sq_high, mp_size), gain, "norm_high")
    before_high = shifted(norm_high, "seq", -1)
    return pl.pallas_call(
        functools.partial(conv_high_kernel, n),
        out_shape=jax.ShapeDtypeStruct((2 * rows, width), BF),
        in_specs=[sm(), sm()] + [vm()] * 11,
        out_specs=vm(),
        compiler_params=params(20),
        cost_estimate=cost(14 * rows * rows * width, 12 * rows * width),
        name="conv_high",
    )(
        slot_map, ids, res_high, norm_high, before_high, norm_low, done_low, spec, skip,
        *forward, *backward,
    )


def power_of_two(value):
    return value & (value - 1) == 0


def on_device(*arrays):
    n = lax.axis_size("seq")
    size = lax.axis_size("mp")
    queries, filters = arrays[1], arrays[6]
    rows = queries.shape[0] // 2
    heads = queries.shape[1] // HD
    fits = (
        heads % n == 0
        and power_of_two(n)
        and power_of_two(size)
        and size >= 8
        and rows % 256 == 0
        and filters.shape[1] <= rows
    )
    return (fast_device if fits else general_device)(*arrays)


def solution(mesh):
    placed = (
        P("seq", "mp"),
        P("seq", "mp"),
        P("seq", "mp"),
        P("seq", "mp"),
        P(None, "mp"),
        P("mp"),
        P("mp", None),
        P("mp"),
        P("mp"),
        P(),
    )
    return jax.shard_map(
        on_device, mesh=mesh, in_specs=placed, out_specs=P("seq", "mp"), check_vma=False
    )
```

```python
import functools

import jax
import jax.numpy as jnp
import numpy as np
from jax import lax
from jax.experimental import pallas as pl
from jax.experimental.pallas import tpu as pltpu
from jax.sharding import PartitionSpec as P


HD = 128
EPS = 1e-05
NEG = -1e30
LOG2E = 1.4426950408889634
BF = jnp.bfloat16
F32 = jnp.float32
VMEM = pltpu.VMEM
SMEM = pltpu.SMEM


def shifted(block, axis, distance):
    devices = range(lax.axis_size(axis))
    route = [(i - distance, i) for i in devices if i - distance in devices]
    return lax.ppermute(block, axis, route)


def block_update(running, query_heads, query_pos, key_part, value_part, key_pos):
    peak_now, total_now, accum_now = running
    key_count = key_part.shape[0]
    head_count = query_heads.shape[1]
    key_heads = key_part.reshape(key_count, head_count, HD)
    value_heads = value_part.reshape(key_count, head_count, HD)
    scores = jnp.einsum(
        "thd,shd->ths", query_heads, key_heads, preferred_element_type=F32
    ) * HD ** (-0.5)
    allowed = key_pos[None, None, :] <= query_pos[:, None, None]
    masked = jnp.where(allowed, scores, NEG)
    peak_next = jnp.maximum(peak_now, jnp.max(masked, axis=2))
    weights = jnp.where(allowed, jnp.exp(masked - peak_next[:, :, None]), 0.0)
    factor = jnp.exp(peak_now - peak_next)
    total_next = total_now * factor + jnp.sum(weights, axis=2)
    summed = jnp.einsum(
        "ths,shd->thd", weights.astype(BF), value_heads, preferred_element_type=F32
    )
    return (peak_next, total_next, accum_now * factor[:, :, None] + summed)


def attend_keys(running, query_heads, query_pos, key_part, value_part, key_pos, block_rows):
    block_count = key_part.shape[0] // block_rows

    def attend_advance(state, item):
        return block_update(state, query_heads, query_pos, *item), None

    stacked = (
        key_part.reshape(block_count, block_rows, -1),
        value_part.reshape(block_count, block_rows, -1),
        key_pos.reshape(block_count, block_rows),
    )
    running, _ = lax.scan(attend_advance, running, stacked)
    return running


def causal_window(extended, taps_lag):
    pair_count, twice, width = extended.shape
    length = twice // 2
    tap_count = taps_lag.shape[0]
    inner = int(np.gcd(tap_count, 16))

    def causal_advance(block, accum):
        base = block * inner
        window = lax.dynamic_slice_in_dim(
            extended, length - base - inner + 1, length + inner - 1, 1
        ).astype(F32)
        tap_block = lax.dynamic_slice_in_dim(taps_lag, base, inner, 0).astype(F32)
        for lag in range(inner):
            offset = inner - 1 - lag
            accum = accum + tap_block[lag][None, None, :] * window[:, offset : offset + length]
        return accum

    start = jnp.zeros((pair_count, length, width), F32)
    return lax.fori_loop(0, tap_count // inner, causal_advance, start)


def general_device(
    incoming, queries, key_vecs, value_vecs, w_out, norm_gain, filters, filter_len, skip_gain, slot_map
):
    tok_rows, local_width = queries.shape
    span_rows = tok_rows // 2
    head_count = local_width // HD
    model_width = w_out.shape[0]
    all_rows = slot_map.shape[0] * span_rows
    row_ids = jnp.arange(all_rows, dtype=jnp.int32)
    position = (
        jnp.repeat(slot_map, span_rows, total_repeat_length=all_rows) * span_rows
        + row_ids % span_rows
    )
    seq_rank = lax.axis_index("seq")
    seq_size = lax.axis_size("seq")
    own_pos = lax.dynamic_slice_in_dim(position, seq_rank * tok_rows, tok_rows)
    query_heads = queries.reshape(tok_rows, head_count, HD)
    keys_all = lax.all_gather(key_vecs, "seq", axis=0, tiled=True)
    values_all = lax.all_gather(value_vecs, "seq", axis=0, tiled=True)
    running = attend_keys(
        (
            jnp.full((tok_rows, head_count), NEG, F32),
            jnp.zeros((tok_rows, head_count), F32),
            jnp.zeros((tok_rows, head_count, HD), F32),
        ),
        query_heads,
        own_pos,
        keys_all,
        values_all,
        position,
        2 * tok_rows,
    )
    attention = (running[2] / running[1][:, :, None]).reshape(-1, local_width).astype(BF)
    projected = jnp.dot(
        lax.all_gather(attention, "mp", axis=1, tiled=True), w_out, preferred_element_type=F32
    )
    residual = incoming.astype(F32) + projected
    square_total = lax.psum(jnp.sum(residual * residual, axis=1), "mp")
    scale = lax.rsqrt(square_total / model_width + EPS)
    normed = (residual * scale[:, None] * norm_gain[None, :]).astype(BF)
    tap_count = filters.shape[1]
    taps = jnp.where(
        jnp.arange(tap_count, dtype=jnp.int32)[None, :] < filter_len[:, None],
        filters,
        jnp.zeros((), filters.dtype),
    )
    pair_ids = lax.dynamic_slice_in_dim(slot_map, 2 * seq_rank, 2)
    low_first = pair_ids[0] < pair_ids[1]
    slots = normed.reshape(2, span_rows, local_width)
    low_rows = jnp.where(low_first, slots[0], slots[1])
    high_rows = jnp.where(low_first, slots[1], slots[0])
    own_pair = jnp.stack([low_rows, high_rows])
    low_before = shifted(low_rows, "seq", 1)
    high_before = shifted(high_rows, "seq", -1)
    high_before = jnp.where(seq_rank == seq_size - 1, low_rows, high_before)
    before_pair = jnp.stack([low_before, high_before])
    conv_pair = causal_window(jnp.concatenate([before_pair, own_pair], axis=1), taps.T)
    conv_slots = jnp.where(low_first, conv_pair, conv_pair[::-1])
    conv_rows = conv_slots.reshape(tok_rows, local_width)
    layer_out = residual + conv_rows + skip_gain[None, :] * normed.astype(F32)
    return layer_out.astype(BF)


def params(megabytes=20):
    return pltpu.CompilerParams(vmem_limit_bytes=megabytes << 20)


def cost(flops, moved, exps=0):
    return pl.CostEstimate(flops=int(flops), bytes_accessed=int(moved), transcendentals=int(exps))


def vm():
    return pl.BlockSpec(memory_space=VMEM)


def sm():
    return pl.BlockSpec(memory_space=SMEM)


def xor_route(count, k):
    return [(i, i ^ k) for i in range(count)]


def half_index(slots_ref, ids_ref, high):
    rank = ids_ref[0]
    first_is_high = slots_ref[2 * rank] > slots_ref[2 * rank + 1]
    return jnp.where(first_is_high, 1 - high, high).astype(jnp.int32)


def pack_kernel(n, high, slots_ref, ids_ref, q_ref, k_ref, v_ref, *rest):
    outs, sem = rest[:n], rest[n]
    rank = ids_ref[0]
    rows = outs[0].shape[0] // 3
    wide = outs[0].shape[1]
    half = half_index(slots_ref, ids_ref, high)
    source_rows = pl.ds(pl.multiple_of(half * rows, rows), rows)
    copies = []
    for k in range(n):
        cols = pl.ds(pl.multiple_of((rank ^ k) * wide, wide), wide)
        for a, ref in enumerate((q_ref, k_ref, v_ref)):
            copy = pltpu.make_async_copy(
                ref.at[source_rows, cols],
                outs[k].at[a * rows : (a + 1) * rows, :],
                sem.at[k, a],
            )
            copy.start()
            copies.append(copy)
    for copy in copies:
        copy.wait()


def pack(n, high, slots, ids, q, k, v):
    rows, width = q.shape[0] // 2, q.shape[1]
    piece = jax.ShapeDtypeStruct((3 * rows, width // n), BF)
    return pl.pallas_call(
        functools.partial(pack_kernel, n, high),
        out_shape=[piece] * n,
        in_specs=[sm(), sm()] + [pl.BlockSpec(memory_space=pltpu.HBM)] * 3,
        out_specs=[vm()] * n,
        scratch_shapes=[pltpu.SemaphoreType.DMA((n, 3))],
        compiler_params=params(8),
        cost_estimate=cost(0, 12 * rows * width),
        name="pack_high" if high else "pack_low",
    )(slots, ids, q, k, v)


def attend_kernel(n, high, rows, ids_ref, *refs):
    chunks = 2 if high else 1
    ins = refs[: chunks * n]
    outs = refs[chunks * n : chunks * n + n]
    q_all, k_all, v_all, o_all = refs[chunks * n + n :]
    rank = ids_ref[0]
    wide = outs[0].shape[1]

    def place(block):
        return pl.ds(pl.multiple_of(block * rows, rows), rows)

    for c in range(chunks):
        for k in range(n):
            source = rank ^ k
            block = source if c == 0 else 2 * n - 1 - source
            piece = ins[c * n + k]
            if c == chunks - 1:
                q_all[place(block - c * n), :] = piece[0:rows, :]
            k_all[place(block), :] = piece[rows : 2 * rows, :]
            v_all[place(block), :] = piece[2 * rows : 3 * rows, :]
    base = n if high else 0
    row_id = lax.broadcasted_iota(jnp.int32, (rows, rows), 0)
    col_id = lax.broadcasted_iota(jnp.int32, (rows, rows), 1)
    causal = col_id <= row_id
    factor = HD ** (-0.5) * LOG2E
    nt = (((1,), (1,)), ((), ()))
    for b in range(n):
        past = (base + b) * rows
        for h in range(wide // HD):
            cols = slice(h * HD, (h + 1) * HD)
            q = q_all[b * rows : (b + 1) * rows, cols]
            near = lax.dot_general(
                q, k_all[past : past + rows, cols], nt, preferred_element_type=F32
            )
            near = jnp.where(causal, near, NEG)
            peak = jnp.max(near, axis=1, keepdims=True)
            if past:
                far = lax.dot_general(q, k_all[0:past, cols], nt, preferred_element_type=F32)
                peak = jnp.maximum(peak, jnp.max(far, axis=1, keepdims=True))
            w_near = jnp.exp2((near - peak) * factor)
            total = jnp.sum(w_near, axis=1, keepdims=True)
            summed = jnp.dot(
                w_near.astype(BF), v_all[past : past + rows, cols], preferred_element_type=F32
            )
            if past:
                w_far = jnp.exp2((far - peak) * factor)
                total = total + jnp.sum(w_far, axis=1, keepdims=True)
                summed = summed + jnp.dot(
                    w_far.astype(BF), v_all[0:past, cols], preferred_element_type=F32
                )
            owner = n - 1 - b if high else b
            o_all[owner * rows : (owner + 1) * rows, cols] = (summed / total).astype(BF)
    for k in range(n):
        outs[k][...] = o_all[place(rank ^ k), :]


def attend(n, high, rows, ids, pieces):
    wide = pieces[0].shape[1]
    chunks = 2 if high else 1
    pairs = n * (n + 1) // 2 + (n * n if high else 0)
    area = pairs * rows * rows * (wide // HD)
    return pl.pallas_call(
        functools.partial(attend_kernel, n, high, rows),
        out_shape=[jax.ShapeDtypeStruct((rows, wide), BF)] * n,
        in_specs=[sm()] + [vm()] * len(pieces),
        out_specs=[vm()] * n,
        scratch_shapes=[
            VMEM((n * rows, wide), BF),
            VMEM((chunks * n * rows, wide), BF),
            VMEM((chunks * n * rows, wide), BF),
            VMEM((n * rows, wide), BF),
        ],
        compiler_params=params(32),
        cost_estimate=cost(4 * area * HD, 8 * n * rows * wide * chunks, area),
        name="attend_high" if high else "attend_low",
    )(ids, *pieces)


def project_kernel(n, high, slots_ref, ids_ref, inc_ref, w_ref, *refs):
    parts = refs[:-4]
    res_ref, raw_ref, sq_ref, lhs = refs[-4:]
    rank = ids_ref[0]
    me = ids_ref[1]
    rows = res_ref.shape[0]
    width = lhs.shape[1]
    wide = width // n
    half = half_index(slots_ref, ids_ref, high)
    total = inc_ref[pl.ds(pl.multiple_of(half * rows, rows), rows), :].astype(F32)
    for index, part in enumerate(parts):
        for k in range(n):
            cols = pl.ds(pl.multiple_of((rank ^ k) * wide, wide), wide)
            lhs[:, cols] = part[k * rows : (k + 1) * rows, :]
        depth = pl.ds(pl.multiple_of((me ^ index) * width, width), width)
        total = total + jnp.dot(lhs[...], w_ref[depth, :], preferred_element_type=F32)
    res_ref[...] = total
    raw_ref[...] = total.astype(BF)
    squares = total * total
    lanes = squares[:, 0:HD]
    for g in range(1, squares.shape[1] // HD):
        lanes = lanes + squares[:, g * HD : (g + 1) * HD]
    sq_ref[...] = jnp.sum(lanes.T, axis=0, keepdims=True)


def project(n, high, slots, ids, incoming, w_out, parts):
    rows, width = incoming.shape[0] // 2, incoming.shape[1]
    return pl.pallas_call(
        functools.partial(project_kernel, n, high),
        out_shape=[
            jax.ShapeDtypeStruct((rows, width), F32),
            jax.ShapeDtypeStruct((rows, width), BF),
            jax.ShapeDtypeStruct((1, rows), F32),
        ],
        in_specs=[sm(), sm()] + [vm()] * (2 + len(parts)),
        out_specs=[vm()] * 3,
        scratch_shapes=[VMEM((rows, width), BF)],
        compiler_params=params(20),
        cost_estimate=cost(2 * rows * width * w_out.shape[0], 2 * w_out.size * 1.5),
        name="project_high" if high else "project_low",
    )(slots, ids, incoming, w_out, *parts)


def normed_rows(res, sq_row, gain, model_width):
    rows, width = res.shape
    scale = lax.rsqrt(sq_row / model_width + EPS)
    column = jnp.broadcast_to(scale, (HD, rows)).T
    parts = [
        (res[:, g * HD : (g + 1) * HD] * column * gain[:, g * HD : (g + 1) * HD]).astype(BF)
        for g in range(width // HD)
    ]
    return jnp.concatenate(parts, axis=1)


def norm_kernel(model_width, res_ref, sq_ref, gain_ref, out_ref):
    out_ref[...] = normed_rows(res_ref[...], sq_ref[...], gain_ref[...], model_width)


def norm(model_width, res, sq, gain):
    return pl.pallas_call(
        functools.partial(norm_kernel, model_width),
        out_shape=jax.ShapeDtypeStruct(res.shape, BF),
        in_specs=[vm()] * 3,
        out_specs=vm(),
        compiler_params=params(8),
        cost_estimate=cost(4 * res.size, 6 * res.size),
    )(res, sq, gain)


def split(array):
    high = array.astype(jnp.bfloat16)
    low = (array - high.astype(np.float64)).astype(jnp.bfloat16)
    return high, low


def transform_tables(rows):
    size = 2 * rows
    freq = np.arange(rows)[:, None].astype(np.float64)
    time = np.arange(rows)[None, :].astype(np.float64)
    angle = 2 * np.pi * ((freq * time) % size) / size
    cosine = np.cos(angle)
    sine = -np.sin(angle)
    nyquist = np.where(np.arange(rows) % 2 == 0, 1.0, -1.0)
    sine[0] = nyquist
    forward = np.concatenate([cosine, sine], axis=0)
    late = 2 * np.pi * ((freq * (time + rows)) % size) / size
    back_cos = 2 * np.cos(late)
    back_cos[0] = 1.0
    back_sin = -2 * np.sin(late)
    back_sin[0] = np.where((np.arange(rows) + rows) % 2 == 0, 1.0, -1.0)
    backward = np.concatenate([back_cos, back_sin], axis=0).T / size
    return split(forward), split(backward)


def spectrum_kernel(filters_ref, len_ref, fh_ref, fl_ref, out_ref):
    taps = filters_ref.shape[1]
    lag = lax.broadcasted_iota(jnp.int32, filters_ref.shape, 1)
    used = jnp.where(lag < len_ref[...], filters_ref[...].astype(F32), 0.0).astype(BF)
    nt = (((1,), (1,)), ((), ()))
    fh = fh_ref[:, 0:taps]
    fl = fl_ref[:, 0:taps]
    out_ref[...] = lax.dot_general(fh, used, nt, preferred_element_type=F32) + lax.dot_general(
        fl, used, nt, preferred_element_type=F32
    )


def spectrum(filters, filter_len, forward):
    return pl.pallas_call(
        spectrum_kernel,
        out_shape=jax.ShapeDtypeStruct((forward[0].shape[0], filters.shape[0]), F32),
        in_specs=[vm()] * 4,
        out_specs=vm(),
        compiler_params=params(12),
        cost_estimate=cost(4 * forward[0].size * filters.shape[0], 8 * filters.size),
        name="spectrum",
    )(filters, filter_len.reshape(-1, 1), *forward)


def conv_rows(before, own, fh, fl, gh, gl, spec):
    rows = own.shape[0]

    def two(a_high, a_low, b):
        return jnp.dot(a_high, b, preferred_element_type=F32) + jnp.dot(
            a_low, b, preferred_element_type=F32
        )

    row_id = lax.broadcasted_iota(jnp.int32, (rows, 1), 0)
    sign = jnp.where(row_id % 2 == 0, 1.0, -1.0)
    first = row_id == 0
    spec_b = two(fh, fl, before)
    spec_o = two(fh, fl, own)
    x_re = spec_b[:rows] + sign * spec_o[:rows]
    x_im = spec_b[rows:] + jnp.where(first, 1.0, sign) * spec_o[rows:]
    h_re, h_im = spec[:rows], spec[rows:]
    h_cross = jnp.where(first, 0.0, h_im)
    h_own = jnp.where(first, h_im, h_re)
    y_re = x_re * h_re - x_im * h_cross
    y_im = x_re * h_cross + x_im * h_own
    y = jnp.concatenate([y_re, y_im], axis=0)
    y_high = y.astype(BF)
    y_low = (y - y_high.astype(F32)).astype(BF)
    return two(gh, gl, y_high) + jnp.dot(gh, y_low, preferred_element_type=F32)


def finish(res, normed, conv, skip):
    return (res + conv + skip * normed.astype(F32)).astype(BF)


def conv_low_kernel(res_ref, own_ref, before_ref, spec_ref, skip_ref, fh, fl, gh, gl, out_ref):
    conv = conv_rows(
        before_ref[...], own_ref[...], fh[...], fl[...], gh[...], gl[...], spec_ref[...]
    )
    out_ref[...] = finish(res_ref[...], own_ref[...], conv, skip_ref[...])


def conv_high_kernel(
    n, model_width, slots_ref, ids_ref, res_ref, sq_ref, raw_ref, raw_sq_ref, low_ref, done_ref,
    spec_ref, gain_ref, skip_ref, fh, fl, gh, gl, out_ref,
):
    rows = res_ref.shape[0]
    last = ids_ref[0] == n - 1
    own = normed_rows(res_ref[...], sq_ref[...], gain_ref[...], model_width)
    raw = normed_rows(raw_ref[...].astype(F32), raw_sq_ref[...], gain_ref[...], model_width)
    before = jnp.where(last, low_ref[...].astype(F32), raw.astype(F32)).astype(BF)
    conv = conv_rows(before, own, fh[...], fl[...], gh[...], gl[...], spec_ref[...])
    half = half_index(slots_ref, ids_ref, 1)
    out_ref[pl.ds(pl.multiple_of((1 - half) * rows, rows), rows), :] = done_ref[...]
    out_ref[pl.ds(pl.multiple_of(half * rows, rows), rows), :] = finish(
        res_ref[...], own, conv, skip_ref[...]
    )


def moved(block, axis, route):
    return lax.ppermute(block, axis, route)


def gather_mp(own, size):
    chips = size // 2
    pieces = [own]
    for k in range(1, chips - 1):
        pieces.append(moved(own, "mp", xor_route(size, 2 * k)))
    inner = [(i, i ^ (size - 2)) for i in range(2, size - 2)]
    direct = moved(own, "mp", inner)
    ends = [(2, 0), (3, 1), (size - 4, size - 2), (size - 3, size - 1)]
    relayed = moved(pieces[chips - 2], "mp", ends)
    pieces.append(direct + relayed)
    parts = []
    for piece in pieces:
        parts.append(piece)
        parts.append(moved(piece, "mp", xor_route(size, 1)))
    return parts


def total_mp(part, size):
    k = 1
    while k < size:
        part = part + moved(part, "mp", xor_route(size, k))
        k *= 2
    return part


def before_rows(block, distance):
    devices = range(lax.axis_size("seq"))
    return moved(block, "seq", [(i - distance, i) for i in devices if i - distance in devices])


def fast_device(
    incoming, queries, key_vecs, value_vecs, w_out, norm_gain, filters, filter_len, skip_gain, slot_map
):
    n = lax.axis_size("seq")
    mp_size = lax.axis_size("mp")
    rows, width = queries.shape[0] // 2, queries.shape[1]
    model_width = w_out.shape[0]
    ids = jnp.stack([lax.axis_index("seq"), lax.axis_index("mp")]).astype(jnp.int32)
    gain = norm_gain.reshape(1, -1)
    skip = skip_gain.reshape(1, -1)
    forward, backward = transform_tables(rows)
    forward = tuple(jnp.asarray(t) for t in forward)
    backward = tuple(jnp.asarray(t) for t in backward)

    def exchange(pieces):
        return [pieces[0]] + [moved(pieces[k], "seq", xor_route(n, k)) for k in range(1, n)]

    low = exchange(pack(n, 0, slot_map, ids, queries, key_vecs, value_vecs))
    high = exchange(pack(n, 1, slot_map, ids, queries, key_vecs, value_vecs))
    spec = spectrum(filters, filter_len, forward)

    att_low = exchange(attend(n, 0, rows, ids, low))
    parts_low = gather_mp(jnp.concatenate(att_low, axis=0), mp_size)
    att_high = exchange(attend(n, 1, rows, ids, low + high))
    parts_high = gather_mp(jnp.concatenate(att_high, axis=0), mp_size)

    res_low, _, sq_low = project(n, 0, slot_map, ids, incoming, w_out, parts_low)
    norm_low = norm(model_width, res_low, total_mp(sq_low, mp_size), gain)
    before_low = before_rows(norm_low, 1)
    done_low = pl.pallas_call(
        conv_low_kernel,
        out_shape=jax.ShapeDtypeStruct((rows, width), BF),
        in_specs=[vm()] * 9,
        out_specs=vm(),
        compiler_params=params(20),
        cost_estimate=cost(14 * rows * rows * width, 12 * rows * width),
        name="conv_low",
    )(res_low, norm_low, before_low, spec, skip, *forward, *backward)

    res_high, raw_high, sq_high = project(n, 1, slot_map, ids, incoming, w_out, parts_high)
    raw_before = before_rows(raw_high, -1)
    sq_high = total_mp(sq_high, mp_size)
    sq_before = before_rows(sq_high, -1)
    return pl.pallas_call(
        functools.partial(conv_high_kernel, n, model_width),
        out_shape=jax.ShapeDtypeStruct((2 * rows, width), BF),
        in_specs=[sm(), sm()] + [vm()] * 13,
        out_specs=vm(),
        compiler_params=params(20),
        cost_estimate=cost(14 * rows * rows * width, 12 * rows * width),
        name="conv_high",
    )(
        slot_map, ids, res_high, sq_high, raw_before, sq_before, norm_low, done_low, spec, gain,
        skip, *forward, *backward,
    )


def power_of_two(value):
    return value & (value - 1) == 0


def on_device(*arrays):
    n = lax.axis_size("seq")
    size = lax.axis_size("mp")
    queries, filters = arrays[1], arrays[6]
    rows = queries.shape[0] // 2
    heads = queries.shape[1] // HD
    fits = (
        heads % n == 0
        and power_of_two(n)
        and power_of_two(size)
        and size >= 8
        and rows % 256 == 0
        and filters.shape[1] <= rows
    )
    if not fits:
        return general_device(*arrays)
    return fast_device(*arrays)


def solution(mesh):
    placed = (
        P("seq", "mp"),
        P("seq", "mp"),
        P("seq", "mp"),
        P("seq", "mp"),
        P(None, "mp"),
        P("mp"),
        P("mp", None),
        P("mp"),
        P("mp"),
        P(),
    )
    return jax.shard_map(
        on_device, mesh=mesh, in_specs=placed, out_specs=P("seq", "mp"), check_vma=False
    )
```

```python
import functools

import jax
import jax.numpy as jnp
import numpy as np
from jax import lax
from jax.experimental import pallas as pl
from jax.experimental.pallas import tpu as pltpu
from jax.sharding import PartitionSpec as P


HD = 128
EPS = 1e-05
NEG = -1e30
LOG2E = 1.4426950408889634
BF = jnp.bfloat16
F32 = jnp.float32
VMEM = pltpu.VMEM
SMEM = pltpu.SMEM


def shifted(block, axis, distance):
    devices = range(lax.axis_size(axis))
    route = [(i - distance, i) for i in devices if i - distance in devices]
    return lax.ppermute(block, axis, route)


def block_update(running, query_heads, query_pos, key_part, value_part, key_pos):
    peak_now, total_now, accum_now = running
    key_count = key_part.shape[0]
    head_count = query_heads.shape[1]
    key_heads = key_part.reshape(key_count, head_count, HD)
    value_heads = value_part.reshape(key_count, head_count, HD)
    scores = jnp.einsum(
        "thd,shd->ths", query_heads, key_heads, preferred_element_type=F32
    ) * HD ** (-0.5)
    allowed = key_pos[None, None, :] <= query_pos[:, None, None]
    masked = jnp.where(allowed, scores, NEG)
    peak_next = jnp.maximum(peak_now, jnp.max(masked, axis=2))
    weights = jnp.where(allowed, jnp.exp(masked - peak_next[:, :, None]), 0.0)
    factor = jnp.exp(peak_now - peak_next)
    total_next = total_now * factor + jnp.sum(weights, axis=2)
    summed = jnp.einsum(
        "ths,shd->thd", weights.astype(BF), value_heads, preferred_element_type=F32
    )
    return (peak_next, total_next, accum_now * factor[:, :, None] + summed)


def attend_keys(running, query_heads, query_pos, key_part, value_part, key_pos, block_rows):
    block_count = key_part.shape[0] // block_rows

    def attend_advance(state, item):
        return block_update(state, query_heads, query_pos, *item), None

    stacked = (
        key_part.reshape(block_count, block_rows, -1),
        value_part.reshape(block_count, block_rows, -1),
        key_pos.reshape(block_count, block_rows),
    )
    running, _ = lax.scan(attend_advance, running, stacked)
    return running


def causal_window(extended, taps_lag):
    pair_count, twice, width = extended.shape
    length = twice // 2
    tap_count = taps_lag.shape[0]
    inner = int(np.gcd(tap_count, 16))

    def causal_advance(block, accum):
        base = block * inner
        window = lax.dynamic_slice_in_dim(
            extended, length - base - inner + 1, length + inner - 1, 1
        ).astype(F32)
        tap_block = lax.dynamic_slice_in_dim(taps_lag, base, inner, 0).astype(F32)
        for lag in range(inner):
            offset = inner - 1 - lag
            accum = accum + tap_block[lag][None, None, :] * window[:, offset : offset + length]
        return accum

    start = jnp.zeros((pair_count, length, width), F32)
    return lax.fori_loop(0, tap_count // inner, causal_advance, start)


def general_device(
    incoming, queries, key_vecs, value_vecs, w_out, norm_gain, filters, filter_len, skip_gain, slot_map
):
    tok_rows, local_width = queries.shape
    span_rows = tok_rows // 2
    head_count = local_width // HD
    model_width = w_out.shape[0]
    all_rows = slot_map.shape[0] * span_rows
    row_ids = jnp.arange(all_rows, dtype=jnp.int32)
    position = (
        jnp.repeat(slot_map, span_rows, total_repeat_length=all_rows) * span_rows
        + row_ids % span_rows
    )
    seq_rank = lax.axis_index("seq")
    seq_size = lax.axis_size("seq")
    own_pos = lax.dynamic_slice_in_dim(position, seq_rank * tok_rows, tok_rows)
    query_heads = queries.reshape(tok_rows, head_count, HD)
    keys_all = lax.all_gather(key_vecs, "seq", axis=0, tiled=True)
    values_all = lax.all_gather(value_vecs, "seq", axis=0, tiled=True)
    running = attend_keys(
        (
            jnp.full((tok_rows, head_count), NEG, F32),
            jnp.zeros((tok_rows, head_count), F32),
            jnp.zeros((tok_rows, head_count, HD), F32),
        ),
        query_heads,
        own_pos,
        keys_all,
        values_all,
        position,
        2 * tok_rows,
    )
    attention = (running[2] / running[1][:, :, None]).reshape(-1, local_width).astype(BF)
    projected = jnp.dot(
        lax.all_gather(attention, "mp", axis=1, tiled=True), w_out, preferred_element_type=F32
    )
    residual = incoming.astype(F32) + projected
    square_total = lax.psum(jnp.sum(residual * residual, axis=1), "mp")
    scale = lax.rsqrt(square_total / model_width + EPS)
    normed = (residual * scale[:, None] * norm_gain[None, :]).astype(BF)
    tap_count = filters.shape[1]
    taps = jnp.where(
        jnp.arange(tap_count, dtype=jnp.int32)[None, :] < filter_len[:, None],
        filters,
        jnp.zeros((), filters.dtype),
    )
    pair_ids = lax.dynamic_slice_in_dim(slot_map, 2 * seq_rank, 2)
    low_first = pair_ids[0] < pair_ids[1]
    slots = normed.reshape(2, span_rows, local_width)
    low_rows = jnp.where(low_first, slots[0], slots[1])
    high_rows = jnp.where(low_first, slots[1], slots[0])
    own_pair = jnp.stack([low_rows, high_rows])
    low_before = shifted(low_rows, "seq", 1)
    high_before = shifted(high_rows, "seq", -1)
    high_before = jnp.where(seq_rank == seq_size - 1, low_rows, high_before)
    before_pair = jnp.stack([low_before, high_before])
    conv_pair = causal_window(jnp.concatenate([before_pair, own_pair], axis=1), taps.T)
    conv_slots = jnp.where(low_first, conv_pair, conv_pair[::-1])
    conv_rows = conv_slots.reshape(tok_rows, local_width)
    layer_out = residual + conv_rows + skip_gain[None, :] * normed.astype(F32)
    return layer_out.astype(BF)


def params(megabytes=20):
    return pltpu.CompilerParams(vmem_limit_bytes=megabytes << 20)


def cost(flops, moved, exps=0):
    return pl.CostEstimate(flops=int(flops), bytes_accessed=int(moved), transcendentals=int(exps))


def vm():
    return pl.BlockSpec(memory_space=VMEM)


def sm():
    return pl.BlockSpec(memory_space=SMEM)


def xor_route(count, k):
    return [(i, i ^ k) for i in range(count)]


def half_index(slots_ref, ids_ref, high):
    rank = ids_ref[0]
    first_is_high = slots_ref[2 * rank] > slots_ref[2 * rank + 1]
    return jnp.where(first_is_high, 1 - high, high).astype(jnp.int32)


def pack_kernel(n, slots_ref, ids_ref, q_ref, k_ref, v_ref, *rest):
    outs, sem = rest[: 2 * n], rest[2 * n]
    rank = ids_ref[0]
    rows = outs[0].shape[0] // 3
    wide = outs[0].shape[1]
    copies = []
    for high in range(2):
        half = half_index(slots_ref, ids_ref, high)
        source_rows = pl.ds(pl.multiple_of(half * rows, rows), rows)
        for k in range(n):
            cols = pl.ds(pl.multiple_of((rank ^ k) * wide, wide), wide)
            for a, ref in enumerate((q_ref, k_ref, v_ref)):
                copy = pltpu.make_async_copy(
                    ref.at[source_rows, cols],
                    outs[high * n + k].at[a * rows : (a + 1) * rows, :],
                    sem.at[high * n + k, a],
                )
                copy.start()
                copies.append(copy)
    for copy in copies:
        copy.wait()


def pack(n, slots, ids, q, k, v):
    rows, width = q.shape[0] // 2, q.shape[1]
    piece = jax.ShapeDtypeStruct((3 * rows, width // n), BF)
    packed = pl.pallas_call(
        functools.partial(pack_kernel, n),
        out_shape=[piece] * (2 * n),
        in_specs=[sm(), sm()] + [pl.BlockSpec(memory_space=pltpu.HBM)] * 3,
        out_specs=[vm()] * (2 * n),
        scratch_shapes=[pltpu.SemaphoreType.DMA((2 * n, 3))],
        compiler_params=params(8),
        cost_estimate=cost(0, 24 * rows * width),
        name="pack",
    )(slots, ids, *(pltpu.with_memory_space_constraint(x, pltpu.HBM) for x in (q, k, v)))
    return packed[:n], packed[n:]


def attend_kernel(n, high, rows, ids_ref, *refs):
    chunks = 2 if high else 1
    ins = refs[: chunks * n]
    outs = refs[chunks * n : chunks * n + n]
    q_all, k_all, v_all, o_all = refs[chunks * n + n :]
    rank = ids_ref[0]
    wide = outs[0].shape[1]

    def place(block):
        return pl.ds(pl.multiple_of(block * rows, rows), rows)

    for c in range(chunks):
        for k in range(n):
            source = rank ^ k
            block = source if c == 0 else 2 * n - 1 - source
            piece = ins[c * n + k]
            if c == chunks - 1:
                q_all[place(block - c * n), :] = piece[0:rows, :]
            k_all[place(block), :] = piece[rows : 2 * rows, :]
            v_all[place(block), :] = piece[2 * rows : 3 * rows, :]
    base = n if high else 0
    row_id = lax.broadcasted_iota(jnp.int32, (rows, rows), 0)
    col_id = lax.broadcasted_iota(jnp.int32, (rows, rows), 1)
    causal = col_id <= row_id
    factor = HD ** (-0.5) * LOG2E
    nt = (((1,), (1,)), ((), ()))
    for b in range(n):
        past = (base + b) * rows
        for h in range(wide // HD):
            cols = slice(h * HD, (h + 1) * HD)
            q = q_all[b * rows : (b + 1) * rows, cols]
            near = lax.dot_general(
                q, k_all[past : past + rows, cols], nt, preferred_element_type=F32
            )
            near = jnp.where(causal, near, NEG)
            peak = jnp.max(near, axis=1, keepdims=True)
            if past:
                far = lax.dot_general(q, k_all[0:past, cols], nt, preferred_element_type=F32)
                peak = jnp.maximum(peak, jnp.max(far, axis=1, keepdims=True))
            w_near = jnp.exp2((near - peak) * factor)
            total = jnp.sum(w_near, axis=1, keepdims=True)
            summed = jnp.dot(
                w_near.astype(BF), v_all[past : past + rows, cols], preferred_element_type=F32
            )
            if past:
                w_far = jnp.exp2((far - peak) * factor)
                total = total + jnp.sum(w_far, axis=1, keepdims=True)
                summed = summed + jnp.dot(
                    w_far.astype(BF), v_all[0:past, cols], preferred_element_type=F32
                )
            owner = n - 1 - b if high else b
            o_all[owner * rows : (owner + 1) * rows, cols] = (summed / total).astype(BF)
    for k in range(n):
        outs[k][...] = o_all[place(rank ^ k), :]


def attend(n, high, rows, ids, pieces):
    wide = pieces[0].shape[1]
    chunks = 2 if high else 1
    pairs = n * (n + 1) // 2 + (n * n if high else 0)
    area = pairs * rows * rows * (wide // HD)
    return pl.pallas_call(
        functools.partial(attend_kernel, n, high, rows),
        out_shape=[jax.ShapeDtypeStruct((rows, wide), BF)] * n,
        in_specs=[sm()] + [vm()] * len(pieces),
        out_specs=[vm()] * n,
        scratch_shapes=[
            VMEM((n * rows, wide), BF),
            VMEM((chunks * n * rows, wide), BF),
            VMEM((chunks * n * rows, wide), BF),
            VMEM((n * rows, wide), BF),
        ],
        compiler_params=params(32),
        cost_estimate=cost(4 * area * HD, 8 * n * rows * wide * chunks, area),
        name="attend_high" if high else "attend_low",
    )(ids, *pieces)


def project_kernel(n, high, indices, slots_ref, ids_ref, base_ref, w_ref, *refs):
    count = len(indices)
    parts, outs, lhs = refs[:count], refs[count:-1], refs[-1]
    rank = ids_ref[0]
    me = ids_ref[1]
    rows, width = lhs.shape
    wide = width // n
    if base_ref.shape[0] == rows:
        total = base_ref[...]
    else:
        half = half_index(slots_ref, ids_ref, high)
        total = base_ref[pl.ds(pl.multiple_of(half * rows, rows), rows), :].astype(F32)
    for index, part in zip(indices, parts):
        for k in range(n):
            cols = pl.ds(pl.multiple_of((rank ^ k) * wide, wide), wide)
            lhs[:, cols] = part[k * rows : (k + 1) * rows, :]
        depth = pl.ds(pl.multiple_of((me ^ index) * width, width), width)
        total = total + jnp.dot(lhs[...], w_ref[depth, :], preferred_element_type=F32)
    outs[0][...] = total
    if len(outs) == 1:
        return
    outs[1][...] = total.astype(BF)
    squares = total * total
    lanes = squares[:, 0:HD]
    for g in range(1, squares.shape[1] // HD):
        lanes = lanes + squares[:, g * HD : (g + 1) * HD]
    outs[2][...] = jnp.sum(lanes.T, axis=0, keepdims=True)


def project(n, high, slots, ids, base, w_out, parts, indices, final):
    rows = parts[0].shape[0] // n
    width = w_out.shape[1]
    shapes = [jax.ShapeDtypeStruct((rows, width), F32)]
    if final:
        shapes.append(jax.ShapeDtypeStruct((rows, width), BF))
        shapes.append(jax.ShapeDtypeStruct((1, rows), F32))
    return pl.pallas_call(
        functools.partial(project_kernel, n, high, indices),
        out_shape=shapes,
        in_specs=[sm(), sm()] + [vm()] * (2 + len(parts)),
        out_specs=[vm()] * len(shapes),
        scratch_shapes=[VMEM((rows, width), BF)],
        compiler_params=params(20),
        cost_estimate=cost(2 * rows * width * width * len(parts), 2 * w_out.size * 1.5),
    )(slots, ids, base, w_out, *parts)


def normed_rows(res, sq_row, gain, model_width):
    rows, width = res.shape
    scale = lax.rsqrt(sq_row / model_width + EPS)
    column = jnp.broadcast_to(scale, (HD, rows)).T
    parts = [
        (res[:, g * HD : (g + 1) * HD] * column * gain[:, g * HD : (g + 1) * HD]).astype(BF)
        for g in range(width // HD)
    ]
    return jnp.concatenate(parts, axis=1)


def norm_kernel(model_width, res_ref, sq_ref, gain_ref, out_ref):
    out_ref[...] = normed_rows(res_ref[...], sq_ref[...], gain_ref[...], model_width)


def norm(model_width, res, sq, gain):
    return pl.pallas_call(
        functools.partial(norm_kernel, model_width),
        out_shape=jax.ShapeDtypeStruct(res.shape, BF),
        in_specs=[vm()] * 3,
        out_specs=vm(),
        compiler_params=params(8),
        cost_estimate=cost(4 * res.size, 6 * res.size),
    )(res, sq, gain)


def split(array):
    high = array.astype(jnp.bfloat16)
    low = (array - high.astype(np.float64)).astype(jnp.bfloat16)
    return high, low


def transform_tables(rows):
    size = 2 * rows
    freq = np.arange(rows)[:, None].astype(np.float64)
    time = np.arange(rows)[None, :].astype(np.float64)
    angle = 2 * np.pi * ((freq * time) % size) / size
    cosine = np.cos(angle)
    sine = -np.sin(angle)
    nyquist = np.where(np.arange(rows) % 2 == 0, 1.0, -1.0)
    sine[0] = nyquist
    forward = np.concatenate([cosine, sine], axis=0)
    late = 2 * np.pi * ((freq * (time + rows)) % size) / size
    back_cos = 2 * np.cos(late)
    back_cos[0] = 1.0
    back_sin = -2 * np.sin(late)
    back_sin[0] = np.where((np.arange(rows) + rows) % 2 == 0, 1.0, -1.0)
    backward = np.concatenate([back_cos, back_sin], axis=0).T / size
    return split(forward), split(backward)


def spectrum_kernel(filters_ref, len_ref, fh_ref, fl_ref, out_ref):
    taps = filters_ref.shape[1]
    lag = lax.broadcasted_iota(jnp.int32, filters_ref.shape, 1)
    used = jnp.where(lag < len_ref[...], filters_ref[...].astype(F32), 0.0).astype(BF)
    nt = (((1,), (1,)), ((), ()))
    fh = fh_ref[:, 0:taps]
    fl = fl_ref[:, 0:taps]
    out_ref[...] = lax.dot_general(fh, used, nt, preferred_element_type=F32) + lax.dot_general(
        fl, used, nt, preferred_element_type=F32
    )


def spectrum(filters, filter_len, forward):
    return pl.pallas_call(
        spectrum_kernel,
        out_shape=jax.ShapeDtypeStruct((forward[0].shape[0], filters.shape[0]), F32),
        in_specs=[vm()] * 4,
        out_specs=vm(),
        compiler_params=params(12),
        cost_estimate=cost(4 * forward[0].size * filters.shape[0], 8 * filters.size),
        name="spectrum",
    )(filters, filter_len.reshape(-1, 1), *forward)


def two(a_high, a_low, b):
    return jnp.dot(a_high, b, preferred_element_type=F32) + jnp.dot(
        a_low, b, preferred_element_type=F32
    )


def frequency_signs(rows):
    row_id = lax.broadcasted_iota(jnp.int32, (rows, 1), 0)
    return row_id == 0, jnp.where(row_id % 2 == 0, 1.0, -1.0)


def late_spectrum(own, fh, fl):
    rows = own.shape[0]
    first, sign = frequency_signs(rows)
    plain = two(fh, fl, own)
    return sign * plain[:rows], jnp.where(first, 1.0, sign) * plain[rows:]


def filtered(x_re, x_im, gh, gl, spec):
    rows = x_re.shape[0]
    first, _ = frequency_signs(rows)
    h_re, h_im = spec[:rows], spec[rows:]
    h_cross = jnp.where(first, 0.0, h_im)
    h_own = jnp.where(first, h_im, h_re)
    y = jnp.concatenate([x_re * h_re - x_im * h_cross, x_re * h_cross + x_im * h_own], axis=0)
    y_high = y.astype(BF)
    y_low = (y - y_high.astype(F32)).astype(BF)
    return two(gh, gl, y_high) + jnp.dot(gh, y_low, preferred_element_type=F32)


def conv_low_kernel(res_ref, own_ref, before_ref, spec_ref, skip_ref, fh, fl, gh, gl, out_ref):
    rows = res_ref.shape[0]
    own = own_ref[...]
    late_re, late_im = late_spectrum(own, fh[...], fl[...])
    early = two(fh[...], fl[...], before_ref[...])
    conv = filtered(early[:rows] + late_re, early[rows:] + late_im, gh[...], gl[...], spec_ref[...])
    out_ref[...] = (res_ref[...] + conv + skip_ref[...] * own.astype(F32)).astype(BF)


def conv_own_kernel(
    model_width, res_ref, sq_ref, spec_ref, gain_ref, skip_ref, fh, fl, gh, gl, out_ref
):
    own = normed_rows(res_ref[...], sq_ref[...], gain_ref[...], model_width)
    late_re, late_im = late_spectrum(own, fh[...], fl[...])
    conv = filtered(late_re, late_im, gh[...], gl[...], spec_ref[...])
    out_ref[...] = res_ref[...] + conv + skip_ref[...] * own.astype(F32)


def conv_high_kernel(
    n, model_width, slots_ref, ids_ref, part_ref, raw_ref, raw_sq_ref, low_ref, done_ref,
    spec_ref, gain_ref, fh, fl, gh, gl, out_ref,
):
    rows = part_ref.shape[0]
    last = ids_ref[0] == n - 1
    raw = normed_rows(raw_ref[...].astype(F32), raw_sq_ref[...], gain_ref[...], model_width)
    before = jnp.where(last, low_ref[...].astype(F32), raw.astype(F32)).astype(BF)
    early = two(fh[...], fl[...], before)
    conv = filtered(early[:rows], early[rows:], gh[...], gl[...], spec_ref[...])
    half = half_index(slots_ref, ids_ref, 1)
    out_ref[pl.ds(pl.multiple_of((1 - half) * rows, rows), rows), :] = done_ref[...]
    out_ref[pl.ds(pl.multiple_of(half * rows, rows), rows), :] = (part_ref[...] + conv).astype(BF)


def moved(block, axis, route):
    return lax.ppermute(block, axis, route)


def gather_mp(own, size):
    chips = size // 2
    pieces = [own]
    for k in range(1, chips - 1):
        pieces.append(moved(own, "mp", xor_route(size, 2 * k)))
    inner = [(i, i ^ (size - 2)) for i in range(2, size - 2)]
    direct = moved(own, "mp", inner)
    ends = [(2, 0), (3, 1), (size - 4, size - 2), (size - 3, size - 1)]
    relayed = moved(pieces[chips - 2], "mp", ends)
    pieces.append(direct + relayed)
    parts = []
    for piece in pieces:
        parts.append(piece)
        parts.append(moved(piece, "mp", xor_route(size, 1)))
    return parts


def total_mp(part, size):
    k = 1
    while k < size:
        part = part + moved(part, "mp", xor_route(size, k))
        k *= 2
    return part


def before_rows(block, distance):
    devices = range(lax.axis_size("seq"))
    return moved(block, "seq", [(i - distance, i) for i in devices if i - distance in devices])


def fast_device(
    incoming, queries, key_vecs, value_vecs, w_out, norm_gain, filters, filter_len, skip_gain, slot_map
):
    n = lax.axis_size("seq")
    mp_size = lax.axis_size("mp")
    rows, width = queries.shape[0] // 2, queries.shape[1]
    model_width = w_out.shape[0]
    ids = jnp.stack([lax.axis_index("seq"), lax.axis_index("mp")]).astype(jnp.int32)
    gain = norm_gain.reshape(1, -1)
    skip = skip_gain.reshape(1, -1)
    forward, backward = transform_tables(rows)
    forward = tuple(jnp.asarray(t) for t in forward)
    backward = tuple(jnp.asarray(t) for t in backward)

    def exchange(pieces):
        return [pieces[0]] + [moved(pieces[k], "seq", xor_route(n, k)) for k in range(1, n)]

    packed_low, packed_high = pack(n, slot_map, ids, queries, key_vecs, value_vecs)
    low = exchange(packed_low)
    high = exchange(packed_high)
    spec = spectrum(filters, filter_len, forward)

    att_low = exchange(attend(n, 0, rows, ids, low))
    parts_low = gather_mp(jnp.concatenate(att_low, axis=0), mp_size)
    att_high = exchange(attend(n, 1, rows, ids, low + high))
    parts_high = gather_mp(jnp.concatenate(att_high, axis=0), mp_size)

    every = tuple(range(mp_size))
    res_low, _, sq_low = project(n, 0, slot_map, ids, incoming, w_out, parts_low, every, True)
    norm_low = norm(model_width, res_low, total_mp(sq_low, mp_size), gain)
    before_low = before_rows(norm_low, 1)
    transforms = forward + backward
    done_low = pl.pallas_call(
        conv_low_kernel,
        out_shape=jax.ShapeDtypeStruct((rows, width), BF),
        in_specs=[vm()] * 9,
        out_specs=vm(),
        compiler_params=params(20),
        cost_estimate=cost(14 * rows * rows * width, 12 * rows * width),
        name="conv_low",
    )(res_low, norm_low, before_low, spec, skip, *transforms)

    most = mp_size - 2
    (base_high,) = project(
        n, 1, slot_map, ids, incoming, w_out, parts_high[:most], every[:most], False
    )
    res_high, raw_high, sq_high = project(
        n, 1, slot_map, ids, base_high, w_out, parts_high[most:], every[most:], True
    )
    raw_before = before_rows(raw_high, -1)
    sq_high = total_mp(sq_high, mp_size)
    sq_before = before_rows(sq_high, -1)
    part_high = pl.pallas_call(
        functools.partial(conv_own_kernel, model_width),
        out_shape=jax.ShapeDtypeStruct((rows, width), F32),
        in_specs=[vm()] * 9,
        out_specs=vm(),
        compiler_params=params(20),
        cost_estimate=cost(10 * rows * rows * width, 12 * rows * width),
        name="conv_own",
    )(res_high, sq_high, spec, gain, skip, *transforms)
    return pl.pallas_call(
        functools.partial(conv_high_kernel, n, model_width),
        out_shape=jax.ShapeDtypeStruct((2 * rows, width), BF),
        in_specs=[sm(), sm()] + [vm()] * 11,
        out_specs=vm(),
        compiler_params=params(20),
        cost_estimate=cost(10 * rows * rows * width, 12 * rows * width),
        name="conv_high",
    )(
        slot_map, ids, part_high, raw_before, sq_before, norm_low, done_low, spec, gain, *transforms
    )


def power_of_two(value):
    return value & (value - 1) == 0


def on_device(*arrays):
    n = lax.axis_size("seq")
    size = lax.axis_size("mp")
    queries, filters = arrays[1], arrays[6]
    rows = queries.shape[0] // 2
    heads = queries.shape[1] // HD
    fits = (
        heads % n == 0
        and power_of_two(n)
        and power_of_two(size)
        and size >= 8
        and rows % 256 == 0
        and filters.shape[1] <= rows
    )
    if not fits:
        return general_device(*arrays)
    return fast_device(*arrays)


def solution(mesh):
    placed = (
        P("seq", "mp"),
        P("seq", "mp"),
        P("seq", "mp"),
        P("seq", "mp"),
        P(None, "mp"),
        P("mp"),
        P("mp", None),
        P("mp"),
        P("mp"),
        P(),
    )
    return jax.shard_map(
        on_device, mesh=mesh, in_specs=placed, out_specs=P("seq", "mp"), check_vma=False
    )
```

```python
import functools

import jax
import jax.numpy as jnp
import numpy as np
from jax import lax
from jax.experimental import pallas as pl
from jax.experimental.pallas import tpu as pltpu
from jax.sharding import PartitionSpec as P


HD = 128
EPS = 1e-05
NEG = -1e30
LOG2E = 1.4426950408889634
BF = jnp.bfloat16
F32 = jnp.float32
VMEM = pltpu.VMEM
SMEM = pltpu.SMEM


def shifted(block, axis, distance):
    devices = range(lax.axis_size(axis))
    route = [(i - distance, i) for i in devices if i - distance in devices]
    return lax.ppermute(block, axis, route)


def block_update(running, query_heads, query_pos, key_part, value_part, key_pos):
    peak_now, total_now, accum_now = running
    key_count = key_part.shape[0]
    head_count = query_heads.shape[1]
    key_heads = key_part.reshape(key_count, head_count, HD)
    value_heads = value_part.reshape(key_count, head_count, HD)
    scores = jnp.einsum(
        "thd,shd->ths", query_heads, key_heads, preferred_element_type=F32
    ) * HD ** (-0.5)
    allowed = key_pos[None, None, :] <= query_pos[:, None, None]
    masked = jnp.where(allowed, scores, NEG)
    peak_next = jnp.maximum(peak_now, jnp.max(masked, axis=2))
    weights = jnp.where(allowed, jnp.exp(masked - peak_next[:, :, None]), 0.0)
    factor = jnp.exp(peak_now - peak_next)
    total_next = total_now * factor + jnp.sum(weights, axis=2)
    summed = jnp.einsum(
        "ths,shd->thd", weights.astype(BF), value_heads, preferred_element_type=F32
    )
    return (peak_next, total_next, accum_now * factor[:, :, None] + summed)


def attend_keys(running, query_heads, query_pos, key_part, value_part, key_pos, block_rows):
    block_count = key_part.shape[0] // block_rows

    def attend_advance(state, item):
        return block_update(state, query_heads, query_pos, *item), None

    stacked = (
        key_part.reshape(block_count, block_rows, -1),
        value_part.reshape(block_count, block_rows, -1),
        key_pos.reshape(block_count, block_rows),
    )
    running, _ = lax.scan(attend_advance, running, stacked)
    return running


def causal_window(extended, taps_lag):
    pair_count, twice, width = extended.shape
    length = twice // 2
    tap_count = taps_lag.shape[0]
    inner = int(np.gcd(tap_count, 16))

    def causal_advance(block, accum):
        base = block * inner
        window = lax.dynamic_slice_in_dim(
            extended, length - base - inner + 1, length + inner - 1, 1
        ).astype(F32)
        tap_block = lax.dynamic_slice_in_dim(taps_lag, base, inner, 0).astype(F32)
        for lag in range(inner):
            offset = inner - 1 - lag
            accum = accum + tap_block[lag][None, None, :] * window[:, offset : offset + length]
        return accum

    start = jnp.zeros((pair_count, length, width), F32)
    return lax.fori_loop(0, tap_count // inner, causal_advance, start)


def general_device(
    incoming, queries, key_vecs, value_vecs, w_out, norm_gain, filters, filter_len, skip_gain, slot_map
):
    tok_rows, local_width = queries.shape
    span_rows = tok_rows // 2
    head_count = local_width // HD
    model_width = w_out.shape[0]
    all_rows = slot_map.shape[0] * span_rows
    row_ids = jnp.arange(all_rows, dtype=jnp.int32)
    position = (
        jnp.repeat(slot_map, span_rows, total_repeat_length=all_rows) * span_rows
        + row_ids % span_rows
    )
    seq_rank = lax.axis_index("seq")
    seq_size = lax.axis_size("seq")
    own_pos = lax.dynamic_slice_in_dim(position, seq_rank * tok_rows, tok_rows)
    query_heads = queries.reshape(tok_rows, head_count, HD)
    keys_all = lax.all_gather(key_vecs, "seq", axis=0, tiled=True)
    values_all = lax.all_gather(value_vecs, "seq", axis=0, tiled=True)
    running = attend_keys(
        (
            jnp.full((tok_rows, head_count), NEG, F32),
            jnp.zeros((tok_rows, head_count), F32),
            jnp.zeros((tok_rows, head_count, HD), F32),
        ),
        query_heads,
        own_pos,
        keys_all,
        values_all,
        position,
        2 * tok_rows,
    )
    attention = (running[2] / running[1][:, :, None]).reshape(-1, local_width).astype(BF)
    projected = jnp.dot(
        lax.all_gather(attention, "mp", axis=1, tiled=True), w_out, preferred_element_type=F32
    )
    residual = incoming.astype(F32) + projected
    square_total = lax.psum(jnp.sum(residual * residual, axis=1), "mp")
    scale = lax.rsqrt(square_total / model_width + EPS)
    normed = (residual * scale[:, None] * norm_gain[None, :]).astype(BF)
    tap_count = filters.shape[1]
    taps = jnp.where(
        jnp.arange(tap_count, dtype=jnp.int32)[None, :] < filter_len[:, None],
        filters,
        jnp.zeros((), filters.dtype),
    )
    pair_ids = lax.dynamic_slice_in_dim(slot_map, 2 * seq_rank, 2)
    low_first = pair_ids[0] < pair_ids[1]
    slots = normed.reshape(2, span_rows, local_width)
    low_rows = jnp.where(low_first, slots[0], slots[1])
    high_rows = jnp.where(low_first, slots[1], slots[0])
    own_pair = jnp.stack([low_rows, high_rows])
    low_before = shifted(low_rows, "seq", 1)
    high_before = shifted(high_rows, "seq", -1)
    high_before = jnp.where(seq_rank == seq_size - 1, low_rows, high_before)
    before_pair = jnp.stack([low_before, high_before])
    conv_pair = causal_window(jnp.concatenate([before_pair, own_pair], axis=1), taps.T)
    conv_slots = jnp.where(low_first, conv_pair, conv_pair[::-1])
    conv_rows = conv_slots.reshape(tok_rows, local_width)
    layer_out = residual + conv_rows + skip_gain[None, :] * normed.astype(F32)
    return layer_out.astype(BF)


def params(megabytes=20):
    return pltpu.CompilerParams(vmem_limit_bytes=megabytes << 20)


def cost(flops, moved, exps=0):
    return pl.CostEstimate(flops=int(flops), bytes_accessed=int(moved), transcendentals=int(exps))


def vm():
    return pl.BlockSpec(memory_space=VMEM)


def sm():
    return pl.BlockSpec(memory_space=SMEM)


def xor_route(count, k):
    return [(i, i ^ k) for i in range(count)]


def half_index(slots_ref, ids_ref, high):
    rank = ids_ref[0]
    first_is_high = slots_ref[2 * rank] > slots_ref[2 * rank + 1]
    return jnp.where(first_is_high, 1 - high, high).astype(jnp.int32)


def pack_kernel(n, slots_ref, ids_ref, q_ref, k_ref, v_ref, *rest):
    outs, sem = rest[: 2 * n], rest[2 * n]
    rank = ids_ref[0]
    rows = outs[0].shape[0] // 3
    wide = outs[0].shape[1]
    copies = []
    for high in range(2):
        half = half_index(slots_ref, ids_ref, high)
        source_rows = pl.ds(pl.multiple_of(half * rows, rows), rows)
        for k in range(n):
            cols = pl.ds(pl.multiple_of((rank ^ k) * wide, wide), wide)
            for a, ref in enumerate((q_ref, k_ref, v_ref)):
                copy = pltpu.make_async_copy(
                    ref.at[source_rows, cols],
                    outs[high * n + k].at[a * rows : (a + 1) * rows, :],
                    sem.at[high * n + k, a],
                )
                copy.start()
                copies.append(copy)
    for copy in copies:
        copy.wait()


def pack(n, slots, ids, q, k, v):
    rows, width = q.shape[0] // 2, q.shape[1]
    piece = jax.ShapeDtypeStruct((3 * rows, width // n), BF)
    packed = pl.pallas_call(
        functools.partial(pack_kernel, n),
        out_shape=[piece] * (2 * n),
        in_specs=[sm(), sm()] + [pl.BlockSpec(memory_space=pltpu.HBM)] * 3,
        out_specs=[vm()] * (2 * n),
        scratch_shapes=[pltpu.SemaphoreType.DMA((2 * n, 3))],
        compiler_params=params(8),
        cost_estimate=cost(0, 24 * rows * width),
        name="pack",
    )(slots, ids, *(pltpu.with_memory_space_constraint(x, pltpu.HBM) for x in (q, k, v)))
    return packed[:n], packed[n:]


def attend_kernel(n, high, rows, ids_ref, *refs):
    chunks = 2 if high else 1
    ins = refs[: chunks * n]
    outs = refs[chunks * n : chunks * n + n]
    q_all, k_all, v_all, o_all = refs[chunks * n + n :]
    rank = ids_ref[0]
    wide = outs[0].shape[1]

    def place(block):
        return pl.ds(pl.multiple_of(block * rows, rows), rows)

    for c in range(chunks):
        for k in range(n):
            source = rank ^ k
            block = source if c == 0 else 2 * n - 1 - source
            piece = ins[c * n + k]
            if c == chunks - 1:
                q_all[place(block - c * n), :] = piece[0:rows, :]
            k_all[place(block), :] = piece[rows : 2 * rows, :]
            v_all[place(block), :] = piece[2 * rows : 3 * rows, :]
    base = n if high else 0
    row_id = lax.broadcasted_iota(jnp.int32, (rows, rows), 0)
    col_id = lax.broadcasted_iota(jnp.int32, (rows, rows), 1)
    causal = col_id <= row_id
    factor = HD ** (-0.5) * LOG2E
    nt = (((1,), (1,)), ((), ()))
    for b in range(n):
        past = (base + b) * rows
        for h in range(wide // HD):
            cols = slice(h * HD, (h + 1) * HD)
            q = q_all[b * rows : (b + 1) * rows, cols]
            near = lax.dot_general(
                q, k_all[past : past + rows, cols], nt, preferred_element_type=F32
            )
            near = jnp.where(causal, near, NEG)
            peak = jnp.max(near, axis=1, keepdims=True)
            if past:
                far = lax.dot_general(q, k_all[0:past, cols], nt, preferred_element_type=F32)
                peak = jnp.maximum(peak, jnp.max(far, axis=1, keepdims=True))
            w_near = jnp.exp2((near - peak) * factor)
            total = jnp.sum(w_near, axis=1, keepdims=True)
            summed = jnp.dot(
                w_near.astype(BF), v_all[past : past + rows, cols], preferred_element_type=F32
            )
            if past:
                w_far = jnp.exp2((far - peak) * factor)
                total = total + jnp.sum(w_far, axis=1, keepdims=True)
                summed = summed + jnp.dot(
                    w_far.astype(BF), v_all[0:past, cols], preferred_element_type=F32
                )
            owner = n - 1 - b if high else b
            o_all[owner * rows : (owner + 1) * rows, cols] = (summed / total).astype(BF)
    for k in range(n):
        outs[k][...] = o_all[place(rank ^ k), :]


def attend(n, high, rows, ids, pieces):
    wide = pieces[0].shape[1]
    chunks = 2 if high else 1
    pairs = n * (n + 1) // 2 + (n * n if high else 0)
    area = pairs * rows * rows * (wide // HD)
    return pl.pallas_call(
        functools.partial(attend_kernel, n, high, rows),
        out_shape=[jax.ShapeDtypeStruct((rows, wide), BF)] * n,
        in_specs=[sm()] + [vm()] * len(pieces),
        out_specs=[vm()] * n,
        scratch_shapes=[
            VMEM((n * rows, wide), BF),
            VMEM((chunks * n * rows, wide), BF),
            VMEM((chunks * n * rows, wide), BF),
            VMEM((n * rows, wide), BF),
        ],
        compiler_params=params(32),
        cost_estimate=cost(4 * area * HD, 8 * n * rows * wide * chunks, area),
        name="attend_high" if high else "attend_low",
    )(ids, *pieces)


def project_kernel(n, high, indices, slots_ref, ids_ref, base_ref, w_ref, *refs):
    count = len(indices)
    parts, outs, lhs = refs[:count], refs[count:-1], refs[-1]
    rank = ids_ref[0]
    me = ids_ref[1]
    rows, width = lhs.shape
    wide = width // n
    if base_ref.shape[0] == rows:
        total = base_ref[...]
    else:
        half = half_index(slots_ref, ids_ref, high)
        total = base_ref[pl.ds(pl.multiple_of(half * rows, rows), rows), :].astype(F32)
    for index, part in zip(indices, parts):
        for k in range(n):
            cols = pl.ds(pl.multiple_of((rank ^ k) * wide, wide), wide)
            lhs[:, cols] = part[k * rows : (k + 1) * rows, :]
        depth = pl.ds(pl.multiple_of((me ^ index) * width, width), width)
        total = total + jnp.dot(lhs[...], w_ref[depth, :], preferred_element_type=F32)
    outs[0][...] = total
    if len(outs) == 1:
        return
    outs[1][...] = total.astype(BF)
    squares = total * total
    lanes = squares[:, 0:HD]
    for g in range(1, squares.shape[1] // HD):
        lanes = lanes + squares[:, g * HD : (g + 1) * HD]
    outs[2][...] = jnp.sum(lanes.T, axis=0, keepdims=True)


def project(n, high, slots, ids, base, w_out, parts, indices, final):
    rows = parts[0].shape[0] // n
    width = w_out.shape[1]
    shapes = [jax.ShapeDtypeStruct((rows, width), F32)]
    if final:
        shapes.append(jax.ShapeDtypeStruct((rows, width), BF))
        shapes.append(jax.ShapeDtypeStruct((1, rows), F32))
    return pl.pallas_call(
        functools.partial(project_kernel, n, high, indices),
        out_shape=shapes,
        in_specs=[sm(), sm()] + [vm()] * (2 + len(parts)),
        out_specs=[vm()] * len(shapes),
        scratch_shapes=[VMEM((rows, width), BF)],
        compiler_params=params(20),
        cost_estimate=cost(2 * rows * width * width * len(parts), 2 * w_out.size * 1.5),
    )(slots, ids, base, w_out, *parts)


def normed_rows(res, sq_row, gain, model_width):
    rows, width = res.shape
    scale = lax.rsqrt(sq_row / model_width + EPS)
    column = jnp.broadcast_to(scale, (HD, rows)).T
    parts = [
        (res[:, g * HD : (g + 1) * HD] * column * gain[:, g * HD : (g + 1) * HD]).astype(BF)
        for g in range(width // HD)
    ]
    return jnp.concatenate(parts, axis=1)


def norm_kernel(model_width, res_ref, sq_ref, gain_ref, out_ref):
    out_ref[...] = normed_rows(res_ref[...], sq_ref[...], gain_ref[...], model_width)


def norm(model_width, res, sq, gain):
    return pl.pallas_call(
        functools.partial(norm_kernel, model_width),
        out_shape=jax.ShapeDtypeStruct(res.shape, BF),
        in_specs=[vm()] * 3,
        out_specs=vm(),
        compiler_params=params(8),
        cost_estimate=cost(4 * res.size, 6 * res.size),
    )(res, sq, gain)


def split(array):
    high = array.astype(jnp.bfloat16)
    low = (array - high.astype(np.float64)).astype(jnp.bfloat16)
    return high, low


def transform_tables(rows):
    size = 2 * rows
    freq = np.arange(rows)[:, None].astype(np.float64)
    time = np.arange(rows)[None, :].astype(np.float64)
    angle = 2 * np.pi * ((freq * time) % size) / size
    cosine = np.cos(angle)
    sine = -np.sin(angle)
    nyquist = np.where(np.arange(rows) % 2 == 0, 1.0, -1.0)
    sine[0] = nyquist
    forward = np.concatenate([cosine, sine], axis=0)
    late = 2 * np.pi * ((freq * (time + rows)) % size) / size
    back_cos = 2 * np.cos(late)
    back_cos[0] = 1.0
    back_sin = -2 * np.sin(late)
    back_sin[0] = np.where((np.arange(rows) + rows) % 2 == 0, 1.0, -1.0)
    backward = np.concatenate([back_cos, back_sin], axis=0).T / size
    return split(forward), split(backward)


def spectrum_kernel(filters_ref, len_ref, fh_ref, fl_ref, out_ref):
    taps = filters_ref.shape[1]
    lag = lax.broadcasted_iota(jnp.int32, filters_ref.shape, 1)
    used = jnp.where(lag < len_ref[...], filters_ref[...].astype(F32), 0.0).astype(BF)
    nt = (((1,), (1,)), ((), ()))
    fh = fh_ref[:, 0:taps]
    fl = fl_ref[:, 0:taps]
    out_ref[...] = lax.dot_general(fh, used, nt, preferred_element_type=F32) + lax.dot_general(
        fl, used, nt, preferred_element_type=F32
    )


def spectrum(filters, filter_len, forward):
    return pl.pallas_call(
        spectrum_kernel,
        out_shape=jax.ShapeDtypeStruct((forward[0].shape[0], filters.shape[0]), F32),
        in_specs=[vm()] * 4,
        out_specs=vm(),
        compiler_params=params(12),
        cost_estimate=cost(4 * forward[0].size * filters.shape[0], 8 * filters.size),
        name="spectrum",
    )(filters, filter_len.reshape(-1, 1), *forward)


def two(a_high, a_low, b):
    return jnp.dot(a_high, b, preferred_element_type=F32) + jnp.dot(
        a_low, b, preferred_element_type=F32
    )


def frequency_signs(rows):
    row_id = lax.broadcasted_iota(jnp.int32, (rows, 1), 0)
    return row_id == 0, jnp.where(row_id % 2 == 0, 1.0, -1.0)


def late_spectrum(own, fh, fl):
    rows = own.shape[0]
    first, sign = frequency_signs(rows)
    plain = two(fh, fl, own)
    return sign * plain[:rows], jnp.where(first, 1.0, sign) * plain[rows:]


def filtered(x_re, x_im, gh, gl, spec):
    rows = x_re.shape[0]
    first, _ = frequency_signs(rows)
    h_re, h_im = spec[:rows], spec[rows:]
    h_cross = jnp.where(first, 0.0, h_im)
    h_own = jnp.where(first, h_im, h_re)
    y = jnp.concatenate([x_re * h_re - x_im * h_cross, x_re * h_cross + x_im * h_own], axis=0)
    y_high = y.astype(BF)
    y_low = (y - y_high.astype(F32)).astype(BF)
    return two(gh, gl, y_high) + jnp.dot(gh, y_low, preferred_element_type=F32)


def conv_low_kernel(res_ref, own_ref, before_ref, spec_ref, skip_ref, fh, fl, gh, gl, out_ref):
    rows = res_ref.shape[0]
    own = own_ref[...]
    late_re, late_im = late_spectrum(own, fh[...], fl[...])
    early = two(fh[...], fl[...], before_ref[...])
    conv = filtered(early[:rows] + late_re, early[rows:] + late_im, gh[...], gl[...], spec_ref[...])
    out_ref[...] = (res_ref[...] + conv + skip_ref[...] * own.astype(F32)).astype(BF)


def conv_own_kernel(
    model_width, res_ref, sq_ref, spec_ref, gain_ref, skip_ref, fh, fl, gh, gl, out_ref
):
    own = normed_rows(res_ref[...], sq_ref[...], gain_ref[...], model_width)
    late_re, late_im = late_spectrum(own, fh[...], fl[...])
    conv = filtered(late_re, late_im, gh[...], gl[...], spec_ref[...])
    out_ref[...] = res_ref[...] + conv + skip_ref[...] * own.astype(F32)


def conv_high_kernel(
    n, model_width, slots_ref, ids_ref, part_ref, raw_ref, raw_sq_ref, low_ref, done_ref,
    spec_ref, gain_ref, fh, fl, gh, gl, out_ref,
):
    rows = part_ref.shape[0]
    last = ids_ref[0] == n - 1
    raw = normed_rows(raw_ref[...].astype(F32), raw_sq_ref[...], gain_ref[...], model_width)
    before = jnp.where(last, low_ref[...].astype(F32), raw.astype(F32)).astype(BF)
    early = two(fh[...], fl[...], before)
    conv = filtered(early[:rows], early[rows:], gh[...], gl[...], spec_ref[...])
    half = half_index(slots_ref, ids_ref, 1)
    out_ref[pl.ds(pl.multiple_of((1 - half) * rows, rows), rows), :] = done_ref[...]
    out_ref[pl.ds(pl.multiple_of(half * rows, rows), rows), :] = (part_ref[...] + conv).astype(BF)


def moved(block, axis, route):
    return lax.ppermute(block, axis, route)


def gather_mp(own, size):
    parts = []
    for k in range(size // 2):
        piece = moved(own, "mp", xor_route(size, 2 * k)) if k else own
        parts.append(piece)
        parts.append(moved(piece, "mp", xor_route(size, 1)))
    return parts


def total_mp(part, size):
    k = 1
    while k < size:
        part = part + moved(part, "mp", xor_route(size, k))
        k *= 2
    return part


def before_rows(block, distance):
    devices = range(lax.axis_size("seq"))
    return moved(block, "seq", [(i - distance, i) for i in devices if i - distance in devices])


def fast_device(
    incoming, queries, key_vecs, value_vecs, w_out, norm_gain, filters, filter_len, skip_gain, slot_map
):
    n = lax.axis_size("seq")
    mp_size = lax.axis_size("mp")
    rows, width = queries.shape[0] // 2, queries.shape[1]
    model_width = w_out.shape[0]
    ids = jnp.stack([lax.axis_index("seq"), lax.axis_index("mp")]).astype(jnp.int32)
    gain = norm_gain.reshape(1, -1)
    skip = skip_gain.reshape(1, -1)
    forward, backward = transform_tables(rows)
    forward = tuple(jnp.asarray(t) for t in forward)
    backward = tuple(jnp.asarray(t) for t in backward)

    def exchange(pieces):
        return [pieces[0]] + [moved(pieces[k], "seq", xor_route(n, k)) for k in range(1, n)]

    packed_low, packed_high = pack(n, slot_map, ids, queries, key_vecs, value_vecs)
    low = exchange(packed_low)
    high = exchange(packed_high)
    spec = spectrum(filters, filter_len, forward)

    att_low = exchange(attend(n, 0, rows, ids, low))
    parts_low = gather_mp(jnp.concatenate(att_low, axis=0), mp_size)
    att_high = exchange(attend(n, 1, rows, ids, low + high))
    parts_high = gather_mp(jnp.concatenate(att_high, axis=0), mp_size)

    every = tuple(range(mp_size))
    res_low, _, sq_low = project(n, 0, slot_map, ids, incoming, w_out, parts_low, every, True)
    norm_low = norm(model_width, res_low, total_mp(sq_low, mp_size), gain)
    before_low = before_rows(norm_low, 1)
    transforms = forward + backward
    done_low = pl.pallas_call(
        conv_low_kernel,
        out_shape=jax.ShapeDtypeStruct((rows, width), BF),
        in_specs=[vm()] * 9,
        out_specs=vm(),
        compiler_params=params(20),
        cost_estimate=cost(14 * rows * rows * width, 12 * rows * width),
        name="conv_low",
    )(res_low, norm_low, before_low, spec, skip, *transforms)

    most = mp_size - 2
    (base_high,) = project(
        n, 1, slot_map, ids, incoming, w_out, parts_high[:most], every[:most], False
    )
    res_high, raw_high, sq_high = project(
        n, 1, slot_map, ids, base_high, w_out, parts_high[most:], every[most:], True
    )
    raw_before = before_rows(raw_high, -1)
    sq_high = total_mp(sq_high, mp_size)
    sq_before = before_rows(sq_high, -1)
    part_high = pl.pallas_call(
        functools.partial(conv_own_kernel, model_width),
        out_shape=jax.ShapeDtypeStruct((rows, width), F32),
        in_specs=[vm()] * 9,
        out_specs=vm(),
        compiler_params=params(20),
        cost_estimate=cost(10 * rows * rows * width, 12 * rows * width),
        name="conv_own",
    )(res_high, sq_high, spec, gain, skip, *transforms)
    return pl.pallas_call(
        functools.partial(conv_high_kernel, n, model_width),
        out_shape=jax.ShapeDtypeStruct((2 * rows, width), BF),
        in_specs=[sm(), sm()] + [vm()] * 11,
        out_specs=vm(),
        compiler_params=params(20),
        cost_estimate=cost(10 * rows * rows * width, 12 * rows * width),
        name="conv_high",
    )(
        slot_map, ids, part_high, raw_before, sq_before, norm_low, done_low, spec, gain, *transforms
    )


def power_of_two(value):
    return value & (value - 1) == 0


def on_device(*arrays):
    n = lax.axis_size("seq")
    size = lax.axis_size("mp")
    queries, filters = arrays[1], arrays[6]
    rows = queries.shape[0] // 2
    heads = queries.shape[1] // HD
    fits = (
        heads % n == 0
        and power_of_two(n)
        and power_of_two(size)
        and size >= 4
        and rows % 256 == 0
        and filters.shape[1] <= rows
    )
    if not fits:
        return general_device(*arrays)
    return fast_device(*arrays)


def solution(mesh):
    placed = (
        P("seq", "mp"),
        P("seq", "mp"),
        P("seq", "mp"),
        P("seq", "mp"),
        P(None, "mp"),
        P("mp"),
        P("mp", None),
        P("mp"),
        P("mp"),
        P(),
    )
    return jax.shard_map(
        on_device, mesh=mesh, in_specs=placed, out_specs=P("seq", "mp"), check_vma=False
    )
```

```python
import functools

import jax
import jax.numpy as jnp
import numpy as np
from jax import lax
from jax.experimental import pallas as pl
from jax.experimental.pallas import tpu as pltpu
from jax.sharding import PartitionSpec as P


HD = 128
EPS = 1e-05
NEG = -1e30
LOG2E = 1.4426950408889634
BF = jnp.bfloat16
F32 = jnp.float32
VMEM = pltpu.VMEM
SMEM = pltpu.SMEM


def shifted(block, axis, distance):
    devices = range(lax.axis_size(axis))
    route = [(i - distance, i) for i in devices if i - distance in devices]
    return lax.ppermute(block, axis, route)


def block_update(running, query_heads, query_pos, key_part, value_part, key_pos):
    peak_now, total_now, accum_now = running
    key_count = key_part.shape[0]
    head_count = query_heads.shape[1]
    key_heads = key_part.reshape(key_count, head_count, HD)
    value_heads = value_part.reshape(key_count, head_count, HD)
    scores = jnp.einsum(
        "thd,shd->ths", query_heads, key_heads, preferred_element_type=F32
    ) * HD ** (-0.5)
    allowed = key_pos[None, None, :] <= query_pos[:, None, None]
    masked = jnp.where(allowed, scores, NEG)
    peak_next = jnp.maximum(peak_now, jnp.max(masked, axis=2))
    weights = jnp.where(allowed, jnp.exp(masked - peak_next[:, :, None]), 0.0)
    factor = jnp.exp(peak_now - peak_next)
    total_next = total_now * factor + jnp.sum(weights, axis=2)
    summed = jnp.einsum(
        "ths,shd->thd", weights.astype(BF), value_heads, preferred_element_type=F32
    )
    return (peak_next, total_next, accum_now * factor[:, :, None] + summed)


def attend_keys(running, query_heads, query_pos, key_part, value_part, key_pos, block_rows):
    block_count = key_part.shape[0] // block_rows

    def attend_advance(state, item):
        return block_update(state, query_heads, query_pos, *item), None

    stacked = (
        key_part.reshape(block_count, block_rows, -1),
        value_part.reshape(block_count, block_rows, -1),
        key_pos.reshape(block_count, block_rows),
    )
    running, _ = lax.scan(attend_advance, running, stacked)
    return running


def causal_window(extended, taps_lag):
    pair_count, twice, width = extended.shape
    length = twice // 2
    tap_count = taps_lag.shape[0]
    inner = int(np.gcd(tap_count, 16))

    def causal_advance(block, accum):
        base = block * inner
        window = lax.dynamic_slice_in_dim(
            extended, length - base - inner + 1, length + inner - 1, 1
        ).astype(F32)
        tap_block = lax.dynamic_slice_in_dim(taps_lag, base, inner, 0).astype(F32)
        for lag in range(inner):
            offset = inner - 1 - lag
            accum = accum + tap_block[lag][None, None, :] * window[:, offset : offset + length]
        return accum

    start = jnp.zeros((pair_count, length, width), F32)
    return lax.fori_loop(0, tap_count // inner, causal_advance, start)


def general_device(
    incoming, queries, key_vecs, value_vecs, w_out, norm_gain, filters, filter_len, skip_gain, slot_map
):
    tok_rows, local_width = queries.shape
    span_rows = tok_rows // 2
    head_count = local_width // HD
    model_width = w_out.shape[0]
    all_rows = slot_map.shape[0] * span_rows
    row_ids = jnp.arange(all_rows, dtype=jnp.int32)
    position = (
        jnp.repeat(slot_map, span_rows, total_repeat_length=all_rows) * span_rows
        + row_ids % span_rows
    )
    seq_rank = lax.axis_index("seq")
    seq_size = lax.axis_size("seq")
    own_pos = lax.dynamic_slice_in_dim(position, seq_rank * tok_rows, tok_rows)
    query_heads = queries.reshape(tok_rows, head_count, HD)
    keys_all = lax.all_gather(key_vecs, "seq", axis=0, tiled=True)
    values_all = lax.all_gather(value_vecs, "seq", axis=0, tiled=True)
    running = attend_keys(
        (
            jnp.full((tok_rows, head_count), NEG, F32),
            jnp.zeros((tok_rows, head_count), F32),
            jnp.zeros((tok_rows, head_count, HD), F32),
        ),
        query_heads,
        own_pos,
        keys_all,
        values_all,
        position,
        2 * tok_rows,
    )
    attention = (running[2] / running[1][:, :, None]).reshape(-1, local_width).astype(BF)
    projected = jnp.dot(
        lax.all_gather(attention, "mp", axis=1, tiled=True), w_out, preferred_element_type=F32
    )
    residual = incoming.astype(F32) + projected
    square_total = lax.psum(jnp.sum(residual * residual, axis=1), "mp")
    scale = lax.rsqrt(square_total / model_width + EPS)
    normed = (residual * scale[:, None] * norm_gain[None, :]).astype(BF)
    tap_count = filters.shape[1]
    taps = jnp.where(
        jnp.arange(tap_count, dtype=jnp.int32)[None, :] < filter_len[:, None],
        filters,
        jnp.zeros((), filters.dtype),
    )
    pair_ids = lax.dynamic_slice_in_dim(slot_map, 2 * seq_rank, 2)
    low_first = pair_ids[0] < pair_ids[1]
    slots = normed.reshape(2, span_rows, local_width)
    low_rows = jnp.where(low_first, slots[0], slots[1])
    high_rows = jnp.where(low_first, slots[1], slots[0])
    own_pair = jnp.stack([low_rows, high_rows])
    low_before = shifted(low_rows, "seq", 1)
    high_before = shifted(high_rows, "seq", -1)
    high_before = jnp.where(seq_rank == seq_size - 1, low_rows, high_before)
    before_pair = jnp.stack([low_before, high_before])
    conv_pair = causal_window(jnp.concatenate([before_pair, own_pair], axis=1), taps.T)
    conv_slots = jnp.where(low_first, conv_pair, conv_pair[::-1])
    conv_rows = conv_slots.reshape(tok_rows, local_width)
    layer_out = residual + conv_rows + skip_gain[None, :] * normed.astype(F32)
    return layer_out.astype(BF)


def params(megabytes=20):
    return pltpu.CompilerParams(vmem_limit_bytes=megabytes << 20)


def cost(flops, moved, exps=0):
    return pl.CostEstimate(flops=int(flops), bytes_accessed=int(moved), transcendentals=int(exps))


def vm():
    return pl.BlockSpec(memory_space=VMEM)


def sm():
    return pl.BlockSpec(memory_space=SMEM)


def xor_route(count, k):
    return [(i, i ^ k) for i in range(count)]


def half_index(slots_ref, ids_ref, high):
    rank = ids_ref[0]
    first_is_high = slots_ref[2 * rank] > slots_ref[2 * rank + 1]
    return jnp.where(first_is_high, 1 - high, high).astype(jnp.int32)


def pack_kernel(n, slots_ref, ids_ref, q_ref, k_ref, v_ref, *rest):
    outs, sem = rest[: 2 * n], rest[2 * n]
    rank = ids_ref[0]
    rows = outs[0].shape[0] // 3
    wide = outs[0].shape[1]
    copies = []
    for high in range(2):
        half = half_index(slots_ref, ids_ref, high)
        source_rows = pl.ds(pl.multiple_of(half * rows, rows), rows)
        for k in range(n):
            cols = pl.ds(pl.multiple_of((rank ^ k) * wide, wide), wide)
            for a, ref in enumerate((q_ref, k_ref, v_ref)):
                copy = pltpu.make_async_copy(
                    ref.at[source_rows, cols],
                    outs[high * n + k].at[a * rows : (a + 1) * rows, :],
                    sem.at[high * n + k, a],
                )
                copy.start()
                copies.append(copy)
    for copy in copies:
        copy.wait()


def pack(n, slots, ids, q, k, v):
    rows, width = q.shape[0] // 2, q.shape[1]
    piece = jax.ShapeDtypeStruct((3 * rows, width // n), BF)
    packed = pl.pallas_call(
        functools.partial(pack_kernel, n),
        out_shape=[piece] * (2 * n),
        in_specs=[sm(), sm()] + [pl.BlockSpec(memory_space=pltpu.HBM)] * 3,
        out_specs=[vm()] * (2 * n),
        scratch_shapes=[pltpu.SemaphoreType.DMA((2 * n, 3))],
        compiler_params=params(8),
        cost_estimate=cost(0, 24 * rows * width),
        name="pack",
    )(slots, ids, *(pltpu.with_memory_space_constraint(x, pltpu.HBM) for x in (q, k, v)))
    return packed[:n], packed[n:]


def attend_kernel(n, high, rows, ids_ref, *refs):
    chunks = 2 if high else 1
    ins = refs[: chunks * n]
    outs = refs[chunks * n : chunks * n + n]
    q_all, k_all, v_all, o_all = refs[chunks * n + n :]
    rank = ids_ref[0]
    wide = outs[0].shape[1]

    def place(block):
        return pl.ds(pl.multiple_of(block * rows, rows), rows)

    for c in range(chunks):
        for k in range(n):
            source = rank ^ k
            block = source if c == 0 else 2 * n - 1 - source
            piece = ins[c * n + k]
            if c == chunks - 1:
                q_all[place(block - c * n), :] = piece[0:rows, :]
            k_all[place(block), :] = piece[rows : 2 * rows, :]
            v_all[place(block), :] = piece[2 * rows : 3 * rows, :]
    base = n if high else 0
    row_id = lax.broadcasted_iota(jnp.int32, (rows, rows), 0)
    col_id = lax.broadcasted_iota(jnp.int32, (rows, rows), 1)
    causal = col_id <= row_id
    factor = HD ** (-0.5) * LOG2E
    nt = (((1,), (1,)), ((), ()))
    for b in range(n):
        past = (base + b) * rows
        for h in range(wide // HD):
            cols = slice(h * HD, (h + 1) * HD)
            q = q_all[b * rows : (b + 1) * rows, cols]
            near = lax.dot_general(
                q, k_all[past : past + rows, cols], nt, preferred_element_type=F32
            )
            near = jnp.where(causal, near, NEG)
            peak = jnp.max(near, axis=1, keepdims=True)
            if past:
                far = lax.dot_general(q, k_all[0:past, cols], nt, preferred_element_type=F32)
                peak = jnp.maximum(peak, jnp.max(far, axis=1, keepdims=True))
            w_near = jnp.exp2((near - peak) * factor)
            total = jnp.sum(w_near, axis=1, keepdims=True)
            summed = jnp.dot(
                w_near.astype(BF), v_all[past : past + rows, cols], preferred_element_type=F32
            )
            if past:
                w_far = jnp.exp2((far - peak) * factor)
                total = total + jnp.sum(w_far, axis=1, keepdims=True)
                summed = summed + jnp.dot(
                    w_far.astype(BF), v_all[0:past, cols], preferred_element_type=F32
                )
            owner = n - 1 - b if high else b
            o_all[owner * rows : (owner + 1) * rows, cols] = (summed / total).astype(BF)
    for k in range(n):
        outs[k][...] = o_all[place(rank ^ k), :]


def attend(n, high, rows, ids, pieces):
    wide = pieces[0].shape[1]
    chunks = 2 if high else 1
    pairs = n * (n + 1) // 2 + (n * n if high else 0)
    area = pairs * rows * rows * (wide // HD)
    return pl.pallas_call(
        functools.partial(attend_kernel, n, high, rows),
        out_shape=[jax.ShapeDtypeStruct((rows, wide), BF)] * n,
        in_specs=[sm()] + [vm()] * len(pieces),
        out_specs=[vm()] * n,
        scratch_shapes=[
            VMEM((n * rows, wide), BF),
            VMEM((chunks * n * rows, wide), BF),
            VMEM((chunks * n * rows, wide), BF),
            VMEM((n * rows, wide), BF),
        ],
        compiler_params=params(32),
        cost_estimate=cost(4 * area * HD, 8 * n * rows * wide * chunks, area),
        name="attend_high" if high else "attend_low",
    )(ids, *pieces)


def project_kernel(n, indices, slots_ref, ids_ref, base_ref, w_ref, *refs):
    count = len(indices)
    chunks, outs, lhs = (refs[:count], refs[count : 2 * count]), refs[2 * count : -1], refs[-1]
    rank = ids_ref[0]
    me = ids_ref[1]
    size, width = lhs.shape
    rows = size // 2
    wide = width // n
    if base_ref.dtype == F32:
        total = base_ref[...]
    else:
        halves = [half_index(slots_ref, ids_ref, high) * rows for high in range(2)]
        total = jnp.concatenate(
            [base_ref[pl.ds(pl.multiple_of(h, rows), rows), :] for h in halves], axis=0
        ).astype(F32)
    for j, index in enumerate(indices):
        for high in range(2):
            for k in range(n):
                cols = pl.ds(pl.multiple_of((rank ^ k) * wide, wide), wide)
                lhs[high * rows : (high + 1) * rows, cols] = chunks[high][j][
                    k * rows : (k + 1) * rows, :
                ]
        depth = pl.ds(pl.multiple_of((me ^ index) * width, width), width)
        total = total + jnp.dot(lhs[...], w_ref[depth, :], preferred_element_type=F32)
    outs[0][...] = total
    if len(outs) == 1:
        return
    outs[1][...] = total[:rows].astype(BF)
    outs[2][...] = total[rows:].astype(BF)
    squares = total * total
    lanes = squares[:, 0:HD]
    for g in range(1, squares.shape[1] // HD):
        lanes = lanes + squares[:, g * HD : (g + 1) * HD]
    outs[3][...] = jnp.sum(lanes.T, axis=0, keepdims=True)


def project(n, slots, ids, base, w_out, low, high, indices, final):
    size, width = base.shape
    shapes = [jax.ShapeDtypeStruct((size, width), F32)]
    if final:
        shapes += [jax.ShapeDtypeStruct((size // 2, width), BF)] * 2
        shapes.append(jax.ShapeDtypeStruct((1, size), F32))
    return pl.pallas_call(
        functools.partial(project_kernel, n, indices),
        out_shape=shapes,
        in_specs=[sm(), sm()] + [vm()] * (2 + 2 * len(indices)),
        out_specs=[vm()] * len(shapes),
        scratch_shapes=[VMEM((size, width), BF)],
        compiler_params=params(20),
        cost_estimate=cost(2 * size * width * width * len(indices), 2 * w_out.size * 1.5),
    )(slots, ids, base, w_out, *low, *high)


def normed_rows(res, sq_row, gain, model_width):
    rows, width = res.shape
    scale = lax.rsqrt(sq_row / model_width + EPS)
    column = jnp.broadcast_to(scale, (HD, rows)).T
    parts = [
        (res[:, g * HD : (g + 1) * HD] * column * gain[:, g * HD : (g + 1) * HD]).astype(BF)
        for g in range(width // HD)
    ]
    return jnp.concatenate(parts, axis=1)


def split(array):
    high = array.astype(jnp.bfloat16)
    low = (array - high.astype(np.float64)).astype(jnp.bfloat16)
    return high, low


def transform_tables(rows):
    size = 2 * rows
    freq = np.arange(rows)[:, None].astype(np.float64)
    time = np.arange(rows)[None, :].astype(np.float64)
    angle = 2 * np.pi * ((freq * time) % size) / size
    cosine = np.cos(angle)
    sine = -np.sin(angle)
    nyquist = np.where(np.arange(rows) % 2 == 0, 1.0, -1.0)
    sine[0] = nyquist
    forward = np.concatenate([cosine, sine], axis=0)
    late = 2 * np.pi * ((freq * (time + rows)) % size) / size
    back_cos = 2 * np.cos(late)
    back_cos[0] = 1.0
    back_sin = -2 * np.sin(late)
    back_sin[0] = np.where((np.arange(rows) + rows) % 2 == 0, 1.0, -1.0)
    backward = np.concatenate([back_cos, back_sin], axis=0).T / size
    return split(forward), split(backward)


def spectrum_kernel(filters_ref, len_ref, fh_ref, fl_ref, out_ref):
    taps = filters_ref.shape[1]
    lag = lax.broadcasted_iota(jnp.int32, filters_ref.shape, 1)
    used = jnp.where(lag < len_ref[...], filters_ref[...].astype(F32), 0.0).astype(BF)
    nt = (((1,), (1,)), ((), ()))
    fh = fh_ref[:, 0:taps]
    fl = fl_ref[:, 0:taps]
    out_ref[...] = lax.dot_general(fh, used, nt, preferred_element_type=F32) + lax.dot_general(
        fl, used, nt, preferred_element_type=F32
    )


def spectrum(filters, filter_len, forward):
    return pl.pallas_call(
        spectrum_kernel,
        out_shape=jax.ShapeDtypeStruct((forward[0].shape[0], filters.shape[0]), F32),
        in_specs=[vm()] * 4,
        out_specs=vm(),
        compiler_params=params(12),
        cost_estimate=cost(4 * forward[0].size * filters.shape[0], 8 * filters.size),
        name="spectrum",
    )(filters, filter_len.reshape(-1, 1), *forward)


def two(a_high, a_low, b):
    return jnp.dot(a_high, b, preferred_element_type=F32) + jnp.dot(
        a_low, b, preferred_element_type=F32
    )


def frequency_signs(rows):
    row_id = lax.broadcasted_iota(jnp.int32, (rows, 1), 0)
    return row_id == 0, jnp.where(row_id % 2 == 0, 1.0, -1.0)


def late_spectrum(own, fh, fl):
    rows = own.shape[0]
    first, sign = frequency_signs(rows)
    plain = two(fh, fl, own)
    return sign * plain[:rows], jnp.where(first, 1.0, sign) * plain[rows:]


def filtered(x_re, x_im, gh, gl, spec):
    rows = x_re.shape[0]
    first, _ = frequency_signs(rows)
    h_re, h_im = spec[:rows], spec[rows:]
    h_cross = jnp.where(first, 0.0, h_im)
    h_own = jnp.where(first, h_im, h_re)
    y = jnp.concatenate([x_re * h_re - x_im * h_cross, x_re * h_cross + x_im * h_own], axis=0)
    y_high = y.astype(BF)
    y_low = (y - y_high.astype(F32)).astype(BF)
    return two(gh, gl, y_high) + jnp.dot(gh, y_low, preferred_element_type=F32)


def conv_own_kernel(
    model_width, res_ref, sq_ref, spec_ref, gain_ref, skip_ref, fh, fl, gh, gl, out_ref, low_ref
):
    rows = spec_ref.shape[0] // 2
    for high in range(2):
        part = slice(high * rows, (high + 1) * rows)
        res = res_ref[part, :]
        own = normed_rows(res, sq_ref[:, part], gain_ref[...], model_width)
        if not high:
            low_ref[...] = own
        late_re, late_im = late_spectrum(own, fh[...], fl[...])
        conv = filtered(late_re, late_im, gh[...], gl[...], spec_ref[...])
        out_ref[part, :] = res + conv + skip_ref[...] * own.astype(F32)


def conv_last_kernel(
    n, model_width, slots_ref, ids_ref, part_ref, low_ref, raw_low, raw_high, sq_low, sq_high,
    spec_ref, gain_ref, fh, fl, gh, gl, out_ref,
):
    rows = low_ref.shape[0]
    last = ids_ref[0] == n - 1
    gain = gain_ref[...]
    for high, raw_ref, sq_ref in ((0, raw_low, sq_low), (1, raw_high, sq_high)):
        before = normed_rows(raw_ref[...].astype(F32), sq_ref[...], gain, model_width)
        if high:
            before = jnp.where(last, low_ref[...].astype(F32), before.astype(F32)).astype(BF)
        early = two(fh[...], fl[...], before)
        conv = filtered(early[:rows], early[rows:], gh[...], gl[...], spec_ref[...])
        half = half_index(slots_ref, ids_ref, high)
        out_ref[pl.ds(pl.multiple_of(half * rows, rows), rows), :] = (
            part_ref[high * rows : (high + 1) * rows, :] + conv
        ).astype(BF)


def moved(block, axis, route):
    return lax.ppermute(block, axis, route)


def far_piece(own, near, size):
    inner = [(i, i ^ (size - 2)) for i in range(2, size - 2)]
    direct = moved(own, "mp", inner)
    ends = [(2, 0), (3, 1), (size - 4, size - 2), (size - 3, size - 1)]
    return direct + moved(near, "mp", ends)


def gather_mp(own, size):
    chips = size // 2
    pieces = [own]
    for k in range(1, chips - 1):
        pieces.append(moved(own, "mp", xor_route(size, 2 * k)))
    pieces.append(far_piece(own, pieces[chips - 2], size))
    parts = []
    for piece in pieces:
        parts.append(piece)
        parts.append(moved(piece, "mp", xor_route(size, 1)))
    return parts


def total_mp(part, size):
    k = 1
    while k < size:
        part = part + moved(part, "mp", xor_route(size, k))
        k *= 2
    return part


def before_rows(block, distance):
    devices = range(lax.axis_size("seq"))
    return moved(block, "seq", [(i - distance, i) for i in devices if i - distance in devices])


def fast_device(
    incoming, queries, key_vecs, value_vecs, w_out, norm_gain, filters, filter_len, skip_gain, slot_map
):
    n = lax.axis_size("seq")
    mp_size = lax.axis_size("mp")
    rows, width = queries.shape[0] // 2, queries.shape[1]
    model_width = w_out.shape[0]
    ids = jnp.stack([lax.axis_index("seq"), lax.axis_index("mp")]).astype(jnp.int32)
    gain = norm_gain.reshape(1, -1)
    skip = skip_gain.reshape(1, -1)
    forward, backward = transform_tables(rows)
    forward = tuple(jnp.asarray(t) for t in forward)
    backward = tuple(jnp.asarray(t) for t in backward)

    def exchange(pieces):
        return [pieces[0]] + [moved(pieces[k], "seq", xor_route(n, k)) for k in range(1, n)]

    packed_low, packed_high = pack(n, slot_map, ids, queries, key_vecs, value_vecs)
    low = exchange(packed_low)
    high = exchange(packed_high)
    spec = spectrum(filters, filter_len, forward)

    att_low = exchange(attend(n, 0, rows, ids, low))
    parts_low = gather_mp(jnp.concatenate(att_low, axis=0), mp_size)
    att_high = exchange(attend(n, 1, rows, ids, low + high))
    parts_high = gather_mp(jnp.concatenate(att_high, axis=0), mp_size)

    most = mp_size - 2
    first, last = tuple(range(most)), tuple(range(most, mp_size))
    (base,) = project(
        n, slot_map, ids, incoming, w_out,
        parts_low[:most], parts_high[:most], first, False,
    )
    res, raw_low, raw_high, squares = project(
        n, slot_map, ids, base, w_out,
        parts_low[most:], parts_high[most:], last, True,
    )
    raw_low = before_rows(raw_low, 1)
    raw_high = before_rows(raw_high, -1)
    squares = total_mp(squares, mp_size)
    sq_low = before_rows(squares[:, :rows], 1)
    sq_high = before_rows(squares[:, rows:], -1)
    transforms = forward + backward
    part, norm_low = pl.pallas_call(
        functools.partial(conv_own_kernel, model_width),
        out_shape=[
            jax.ShapeDtypeStruct((2 * rows, width), F32),
            jax.ShapeDtypeStruct((rows, width), BF),
        ],
        in_specs=[vm()] * 9,
        out_specs=[vm()] * 2,
        compiler_params=params(20),
        cost_estimate=cost(20 * rows * rows * width, 24 * rows * width),
        name="conv_own",
    )(res, squares, spec, gain, skip, *transforms)
    return pl.pallas_call(
        functools.partial(conv_last_kernel, n, model_width),
        out_shape=jax.ShapeDtypeStruct((2 * rows, width), BF),
        in_specs=[sm(), sm()] + [vm()] * 12,
        out_specs=vm(),
        compiler_params=params(20),
        cost_estimate=cost(20 * rows * rows * width, 24 * rows * width),
        name="conv_last",
    )(
        slot_map, ids, part, norm_low, raw_low, raw_high, sq_low, sq_high, spec, gain, *transforms
    )


def power_of_two(value):
    return value & (value - 1) == 0


def on_device(*arrays):
    n = lax.axis_size("seq")
    size = lax.axis_size("mp")
    queries, filters = arrays[1], arrays[6]
    rows = queries.shape[0] // 2
    heads = queries.shape[1] // HD
    fits = (
        heads % n == 0
        and power_of_two(n)
        and power_of_two(size)
        and size >= 8
        and rows % 256 == 0
        and filters.shape[1] <= rows
    )
    if not fits:
        return general_device(*arrays)
    return fast_device(*arrays)


def solution(mesh):
    placed = (
        P("seq", "mp"),
        P("seq", "mp"),
        P("seq", "mp"),
        P("seq", "mp"),
        P(None, "mp"),
        P("mp"),
        P("mp", None),
        P("mp"),
        P("mp"),
        P(),
    )
    return jax.shard_map(
        on_device, mesh=mesh, in_specs=placed, out_specs=P("seq", "mp"), check_vma=False
    )
```

```python
import functools

import jax
import jax.numpy as jnp
import numpy as np
from jax import lax
from jax.experimental import pallas as pl
from jax.experimental.pallas import tpu as pltpu
from jax.sharding import PartitionSpec as P


HD = 128
EPS = 1e-05
NEG = -1e30
LOG2E = 1.4426950408889634
BF = jnp.bfloat16
F32 = jnp.float32
VMEM = pltpu.VMEM
SMEM = pltpu.SMEM


def shifted(block, axis, distance):
    devices = range(lax.axis_size(axis))
    route = [(i - distance, i) for i in devices if i - distance in devices]
    return lax.ppermute(block, axis, route)


def block_update(running, query_heads, query_pos, key_part, value_part, key_pos):
    peak_now, total_now, accum_now = running
    key_count = key_part.shape[0]
    head_count = query_heads.shape[1]
    key_heads = key_part.reshape(key_count, head_count, HD)
    value_heads = value_part.reshape(key_count, head_count, HD)
    scores = jnp.einsum(
        "thd,shd->ths", query_heads, key_heads, preferred_element_type=F32
    ) * HD ** (-0.5)
    allowed = key_pos[None, None, :] <= query_pos[:, None, None]
    masked = jnp.where(allowed, scores, NEG)
    peak_next = jnp.maximum(peak_now, jnp.max(masked, axis=2))
    weights = jnp.where(allowed, jnp.exp(masked - peak_next[:, :, None]), 0.0)
    factor = jnp.exp(peak_now - peak_next)
    total_next = total_now * factor + jnp.sum(weights, axis=2)
    summed = jnp.einsum(
        "ths,shd->thd", weights.astype(BF), value_heads, preferred_element_type=F32
    )
    return (peak_next, total_next, accum_now * factor[:, :, None] + summed)


def attend_keys(running, query_heads, query_pos, key_part, value_part, key_pos, block_rows):
    block_count = key_part.shape[0] // block_rows

    def attend_advance(state, item):
        return block_update(state, query_heads, query_pos, *item), None

    stacked = (
        key_part.reshape(block_count, block_rows, -1),
        value_part.reshape(block_count, block_rows, -1),
        key_pos.reshape(block_count, block_rows),
    )
    running, _ = lax.scan(attend_advance, running, stacked)
    return running


def causal_window(extended, taps_lag):
    pair_count, twice, width = extended.shape
    length = twice // 2
    tap_count = taps_lag.shape[0]
    inner = int(np.gcd(tap_count, 16))

    def causal_advance(block, accum):
        base = block * inner
        window = lax.dynamic_slice_in_dim(
            extended, length - base - inner + 1, length + inner - 1, 1
        ).astype(F32)
        tap_block = lax.dynamic_slice_in_dim(taps_lag, base, inner, 0).astype(F32)
        for lag in range(inner):
            offset = inner - 1 - lag
            accum = accum + tap_block[lag][None, None, :] * window[:, offset : offset + length]
        return accum

    start = jnp.zeros((pair_count, length, width), F32)
    return lax.fori_loop(0, tap_count // inner, causal_advance, start)


def general_device(
    incoming, queries, key_vecs, value_vecs, w_out, norm_gain, filters, filter_len, skip_gain, slot_map
):
    tok_rows, local_width = queries.shape
    span_rows = tok_rows // 2
    head_count = local_width // HD
    model_width = w_out.shape[0]
    all_rows = slot_map.shape[0] * span_rows
    row_ids = jnp.arange(all_rows, dtype=jnp.int32)
    position = (
        jnp.repeat(slot_map, span_rows, total_repeat_length=all_rows) * span_rows
        + row_ids % span_rows
    )
    seq_rank = lax.axis_index("seq")
    seq_size = lax.axis_size("seq")
    own_pos = lax.dynamic_slice_in_dim(position, seq_rank * tok_rows, tok_rows)
    query_heads = queries.reshape(tok_rows, head_count, HD)
    keys_all = lax.all_gather(key_vecs, "seq", axis=0, tiled=True)
    values_all = lax.all_gather(value_vecs, "seq", axis=0, tiled=True)
    running = attend_keys(
        (
            jnp.full((tok_rows, head_count), NEG, F32),
            jnp.zeros((tok_rows, head_count), F32),
            jnp.zeros((tok_rows, head_count, HD), F32),
        ),
        query_heads,
        own_pos,
        keys_all,
        values_all,
        position,
        2 * tok_rows,
    )
    attention = (running[2] / running[1][:, :, None]).reshape(-1, local_width).astype(BF)
    projected = jnp.dot(
        lax.all_gather(attention, "mp", axis=1, tiled=True), w_out, preferred_element_type=F32
    )
    residual = incoming.astype(F32) + projected
    square_total = lax.psum(jnp.sum(residual * residual, axis=1), "mp")
    scale = lax.rsqrt(square_total / model_width + EPS)
    normed = (residual * scale[:, None] * norm_gain[None, :]).astype(BF)
    tap_count = filters.shape[1]
    taps = jnp.where(
        jnp.arange(tap_count, dtype=jnp.int32)[None, :] < filter_len[:, None],
        filters,
        jnp.zeros((), filters.dtype),
    )
    pair_ids = lax.dynamic_slice_in_dim(slot_map, 2 * seq_rank, 2)
    low_first = pair_ids[0] < pair_ids[1]
    slots = normed.reshape(2, span_rows, local_width)
    low_rows = jnp.where(low_first, slots[0], slots[1])
    high_rows = jnp.where(low_first, slots[1], slots[0])
    own_pair = jnp.stack([low_rows, high_rows])
    low_before = shifted(low_rows, "seq", 1)
    high_before = shifted(high_rows, "seq", -1)
    high_before = jnp.where(seq_rank == seq_size - 1, low_rows, high_before)
    before_pair = jnp.stack([low_before, high_before])
    conv_pair = causal_window(jnp.concatenate([before_pair, own_pair], axis=1), taps.T)
    conv_slots = jnp.where(low_first, conv_pair, conv_pair[::-1])
    conv_rows = conv_slots.reshape(tok_rows, local_width)
    layer_out = residual + conv_rows + skip_gain[None, :] * normed.astype(F32)
    return layer_out.astype(BF)


def params(megabytes=20):
    return pltpu.CompilerParams(vmem_limit_bytes=megabytes << 20)


def cost(flops, moved, exps=0):
    return pl.CostEstimate(flops=int(flops), bytes_accessed=int(moved), transcendentals=int(exps))


def vm():
    return pl.BlockSpec(memory_space=VMEM)


def sm():
    return pl.BlockSpec(memory_space=SMEM)


def xor_route(count, k):
    return [(i, i ^ k) for i in range(count)]


def half_index(slots_ref, ids_ref, high):
    rank = ids_ref[0]
    first_is_high = slots_ref[2 * rank] > slots_ref[2 * rank + 1]
    return jnp.where(first_is_high, 1 - high, high).astype(jnp.int32)


def pack_kernel(n, slots_ref, ids_ref, q_ref, k_ref, v_ref, *rest):
    outs, sem = rest[: 2 * n], rest[2 * n]
    rank = ids_ref[0]
    rows = outs[0].shape[0] // 3
    wide = outs[0].shape[1]
    copies = []
    for high in range(2):
        half = half_index(slots_ref, ids_ref, high)
        source_rows = pl.ds(pl.multiple_of(half * rows, rows), rows)
        for k in range(n):
            cols = pl.ds(pl.multiple_of((rank ^ k) * wide, wide), wide)
            for a, ref in enumerate((q_ref, k_ref, v_ref)):
                copy = pltpu.make_async_copy(
                    ref.at[source_rows, cols],
                    outs[high * n + k].at[a * rows : (a + 1) * rows, :],
                    sem.at[high * n + k, a],
                )
                copy.start()
                copies.append(copy)
    for copy in copies:
        copy.wait()


def pack(n, slots, ids, q, k, v):
    rows, width = q.shape[0] // 2, q.shape[1]
    piece = jax.ShapeDtypeStruct((3 * rows, width // n), BF)
    packed = pl.pallas_call(
        functools.partial(pack_kernel, n),
        out_shape=[piece] * (2 * n),
        in_specs=[sm(), sm()] + [pl.BlockSpec(memory_space=pltpu.HBM)] * 3,
        out_specs=[vm()] * (2 * n),
        scratch_shapes=[pltpu.SemaphoreType.DMA((2 * n, 3))],
        compiler_params=params(8),
        cost_estimate=cost(0, 24 * rows * width),
        name="pack",
    )(slots, ids, *(pltpu.with_memory_space_constraint(x, pltpu.HBM) for x in (q, k, v)))
    return packed[:n], packed[n:]


def attend_kernel(n, high, rows, ids_ref, *refs):
    chunks = 2 if high else 1
    ins = refs[: chunks * n]
    outs = refs[chunks * n : chunks * n + n]
    q_all, k_all, v_all, o_all = refs[chunks * n + n :]
    rank = ids_ref[0]
    wide = outs[0].shape[1]

    def place(block):
        return pl.ds(pl.multiple_of(block * rows, rows), rows)

    for c in range(chunks):
        for k in range(n):
            source = rank ^ k
            block = source if c == 0 else 2 * n - 1 - source
            piece = ins[c * n + k]
            if c == chunks - 1:
                q_all[place(block - c * n), :] = piece[0:rows, :]
            k_all[place(block), :] = piece[rows : 2 * rows, :]
            v_all[place(block), :] = piece[2 * rows : 3 * rows, :]
    base = n if high else 0
    row_id = lax.broadcasted_iota(jnp.int32, (rows, rows), 0)
    col_id = lax.broadcasted_iota(jnp.int32, (rows, rows), 1)
    causal = col_id <= row_id
    factor = HD ** (-0.5) * LOG2E
    nt = (((1,), (1,)), ((), ()))
    for b in range(n):
        past = (base + b) * rows
        for h in range(wide // HD):
            cols = slice(h * HD, (h + 1) * HD)
            q = q_all[b * rows : (b + 1) * rows, cols]
            near = lax.dot_general(
                q, k_all[past : past + rows, cols], nt, preferred_element_type=F32
            )
            near = jnp.where(causal, near, NEG)
            peak = jnp.max(near, axis=1, keepdims=True)
            if past:
                far = lax.dot_general(q, k_all[0:past, cols], nt, preferred_element_type=F32)
                peak = jnp.maximum(peak, jnp.max(far, axis=1, keepdims=True))
            w_near = jnp.exp2((near - peak) * factor)
            total = jnp.sum(w_near, axis=1, keepdims=True)
            summed = jnp.dot(
                w_near.astype(BF), v_all[past : past + rows, cols], preferred_element_type=F32
            )
            if past:
                w_far = jnp.exp2((far - peak) * factor)
                total = total + jnp.sum(w_far, axis=1, keepdims=True)
                summed = summed + jnp.dot(
                    w_far.astype(BF), v_all[0:past, cols], preferred_element_type=F32
                )
            owner = n - 1 - b if high else b
            o_all[owner * rows : (owner + 1) * rows, cols] = (summed / total).astype(BF)
    for k in range(n):
        outs[k][...] = o_all[place(rank ^ k), :]


def attend(n, high, rows, ids, pieces):
    wide = pieces[0].shape[1]
    chunks = 2 if high else 1
    pairs = n * (n + 1) // 2 + (n * n if high else 0)
    area = pairs * rows * rows * (wide // HD)
    return pl.pallas_call(
        functools.partial(attend_kernel, n, high, rows),
        out_shape=[jax.ShapeDtypeStruct((rows, wide), BF)] * n,
        in_specs=[sm()] + [vm()] * len(pieces),
        out_specs=[vm()] * n,
        scratch_shapes=[
            VMEM((n * rows, wide), BF),
            VMEM((chunks * n * rows, wide), BF),
            VMEM((chunks * n * rows, wide), BF),
            VMEM((n * rows, wide), BF),
        ],
        compiler_params=params(32),
        cost_estimate=cost(4 * area * HD, 8 * n * rows * wide * chunks, area),
        name="attend_high" if high else "attend_low",
    )(ids, *pieces)


def project_kernel(n, high, indices, slots_ref, ids_ref, base_ref, w_ref, *refs):
    count = len(indices)
    parts, outs, lhs = refs[:count], refs[count:-1], refs[-1]
    rank = ids_ref[0]
    me = ids_ref[1]
    rows, width = lhs.shape
    wide = width // n
    if base_ref.shape[0] == rows:
        total = base_ref[...]
    else:
        half = half_index(slots_ref, ids_ref, high)
        total = base_ref[pl.ds(pl.multiple_of(half * rows, rows), rows), :].astype(F32)
    for index, part in zip(indices, parts):
        for k in range(n):
            cols = pl.ds(pl.multiple_of((rank ^ k) * wide, wide), wide)
            lhs[:, cols] = part[k * rows : (k + 1) * rows, :]
        depth = pl.ds(pl.multiple_of((me ^ index) * width, width), width)
        total = total + jnp.dot(lhs[...], w_ref[depth, :], preferred_element_type=F32)
    outs[0][...] = total
    if len(outs) == 1:
        return
    outs[1][...] = total.astype(BF)
    squares = total * total
    lanes = squares[:, 0:HD]
    for g in range(1, squares.shape[1] // HD):
        lanes = lanes + squares[:, g * HD : (g + 1) * HD]
    outs[2][...] = jnp.sum(lanes.T, axis=0, keepdims=True)


def project(n, high, slots, ids, base, w_out, parts, indices, final):
    rows = parts[0].shape[0] // n
    width = w_out.shape[1]
    shapes = [jax.ShapeDtypeStruct((rows, width), F32)]
    if final:
        shapes.append(jax.ShapeDtypeStruct((rows, width), BF))
        shapes.append(jax.ShapeDtypeStruct((1, rows), F32))
    return pl.pallas_call(
        functools.partial(project_kernel, n, high, indices),
        out_shape=shapes,
        in_specs=[sm(), sm()] + [vm()] * (2 + len(parts)),
        out_specs=[vm()] * len(shapes),
        scratch_shapes=[VMEM((rows, width), BF)],
        compiler_params=params(20),
        cost_estimate=cost(2 * rows * width * width * len(parts), 2 * w_out.size * 1.5),
    )(slots, ids, base, w_out, *parts)


def normed_rows(res, sq_row, gain, model_width):
    rows, width = res.shape
    scale = lax.rsqrt(sq_row / model_width + EPS)
    column = jnp.broadcast_to(scale, (HD, rows)).T
    parts = [
        (res[:, g * HD : (g + 1) * HD] * column * gain[:, g * HD : (g + 1) * HD]).astype(BF)
        for g in range(width // HD)
    ]
    return jnp.concatenate(parts, axis=1)


def norm_kernel(model_width, res_ref, sq_ref, gain_ref, out_ref):
    out_ref[...] = normed_rows(res_ref[...], sq_ref[...], gain_ref[...], model_width)


def norm(model_width, res, sq, gain):
    return pl.pallas_call(
        functools.partial(norm_kernel, model_width),
        out_shape=jax.ShapeDtypeStruct(res.shape, BF),
        in_specs=[vm()] * 3,
        out_specs=vm(),
        compiler_params=params(8),
        cost_estimate=cost(4 * res.size, 6 * res.size),
    )(res, sq, gain)


def split(array):
    high = array.astype(jnp.bfloat16)
    low = (array - high.astype(np.float64)).astype(jnp.bfloat16)
    return high, low


def transform_tables(rows):
    size = 2 * rows
    freq = np.arange(rows)[:, None].astype(np.float64)
    time = np.arange(rows)[None, :].astype(np.float64)
    angle = 2 * np.pi * ((freq * time) % size) / size
    cosine = np.cos(angle)
    sine = -np.sin(angle)
    nyquist = np.where(np.arange(rows) % 2 == 0, 1.0, -1.0)
    sine[0] = nyquist
    forward = np.concatenate([cosine, sine], axis=0)
    late = 2 * np.pi * ((freq * (time + rows)) % size) / size
    back_cos = 2 * np.cos(late)
    back_cos[0] = 1.0
    back_sin = -2 * np.sin(late)
    back_sin[0] = np.where((np.arange(rows) + rows) % 2 == 0, 1.0, -1.0)
    backward = np.concatenate([back_cos, back_sin], axis=0).T / size
    return split(forward), split(backward)


def spectrum_kernel(filters_ref, len_ref, fh_ref, fl_ref, out_ref):
    taps = filters_ref.shape[1]
    lag = lax.broadcasted_iota(jnp.int32, filters_ref.shape, 1)
    used = jnp.where(lag < len_ref[...], filters_ref[...].astype(F32), 0.0).astype(BF)
    nt = (((1,), (1,)), ((), ()))
    fh = fh_ref[:, 0:taps]
    fl = fl_ref[:, 0:taps]
    out_ref[...] = lax.dot_general(fh, used, nt, preferred_element_type=F32) + lax.dot_general(
        fl, used, nt, preferred_element_type=F32
    )


def spectrum(filters, filter_len, forward):
    return pl.pallas_call(
        spectrum_kernel,
        out_shape=jax.ShapeDtypeStruct((forward[0].shape[0], filters.shape[0]), F32),
        in_specs=[vm()] * 4,
        out_specs=vm(),
        compiler_params=params(12),
        cost_estimate=cost(4 * forward[0].size * filters.shape[0], 8 * filters.size),
        name="spectrum",
    )(filters, filter_len.reshape(-1, 1), *forward)


def two(a_high, a_low, b):
    return jnp.dot(a_high, b, preferred_element_type=F32) + jnp.dot(
        a_low, b, preferred_element_type=F32
    )


def frequency_signs(rows):
    row_id = lax.broadcasted_iota(jnp.int32, (rows, 1), 0)
    return row_id == 0, jnp.where(row_id % 2 == 0, 1.0, -1.0)


def late_spectrum(own, fh, fl):
    rows = own.shape[0]
    first, sign = frequency_signs(rows)
    plain = two(fh, fl, own)
    return sign * plain[:rows], jnp.where(first, 1.0, sign) * plain[rows:]


def filtered(x_re, x_im, gh, gl, spec):
    rows = x_re.shape[0]
    first, _ = frequency_signs(rows)
    h_re, h_im = spec[:rows], spec[rows:]
    h_cross = jnp.where(first, 0.0, h_im)
    h_own = jnp.where(first, h_im, h_re)
    y = jnp.concatenate([x_re * h_re - x_im * h_cross, x_re * h_cross + x_im * h_own], axis=0)
    y_high = y.astype(BF)
    y_low = (y - y_high.astype(F32)).astype(BF)
    return two(gh, gl, y_high) + jnp.dot(gh, y_low, preferred_element_type=F32)


def conv_low_kernel(res_ref, own_ref, before_ref, spec_ref, skip_ref, fh, fl, gh, gl, out_ref):
    rows = res_ref.shape[0]
    own = own_ref[...]
    late_re, late_im = late_spectrum(own, fh[...], fl[...])
    early = two(fh[...], fl[...], before_ref[...])
    conv = filtered(early[:rows] + late_re, early[rows:] + late_im, gh[...], gl[...], spec_ref[...])
    out_ref[...] = (res_ref[...] + conv + skip_ref[...] * own.astype(F32)).astype(BF)


def conv_own_kernel(
    model_width, res_ref, sq_ref, spec_ref, gain_ref, skip_ref, fh, fl, gh, gl, out_ref
):
    own = normed_rows(res_ref[...], sq_ref[...], gain_ref[...], model_width)
    late_re, late_im = late_spectrum(own, fh[...], fl[...])
    conv = filtered(late_re, late_im, gh[...], gl[...], spec_ref[...])
    out_ref[...] = res_ref[...] + conv + skip_ref[...] * own.astype(F32)


def conv_high_kernel(
    n, model_width, slots_ref, ids_ref, part_ref, raw_ref, raw_sq_ref, low_ref, done_ref,
    spec_ref, gain_ref, fh, fl, gh, gl, out_ref,
):
    rows = part_ref.shape[0]
    last = ids_ref[0] == n - 1
    raw = normed_rows(raw_ref[...].astype(F32), raw_sq_ref[...], gain_ref[...], model_width)
    before = jnp.where(last, low_ref[...].astype(F32), raw.astype(F32)).astype(BF)
    early = two(fh[...], fl[...], before)
    conv = filtered(early[:rows], early[rows:], gh[...], gl[...], spec_ref[...])
    half = half_index(slots_ref, ids_ref, 1)
    out_ref[pl.ds(pl.multiple_of((1 - half) * rows, rows), rows), :] = done_ref[...]
    out_ref[pl.ds(pl.multiple_of(half * rows, rows), rows), :] = (part_ref[...] + conv).astype(BF)


def moved(block, axis, route):
    return lax.ppermute(block, axis, route)


def relayed_piece(own, near, size):
    inner = [(i, i ^ (size - 2)) for i in range(2, size - 2)]
    direct = moved(own, "mp", inner)
    ends = [(2, 0), (3, 1), (size - 4, size - 2), (size - 3, size - 1)]
    return direct + moved(near, "mp", ends)


def gather_mp(own, size, relay):
    chips = size // 2
    pieces = [own]
    for k in range(1, chips):
        if relay and k == chips - 1:
            pieces.append(relayed_piece(own, pieces[k - 1], size))
        else:
            pieces.append(moved(own, "mp", xor_route(size, 2 * k)))
    parts = []
    for piece in pieces:
        parts.append(piece)
        parts.append(moved(piece, "mp", xor_route(size, 1)))
    return parts


def total_mp(part, size):
    k = 1
    while k < size:
        part = part + moved(part, "mp", xor_route(size, k))
        k *= 2
    return part


def before_rows(block, distance):
    devices = range(lax.axis_size("seq"))
    return moved(block, "seq", [(i - distance, i) for i in devices if i - distance in devices])


def fast_device(
    incoming, queries, key_vecs, value_vecs, w_out, norm_gain, filters, filter_len, skip_gain, slot_map
):
    n = lax.axis_size("seq")
    mp_size = lax.axis_size("mp")
    rows, width = queries.shape[0] // 2, queries.shape[1]
    model_width = w_out.shape[0]
    ids = jnp.stack([lax.axis_index("seq"), lax.axis_index("mp")]).astype(jnp.int32)
    gain = norm_gain.reshape(1, -1)
    skip = skip_gain.reshape(1, -1)
    forward, backward = transform_tables(rows)
    forward = tuple(jnp.asarray(t) for t in forward)
    backward = tuple(jnp.asarray(t) for t in backward)

    def exchange(pieces):
        return [pieces[0]] + [moved(pieces[k], "seq", xor_route(n, k)) for k in range(1, n)]

    packed_low, packed_high = pack(n, slot_map, ids, queries, key_vecs, value_vecs)
    low = exchange(packed_low)
    high = exchange(packed_high)
    spec = spectrum(filters, filter_len, forward)

    att_low = exchange(attend(n, 0, rows, ids, low))
    parts_low = gather_mp(jnp.concatenate(att_low, axis=0), mp_size, True)
    att_high = exchange(attend(n, 1, rows, ids, low + high))
    parts_high = gather_mp(jnp.concatenate(att_high, axis=0), mp_size, False)

    every = tuple(range(mp_size))
    res_low, _, sq_low = project(n, 0, slot_map, ids, incoming, w_out, parts_low, every, True)
    norm_low = norm(model_width, res_low, total_mp(sq_low, mp_size), gain)
    before_low = before_rows(norm_low, 1)
    transforms = forward + backward
    done_low = pl.pallas_call(
        conv_low_kernel,
        out_shape=jax.ShapeDtypeStruct((rows, width), BF),
        in_specs=[vm()] * 9,
        out_specs=vm(),
        compiler_params=params(20),
        cost_estimate=cost(14 * rows * rows * width, 12 * rows * width),
        name="conv_low",
    )(res_low, norm_low, before_low, spec, skip, *transforms)

    most = mp_size - 2
    (base_high,) = project(
        n, 1, slot_map, ids, incoming, w_out, parts_high[:most], every[:most], False
    )
    res_high, raw_high, sq_high = project(
        n, 1, slot_map, ids, base_high, w_out, parts_high[most:], every[most:], True
    )
    raw_before = before_rows(raw_high, -1)
    sq_high = total_mp(sq_high, mp_size)
    sq_before = before_rows(sq_high, -1)
    part_high = pl.pallas_call(
        functools.partial(conv_own_kernel, model_width),
        out_shape=jax.ShapeDtypeStruct((rows, width), F32),
        in_specs=[vm()] * 9,
        out_specs=vm(),
        compiler_params=params(20),
        cost_estimate=cost(10 * rows * rows * width, 12 * rows * width),
        name="conv_own",
    )(res_high, sq_high, spec, gain, skip, *transforms)
    return pl.pallas_call(
        functools.partial(conv_high_kernel, n, model_width),
        out_shape=jax.ShapeDtypeStruct((2 * rows, width), BF),
        in_specs=[sm(), sm()] + [vm()] * 11,
        out_specs=vm(),
        compiler_params=params(20),
        cost_estimate=cost(10 * rows * rows * width, 12 * rows * width),
        name="conv_high",
    )(
        slot_map, ids, part_high, raw_before, sq_before, norm_low, done_low, spec, gain, *transforms
    )


def power_of_two(value):
    return value & (value - 1) == 0


def on_device(*arrays):
    n = lax.axis_size("seq")
    size = lax.axis_size("mp")
    queries, filters = arrays[1], arrays[6]
    rows = queries.shape[0] // 2
    heads = queries.shape[1] // HD
    fits = (
        heads % n == 0
        and power_of_two(n)
        and power_of_two(size)
        and size >= 8
        and rows % 256 == 0
        and filters.shape[1] <= rows
    )
    if not fits:
        return general_device(*arrays)
    return fast_device(*arrays)


def solution(mesh):
    placed = (
        P("seq", "mp"),
        P("seq", "mp"),
        P("seq", "mp"),
        P("seq", "mp"),
        P(None, "mp"),
        P("mp"),
        P("mp", None),
        P("mp"),
        P("mp"),
        P(),
    )
    return jax.shard_map(
        on_device, mesh=mesh, in_specs=placed, out_specs=P("seq", "mp"), check_vma=False
    )
```

```python
import functools

import jax
import jax.numpy as jnp
import numpy as np
from jax import lax
from jax.experimental import pallas as pl
from jax.experimental.pallas import tpu as pltpu
from jax.sharding import PartitionSpec as P


HD = 128
EPS = 1e-05
NEG = -1e30
LOG2E = 1.4426950408889634
BF = jnp.bfloat16
F32 = jnp.float32
VMEM = pltpu.VMEM
SMEM = pltpu.SMEM


def shifted(block, axis, distance):
    devices = range(lax.axis_size(axis))
    route = [(i - distance, i) for i in devices if i - distance in devices]
    return lax.ppermute(block, axis, route)


def block_update(running, query_heads, query_pos, key_part, value_part, key_pos):
    peak_now, total_now, accum_now = running
    key_count = key_part.shape[0]
    head_count = query_heads.shape[1]
    key_heads = key_part.reshape(key_count, head_count, HD)
    value_heads = value_part.reshape(key_count, head_count, HD)
    scores = jnp.einsum(
        "thd,shd->ths", query_heads, key_heads, preferred_element_type=F32
    ) * HD ** (-0.5)
    allowed = key_pos[None, None, :] <= query_pos[:, None, None]
    masked = jnp.where(allowed, scores, NEG)
    peak_next = jnp.maximum(peak_now, jnp.max(masked, axis=2))
    weights = jnp.where(allowed, jnp.exp(masked - peak_next[:, :, None]), 0.0)
    factor = jnp.exp(peak_now - peak_next)
    total_next = total_now * factor + jnp.sum(weights, axis=2)
    summed = jnp.einsum(
        "ths,shd->thd", weights.astype(BF), value_heads, preferred_element_type=F32
    )
    return (peak_next, total_next, accum_now * factor[:, :, None] + summed)


def attend_keys(running, query_heads, query_pos, key_part, value_part, key_pos, block_rows):
    block_count = key_part.shape[0] // block_rows

    def attend_advance(state, item):
        return block_update(state, query_heads, query_pos, *item), None

    stacked = (
        key_part.reshape(block_count, block_rows, -1),
        value_part.reshape(block_count, block_rows, -1),
        key_pos.reshape(block_count, block_rows),
    )
    running, _ = lax.scan(attend_advance, running, stacked)
    return running


def causal_window(extended, taps_lag):
    pair_count, twice, width = extended.shape
    length = twice // 2
    tap_count = taps_lag.shape[0]
    inner = int(np.gcd(tap_count, 16))

    def causal_advance(block, accum):
        base = block * inner
        window = lax.dynamic_slice_in_dim(
            extended, length - base - inner + 1, length + inner - 1, 1
        ).astype(F32)
        tap_block = lax.dynamic_slice_in_dim(taps_lag, base, inner, 0).astype(F32)
        for lag in range(inner):
            offset = inner - 1 - lag
            accum = accum + tap_block[lag][None, None, :] * window[:, offset : offset + length]
        return accum

    start = jnp.zeros((pair_count, length, width), F32)
    return lax.fori_loop(0, tap_count // inner, causal_advance, start)


def general_device(
    incoming, queries, key_vecs, value_vecs, w_out, norm_gain, filters, filter_len, skip_gain, slot_map
):
    tok_rows, local_width = queries.shape
    span_rows = tok_rows // 2
    head_count = local_width // HD
    model_width = w_out.shape[0]
    all_rows = slot_map.shape[0] * span_rows
    row_ids = jnp.arange(all_rows, dtype=jnp.int32)
    position = (
        jnp.repeat(slot_map, span_rows, total_repeat_length=all_rows) * span_rows
        + row_ids % span_rows
    )
    seq_rank = lax.axis_index("seq")
    seq_size = lax.axis_size("seq")
    own_pos = lax.dynamic_slice_in_dim(position, seq_rank * tok_rows, tok_rows)
    query_heads = queries.reshape(tok_rows, head_count, HD)
    keys_all = lax.all_gather(key_vecs, "seq", axis=0, tiled=True)
    values_all = lax.all_gather(value_vecs, "seq", axis=0, tiled=True)
    running = attend_keys(
        (
            jnp.full((tok_rows, head_count), NEG, F32),
            jnp.zeros((tok_rows, head_count), F32),
            jnp.zeros((tok_rows, head_count, HD), F32),
        ),
        query_heads,
        own_pos,
        keys_all,
        values_all,
        position,
        2 * tok_rows,
    )
    attention = (running[2] / running[1][:, :, None]).reshape(-1, local_width).astype(BF)
    projected = jnp.dot(
        lax.all_gather(attention, "mp", axis=1, tiled=True), w_out, preferred_element_type=F32
    )
    residual = incoming.astype(F32) + projected
    square_total = lax.psum(jnp.sum(residual * residual, axis=1), "mp")
    scale = lax.rsqrt(square_total / model_width + EPS)
    normed = (residual * scale[:, None] * norm_gain[None, :]).astype(BF)
    tap_count = filters.shape[1]
    taps = jnp.where(
        jnp.arange(tap_count, dtype=jnp.int32)[None, :] < filter_len[:, None],
        filters,
        jnp.zeros((), filters.dtype),
    )
    pair_ids = lax.dynamic_slice_in_dim(slot_map, 2 * seq_rank, 2)
    low_first = pair_ids[0] < pair_ids[1]
    slots = normed.reshape(2, span_rows, local_width)
    low_rows = jnp.where(low_first, slots[0], slots[1])
    high_rows = jnp.where(low_first, slots[1], slots[0])
    own_pair = jnp.stack([low_rows, high_rows])
    low_before = shifted(low_rows, "seq", 1)
    high_before = shifted(high_rows, "seq", -1)
    high_before = jnp.where(seq_rank == seq_size - 1, low_rows, high_before)
    before_pair = jnp.stack([low_before, high_before])
    conv_pair = causal_window(jnp.concatenate([before_pair, own_pair], axis=1), taps.T)
    conv_slots = jnp.where(low_first, conv_pair, conv_pair[::-1])
    conv_rows = conv_slots.reshape(tok_rows, local_width)
    layer_out = residual + conv_rows + skip_gain[None, :] * normed.astype(F32)
    return layer_out.astype(BF)


def params(megabytes=20):
    return pltpu.CompilerParams(vmem_limit_bytes=megabytes << 20)


def cost(flops, moved, exps=0):
    return pl.CostEstimate(flops=int(flops), bytes_accessed=int(moved), transcendentals=int(exps))


def vm():
    return pl.BlockSpec(memory_space=VMEM)


def sm():
    return pl.BlockSpec(memory_space=SMEM)


def xor_route(count, k):
    return [(i, i ^ k) for i in range(count)]


def half_index(slots_ref, ids_ref, high):
    rank = ids_ref[0]
    first_is_high = slots_ref[2 * rank] > slots_ref[2 * rank + 1]
    return jnp.where(first_is_high, 1 - high, high).astype(jnp.int32)


def pack_kernel(n, high, slots_ref, ids_ref, q_ref, k_ref, v_ref, *rest):
    outs, sem = rest[:n], rest[n]
    rank = ids_ref[0]
    rows = outs[0].shape[0] // 3
    wide = outs[0].shape[1]
    half = half_index(slots_ref, ids_ref, high)
    source_rows = pl.ds(pl.multiple_of(half * rows, rows), rows)
    copies = []
    for k in range(n):
        cols = pl.ds(pl.multiple_of((rank ^ k) * wide, wide), wide)
        for a, ref in enumerate((q_ref, k_ref, v_ref)):
            copy = pltpu.make_async_copy(
                ref.at[source_rows, cols],
                outs[k].at[a * rows : (a + 1) * rows, :],
                sem.at[k, a],
            )
            copy.start()
            copies.append(copy)
    for copy in copies:
        copy.wait()


def pack(n, high, slots, ids, arrays):
    rows, width = arrays[0].shape[0] // 2, arrays[0].shape[1]
    piece = jax.ShapeDtypeStruct((3 * rows, width // n), BF)
    return pl.pallas_call(
        functools.partial(pack_kernel, n, high),
        out_shape=[piece] * n,
        in_specs=[sm(), sm()] + [pl.BlockSpec(memory_space=pltpu.HBM)] * 3,
        out_specs=[vm()] * n,
        scratch_shapes=[pltpu.SemaphoreType.DMA((n, 3))],
        compiler_params=params(8),
        cost_estimate=cost(0, 12 * rows * width),
    )(slots, ids, *(pltpu.with_memory_space_constraint(x, pltpu.HBM) for x in arrays))


def attend_kernel(n, high, rows, ids_ref, *refs):
    chunks = 2 if high else 1
    ins = refs[: chunks * n]
    outs = refs[chunks * n : chunks * n + n]
    q_all, k_all, v_all, o_all = refs[chunks * n + n :]
    rank = ids_ref[0]
    wide = outs[0].shape[1]

    def place(block):
        return pl.ds(pl.multiple_of(block * rows, rows), rows)

    for c in range(chunks):
        for k in range(n):
            source = rank ^ k
            block = source if c == 0 else 2 * n - 1 - source
            piece = ins[c * n + k]
            if c == chunks - 1:
                q_all[place(block - c * n), :] = piece[0:rows, :]
            k_all[place(block), :] = piece[rows : 2 * rows, :]
            v_all[place(block), :] = piece[2 * rows : 3 * rows, :]
    base = n if high else 0
    row_id = lax.broadcasted_iota(jnp.int32, (rows, rows), 0)
    col_id = lax.broadcasted_iota(jnp.int32, (rows, rows), 1)
    causal = col_id <= row_id
    factor = HD ** (-0.5) * LOG2E
    nt = (((1,), (1,)), ((), ()))
    for b in range(n):
        past = (base + b) * rows
        for h in range(wide // HD):
            cols = slice(h * HD, (h + 1) * HD)
            q = q_all[b * rows : (b + 1) * rows, cols]
            near = lax.dot_general(
                q, k_all[past : past + rows, cols], nt, preferred_element_type=F32
            )
            near = jnp.where(causal, near, NEG)
            peak = jnp.max(near, axis=1, keepdims=True)
            if past:
                far = lax.dot_general(q, k_all[0:past, cols], nt, preferred_element_type=F32)
                peak = jnp.maximum(peak, jnp.max(far, axis=1, keepdims=True))
            w_near = jnp.exp2((near - peak) * factor)
            total = jnp.sum(w_near, axis=1, keepdims=True)
            summed = jnp.dot(
                w_near.astype(BF), v_all[past : past + rows, cols], preferred_element_type=F32
            )
            if past:
                w_far = jnp.exp2((far - peak) * factor)
                total = total + jnp.sum(w_far, axis=1, keepdims=True)
                summed = summed + jnp.dot(
                    w_far.astype(BF), v_all[0:past, cols], preferred_element_type=F32
                )
            owner = n - 1 - b if high else b
            o_all[owner * rows : (owner + 1) * rows, cols] = (summed / total).astype(BF)
    for k in range(n):
        outs[k][...] = o_all[place(rank ^ k), :]


def attend(n, high, rows, ids, pieces):
    wide = pieces[0].shape[1]
    chunks = 2 if high else 1
    pairs = n * (n + 1) // 2 + (n * n if high else 0)
    area = pairs * rows * rows * (wide // HD)
    return pl.pallas_call(
        functools.partial(attend_kernel, n, high, rows),
        out_shape=[jax.ShapeDtypeStruct((rows, wide), BF)] * n,
        in_specs=[sm()] + [vm()] * len(pieces),
        out_specs=[vm()] * n,
        scratch_shapes=[
            VMEM((n * rows, wide), BF),
            VMEM((chunks * n * rows, wide), BF),
            VMEM((chunks * n * rows, wide), BF),
            VMEM((n * rows, wide), BF),
        ],
        compiler_params=params(32),
        cost_estimate=cost(4 * area * HD, 8 * n * rows * wide * chunks, area),
        name="attend_high" if high else "attend_low",
    )(ids, *pieces)


def project_kernel(n, indices, slots_ref, ids_ref, base_ref, w_ref, *refs):
    count = len(indices)
    chunks, outs, lhs = (refs[:count], refs[count : 2 * count]), refs[2 * count : -1], refs[-1]
    rank = ids_ref[0]
    me = ids_ref[1]
    size, width = lhs.shape
    rows = size // 2
    wide = width // n
    if base_ref.dtype == F32:
        total = base_ref[...]
    else:
        halves = [half_index(slots_ref, ids_ref, high) * rows for high in range(2)]
        total = jnp.concatenate(
            [base_ref[pl.ds(pl.multiple_of(h, rows), rows), :] for h in halves], axis=0
        ).astype(F32)
    for j, index in enumerate(indices):
        for high in range(2):
            for k in range(n):
                cols = pl.ds(pl.multiple_of((rank ^ k) * wide, wide), wide)
                lhs[high * rows : (high + 1) * rows, cols] = chunks[high][j][
                    k * rows : (k + 1) * rows, :
                ]
        depth = pl.ds(pl.multiple_of((me ^ index) * width, width), width)
        total = total + jnp.dot(lhs[...], w_ref[depth, :], preferred_element_type=F32)
    outs[0][...] = total
    if len(outs) == 1:
        return
    outs[1][...] = total[:rows].astype(BF)
    outs[2][...] = total[rows:].astype(BF)
    squares = total * total
    lanes = squares[:, 0:HD]
    for g in range(1, squares.shape[1] // HD):
        lanes = lanes + squares[:, g * HD : (g + 1) * HD]
    outs[3][...] = jnp.sum(lanes.T, axis=0, keepdims=True)


def project(n, slots, ids, base, w_out, low, high, indices, final):
    size, width = base.shape
    shapes = [jax.ShapeDtypeStruct((size, width), F32)]
    if final:
        shapes += [jax.ShapeDtypeStruct((size // 2, width), BF)] * 2
        shapes.append(jax.ShapeDtypeStruct((1, size), F32))
    return pl.pallas_call(
        functools.partial(project_kernel, n, indices),
        out_shape=shapes,
        in_specs=[sm(), sm()] + [vm()] * (2 + 2 * len(indices)),
        out_specs=[vm()] * len(shapes),
        scratch_shapes=[VMEM((size, width), BF)],
        compiler_params=params(20),
        cost_estimate=cost(2 * size * width * width * len(indices), 2 * w_out.size * 1.5),
    )(slots, ids, base, w_out, *low, *high)


def normed_rows(res, sq_row, gain, model_width):
    rows, width = res.shape
    scale = lax.rsqrt(sq_row / model_width + EPS)
    column = jnp.broadcast_to(scale, (HD, rows)).T
    parts = [
        (res[:, g * HD : (g + 1) * HD] * column * gain[:, g * HD : (g + 1) * HD]).astype(BF)
        for g in range(width // HD)
    ]
    return jnp.concatenate(parts, axis=1)


def split(array):
    high = array.astype(jnp.bfloat16)
    low = (array - high.astype(np.float64)).astype(jnp.bfloat16)
    return high, low


def transform_tables(rows):
    size = 2 * rows
    freq = np.arange(rows)[:, None].astype(np.float64)
    time = np.arange(rows)[None, :].astype(np.float64)
    angle = 2 * np.pi * ((freq * time) % size) / size
    cosine = np.cos(angle)
    sine = -np.sin(angle)
    nyquist = np.where(np.arange(rows) % 2 == 0, 1.0, -1.0)
    sine[0] = nyquist
    forward = np.concatenate([cosine, sine], axis=0)
    late = 2 * np.pi * ((freq * (time + rows)) % size) / size
    back_cos = 2 * np.cos(late)
    back_cos[0] = 1.0
    back_sin = -2 * np.sin(late)
    back_sin[0] = np.where((np.arange(rows) + rows) % 2 == 0, 1.0, -1.0)
    backward = np.concatenate([back_cos, back_sin], axis=0).T / size
    return split(forward), split(backward)


def spectrum_kernel(filters_ref, len_ref, fh_ref, fl_ref, out_ref):
    taps = filters_ref.shape[1]
    lag = lax.broadcasted_iota(jnp.int32, filters_ref.shape, 1)
    used = jnp.where(lag < len_ref[...], filters_ref[...].astype(F32), 0.0).astype(BF)
    nt = (((1,), (1,)), ((), ()))
    fh = fh_ref[:, 0:taps]
    fl = fl_ref[:, 0:taps]
    out_ref[...] = lax.dot_general(fh, used, nt, preferred_element_type=F32) + lax.dot_general(
        fl, used, nt, preferred_element_type=F32
    )


def spectrum(filters, filter_len, forward):
    return pl.pallas_call(
        spectrum_kernel,
        out_shape=jax.ShapeDtypeStruct((forward[0].shape[0], filters.shape[0]), F32),
        in_specs=[vm()] * 4,
        out_specs=vm(),
        compiler_params=params(12),
        cost_estimate=cost(4 * forward[0].size * filters.shape[0], 8 * filters.size),
        name="spectrum",
    )(filters, filter_len.reshape(-1, 1), *forward)


def two(a_high, a_low, b):
    return jnp.dot(a_high, b, preferred_element_type=F32) + jnp.dot(
        a_low, b, preferred_element_type=F32
    )


def frequency_signs(rows):
    row_id = lax.broadcasted_iota(jnp.int32, (rows, 1), 0)
    return row_id == 0, jnp.where(row_id % 2 == 0, 1.0, -1.0)


def late_spectrum(own, fh, fl):
    rows = own.shape[0]
    first, sign = frequency_signs(rows)
    plain = two(fh, fl, own)
    return sign * plain[:rows], jnp.where(first, 1.0, sign) * plain[rows:]


def filtered(x_re, x_im, gh, gl, spec):
    rows = x_re.shape[0]
    first, _ = frequency_signs(rows)
    h_re, h_im = spec[:rows], spec[rows:]
    h_cross = jnp.where(first, 0.0, h_im)
    h_own = jnp.where(first, h_im, h_re)
    y = jnp.concatenate([x_re * h_re - x_im * h_cross, x_re * h_cross + x_im * h_own], axis=0)
    y_high = y.astype(BF)
    y_low = (y - y_high.astype(F32)).astype(BF)
    return two(gh, gl, y_high) + jnp.dot(gh, y_low, preferred_element_type=F32)


def conv_own_kernel(
    model_width, res_ref, sq_ref, spec_ref, gain_ref, skip_ref, fh, fl, gh, gl, out_ref, low_ref
):
    rows = spec_ref.shape[0] // 2
    for high in range(2):
        part = slice(high * rows, (high + 1) * rows)
        res = res_ref[part, :]
        own = normed_rows(res, sq_ref[:, part], gain_ref[...], model_width)
        if not high:
            low_ref[...] = own
        late_re, late_im = late_spectrum(own, fh[...], fl[...])
        conv = filtered(late_re, late_im, gh[...], gl[...], spec_ref[...])
        out_ref[part, :] = res + conv + skip_ref[...] * own.astype(F32)


def conv_last_kernel(
    n, model_width, slots_ref, ids_ref, part_ref, low_ref, raw_low, raw_high, sq_low, sq_high,
    spec_ref, gain_ref, fh, fl, gh, gl, out_ref,
):
    rows = low_ref.shape[0]
    last = ids_ref[0] == n - 1
    gain = gain_ref[...]
    for high, raw_ref, sq_ref in ((0, raw_low, sq_low), (1, raw_high, sq_high)):
        before = normed_rows(raw_ref[...].astype(F32), sq_ref[...], gain, model_width)
        if high:
            before = jnp.where(last, low_ref[...].astype(F32), before.astype(F32)).astype(BF)
        early = two(fh[...], fl[...], before)
        conv = filtered(early[:rows], early[rows:], gh[...], gl[...], spec_ref[...])
        half = half_index(slots_ref, ids_ref, high)
        out_ref[pl.ds(pl.multiple_of(half * rows, rows), rows), :] = (
            part_ref[high * rows : (high + 1) * rows, :] + conv
        ).astype(BF)


def moved(block, axis, route):
    return lax.ppermute(block, axis, route)


def gather_mp(own, size):
    parts = []
    for k in range(size // 2):
        piece = moved(own, "mp", xor_route(size, 2 * k)) if k else own
        parts.append(piece)
        parts.append(moved(piece, "mp", xor_route(size, 1)))
    return parts


def total_mp(part, size):
    k = 1
    while k < size:
        part = part + moved(part, "mp", xor_route(size, k))
        k *= 2
    return part


def before_rows(block, distance):
    devices = range(lax.axis_size("seq"))
    return moved(block, "seq", [(i - distance, i) for i in devices if i - distance in devices])


def fast_device(
    incoming, queries, key_vecs, value_vecs, w_out, norm_gain, filters, filter_len, skip_gain, slot_map
):
    n = lax.axis_size("seq")
    mp_size = lax.axis_size("mp")
    rows, width = queries.shape[0] // 2, queries.shape[1]
    model_width = w_out.shape[0]
    ids = jnp.stack([lax.axis_index("seq"), lax.axis_index("mp")]).astype(jnp.int32)
    gain = norm_gain.reshape(1, -1)
    skip = skip_gain.reshape(1, -1)
    forward, backward = transform_tables(rows)
    forward = tuple(jnp.asarray(t) for t in forward)
    backward = tuple(jnp.asarray(t) for t in backward)

    def exchange(pieces):
        return [pieces[0]] + [moved(pieces[k], "seq", xor_route(n, k)) for k in range(1, n)]

    inputs = (queries, key_vecs, value_vecs)
    low = exchange(pack(n, 0, slot_map, ids, inputs))
    high = exchange(pack(n, 1, slot_map, ids, inputs))
    spec = spectrum(filters, filter_len, forward)

    att_low = exchange(attend(n, 0, rows, ids, low))
    parts_low = gather_mp(jnp.concatenate(att_low, axis=0), mp_size)
    att_high = exchange(attend(n, 1, rows, ids, low + high))
    parts_high = gather_mp(jnp.concatenate(att_high, axis=0), mp_size)

    most = mp_size // 2
    first, last = tuple(range(most)), tuple(range(most, mp_size))
    (base,) = project(
        n, slot_map, ids, incoming, w_out,
        parts_low[:most], parts_high[:most], first, False,
    )
    res, raw_low, raw_high, squares = project(
        n, slot_map, ids, base, w_out,
        parts_low[most:], parts_high[most:], last, True,
    )
    raw_low = before_rows(raw_low, 1)
    raw_high = before_rows(raw_high, -1)
    squares = total_mp(squares, mp_size)
    sq_low = before_rows(squares[:, :rows], 1)
    sq_high = before_rows(squares[:, rows:], -1)
    transforms = forward + backward
    part, norm_low = pl.pallas_call(
        functools.partial(conv_own_kernel, model_width),
        out_shape=[
            jax.ShapeDtypeStruct((2 * rows, width), F32),
            jax.ShapeDtypeStruct((rows, width), BF),
        ],
        in_specs=[vm()] * 9,
        out_specs=[vm()] * 2,
        compiler_params=params(20),
        cost_estimate=cost(20 * rows * rows * width, 24 * rows * width),
        name="conv_own",
    )(res, squares, spec, gain, skip, *transforms)
    return pl.pallas_call(
        functools.partial(conv_last_kernel, n, model_width),
        out_shape=jax.ShapeDtypeStruct((2 * rows, width), BF),
        in_specs=[sm(), sm()] + [vm()] * 12,
        out_specs=vm(),
        compiler_params=params(20),
        cost_estimate=cost(20 * rows * rows * width, 24 * rows * width),
        name="conv_last",
    )(
        slot_map, ids, part, norm_low, raw_low, raw_high, sq_low, sq_high, spec, gain, *transforms
    )


def power_of_two(value):
    return value & (value - 1) == 0


def on_device(*arrays):
    n = lax.axis_size("seq")
    size = lax.axis_size("mp")
    queries, filters = arrays[1], arrays[6]
    rows = queries.shape[0] // 2
    heads = queries.shape[1] // HD
    fits = (
        heads % n == 0
        and power_of_two(n)
        and power_of_two(size)
        and size >= 4
        and rows % 256 == 0
        and filters.shape[1] <= rows
    )
    if not fits:
        return general_device(*arrays)
    return fast_device(*arrays)


def solution(mesh):
    placed = (
        P("seq", "mp"),
        P("seq", "mp"),
        P("seq", "mp"),
        P("seq", "mp"),
        P(None, "mp"),
        P("mp"),
        P("mp", None),
        P("mp"),
        P("mp"),
        P(),
    )
    return jax.shard_map(
        on_device, mesh=mesh, in_specs=placed, out_specs=P("seq", "mp"), check_vma=False
    )
```

```python
import functools

import jax
import jax.numpy as jnp
import numpy as np
from jax import lax
from jax.experimental import pallas as pl
from jax.experimental.pallas import tpu as pltpu
from jax.sharding import PartitionSpec as P


HD = 128
EPS = 1e-05
NEG = -1e30
LOG2E = 1.4426950408889634
BF = jnp.bfloat16
F32 = jnp.float32
VMEM = pltpu.VMEM
SMEM = pltpu.SMEM


def shifted(block, axis, distance):
    devices = range(lax.axis_size(axis))
    route = [(i - distance, i) for i in devices if i - distance in devices]
    return lax.ppermute(block, axis, route)


def block_update(running, query_heads, query_pos, key_part, value_part, key_pos):
    peak_now, total_now, accum_now = running
    key_count = key_part.shape[0]
    head_count = query_heads.shape[1]
    key_heads = key_part.reshape(key_count, head_count, HD)
    value_heads = value_part.reshape(key_count, head_count, HD)
    scores = jnp.einsum(
        "thd,shd->ths", query_heads, key_heads, preferred_element_type=F32
    ) * HD ** (-0.5)
    allowed = key_pos[None, None, :] <= query_pos[:, None, None]
    masked = jnp.where(allowed, scores, NEG)
    peak_next = jnp.maximum(peak_now, jnp.max(masked, axis=2))
    weights = jnp.where(allowed, jnp.exp(masked - peak_next[:, :, None]), 0.0)
    factor = jnp.exp(peak_now - peak_next)
    total_next = total_now * factor + jnp.sum(weights, axis=2)
    summed = jnp.einsum(
        "ths,shd->thd", weights.astype(BF), value_heads, preferred_element_type=F32
    )
    return (peak_next, total_next, accum_now * factor[:, :, None] + summed)


def attend_keys(running, query_heads, query_pos, key_part, value_part, key_pos, block_rows):
    block_count = key_part.shape[0] // block_rows

    def attend_advance(state, item):
        return block_update(state, query_heads, query_pos, *item), None

    stacked = (
        key_part.reshape(block_count, block_rows, -1),
        value_part.reshape(block_count, block_rows, -1),
        key_pos.reshape(block_count, block_rows),
    )
    running, _ = lax.scan(attend_advance, running, stacked)
    return running


def causal_window(extended, taps_lag):
    pair_count, twice, width = extended.shape
    length = twice // 2
    tap_count = taps_lag.shape[0]
    inner = int(np.gcd(tap_count, 16))

    def causal_advance(block, accum):
        base = block * inner
        window = lax.dynamic_slice_in_dim(
            extended, length - base - inner + 1, length + inner - 1, 1
        ).astype(F32)
        tap_block = lax.dynamic_slice_in_dim(taps_lag, base, inner, 0).astype(F32)
        for lag in range(inner):
            offset = inner - 1 - lag
            accum = accum + tap_block[lag][None, None, :] * window[:, offset : offset + length]
        return accum

    start = jnp.zeros((pair_count, length, width), F32)
    return lax.fori_loop(0, tap_count // inner, causal_advance, start)


def general_device(
    incoming, queries, key_vecs, value_vecs, w_out, norm_gain, filters, filter_len, skip_gain, slot_map
):
    tok_rows, local_width = queries.shape
    span_rows = tok_rows // 2
    head_count = local_width // HD
    model_width = w_out.shape[0]
    all_rows = slot_map.shape[0] * span_rows
    row_ids = jnp.arange(all_rows, dtype=jnp.int32)
    position = (
        jnp.repeat(slot_map, span_rows, total_repeat_length=all_rows) * span_rows
        + row_ids % span_rows
    )
    seq_rank = lax.axis_index("seq")
    seq_size = lax.axis_size("seq")
    own_pos = lax.dynamic_slice_in_dim(position, seq_rank * tok_rows, tok_rows)
    query_heads = queries.reshape(tok_rows, head_count, HD)
    keys_all = lax.all_gather(key_vecs, "seq", axis=0, tiled=True)
    values_all = lax.all_gather(value_vecs, "seq", axis=0, tiled=True)
    running = attend_keys(
        (
            jnp.full((tok_rows, head_count), NEG, F32),
            jnp.zeros((tok_rows, head_count), F32),
            jnp.zeros((tok_rows, head_count, HD), F32),
        ),
        query_heads,
        own_pos,
        keys_all,
        values_all,
        position,
        2 * tok_rows,
    )
    attention = (running[2] / running[1][:, :, None]).reshape(-1, local_width).astype(BF)
    projected = jnp.dot(
        lax.all_gather(attention, "mp", axis=1, tiled=True), w_out, preferred_element_type=F32
    )
    residual = incoming.astype(F32) + projected
    square_total = lax.psum(jnp.sum(residual * residual, axis=1), "mp")
    scale = lax.rsqrt(square_total / model_width + EPS)
    normed = (residual * scale[:, None] * norm_gain[None, :]).astype(BF)
    tap_count = filters.shape[1]
    taps = jnp.where(
        jnp.arange(tap_count, dtype=jnp.int32)[None, :] < filter_len[:, None],
        filters,
        jnp.zeros((), filters.dtype),
    )
    pair_ids = lax.dynamic_slice_in_dim(slot_map, 2 * seq_rank, 2)
    low_first = pair_ids[0] < pair_ids[1]
    slots = normed.reshape(2, span_rows, local_width)
    low_rows = jnp.where(low_first, slots[0], slots[1])
    high_rows = jnp.where(low_first, slots[1], slots[0])
    own_pair = jnp.stack([low_rows, high_rows])
    low_before = shifted(low_rows, "seq", 1)
    high_before = shifted(high_rows, "seq", -1)
    high_before = jnp.where(seq_rank == seq_size - 1, low_rows, high_before)
    before_pair = jnp.stack([low_before, high_before])
    conv_pair = causal_window(jnp.concatenate([before_pair, own_pair], axis=1), taps.T)
    conv_slots = jnp.where(low_first, conv_pair, conv_pair[::-1])
    conv_rows = conv_slots.reshape(tok_rows, local_width)
    layer_out = residual + conv_rows + skip_gain[None, :] * normed.astype(F32)
    return layer_out.astype(BF)


def params(megabytes=20):
    return pltpu.CompilerParams(vmem_limit_bytes=megabytes << 20)


def cost(flops, moved, exps=0):
    return pl.CostEstimate(flops=int(flops), bytes_accessed=int(moved), transcendentals=int(exps))


def vm():
    return pl.BlockSpec(memory_space=VMEM)


def sm():
    return pl.BlockSpec(memory_space=SMEM)


def xor_route(count, k):
    return [(i, i ^ k) for i in range(count)]


def half_index(slots_ref, ids_ref, high):
    rank = ids_ref[0]
    first_is_high = slots_ref[2 * rank] > slots_ref[2 * rank + 1]
    return jnp.where(first_is_high, 1 - high, high).astype(jnp.int32)


def pack_kernel(n, high, slots_ref, ids_ref, q_ref, k_ref, v_ref, *rest):
    outs, sem = rest[:n], rest[n]
    rank = ids_ref[0]
    rows = outs[0].shape[0] // 3
    wide = outs[0].shape[1]
    half = half_index(slots_ref, ids_ref, high)
    source_rows = pl.ds(pl.multiple_of(half * rows, rows), rows)
    copies = []
    for k in range(n):
        cols = pl.ds(pl.multiple_of((rank ^ k) * wide, wide), wide)
        for a, ref in enumerate((q_ref, k_ref, v_ref)):
            copy = pltpu.make_async_copy(
                ref.at[source_rows, cols],
                outs[k].at[a * rows : (a + 1) * rows, :],
                sem.at[k, a],
            )
            copy.start()
            copies.append(copy)
    for copy in copies:
        copy.wait()


def pack(n, high, slots, ids, arrays):
    rows, width = arrays[0].shape[0] // 2, arrays[0].shape[1]
    piece = jax.ShapeDtypeStruct((3 * rows, width // n), BF)
    return pl.pallas_call(
        functools.partial(pack_kernel, n, high),
        out_shape=[piece] * n,
        in_specs=[sm(), sm()] + [pl.BlockSpec(memory_space=pltpu.HBM)] * 3,
        out_specs=[vm()] * n,
        scratch_shapes=[pltpu.SemaphoreType.DMA((n, 3))],
        compiler_params=params(8),
        cost_estimate=cost(0, 12 * rows * width),
    )(slots, ids, *(pltpu.with_memory_space_constraint(x, pltpu.HBM) for x in arrays))


def attend_kernel(n, high, rows, ids_ref, *refs):
    chunks = 2 if high else 1
    ins = refs[: chunks * n]
    outs = refs[chunks * n : chunks * n + n]
    q_all, k_all, v_all, o_all = refs[chunks * n + n :]
    rank = ids_ref[0]
    wide = outs[0].shape[1]

    def place(block):
        return pl.ds(pl.multiple_of(block * rows, rows), rows)

    for c in range(chunks):
        for k in range(n):
            source = rank ^ k
            block = source if c == 0 else 2 * n - 1 - source
            piece = ins[c * n + k]
            if c == chunks - 1:
                q_all[place(block - c * n), :] = piece[0:rows, :]
            k_all[place(block), :] = piece[rows : 2 * rows, :]
            v_all[place(block), :] = piece[2 * rows : 3 * rows, :]
    base = n if high else 0
    row_id = lax.broadcasted_iota(jnp.int32, (rows, rows), 0)
    col_id = lax.broadcasted_iota(jnp.int32, (rows, rows), 1)
    causal = col_id <= row_id
    factor = HD ** (-0.5) * LOG2E
    nt = (((1,), (1,)), ((), ()))
    for b in range(n):
        past = (base + b) * rows
        for h in range(wide // HD):
            cols = slice(h * HD, (h + 1) * HD)
            q = q_all[b * rows : (b + 1) * rows, cols]
            near = lax.dot_general(
                q, k_all[past : past + rows, cols], nt, preferred_element_type=F32
            )
            near = jnp.where(causal, near, NEG)
            peak = jnp.max(near, axis=1, keepdims=True)
            if past:
                far = lax.dot_general(q, k_all[0:past, cols], nt, preferred_element_type=F32)
                peak = jnp.maximum(peak, jnp.max(far, axis=1, keepdims=True))
            w_near = jnp.exp2((near - peak) * factor)
            total = jnp.sum(w_near, axis=1, keepdims=True)
            summed = jnp.dot(
                w_near.astype(BF), v_all[past : past + rows, cols], preferred_element_type=F32
            )
            if past:
                w_far = jnp.exp2((far - peak) * factor)
                total = total + jnp.sum(w_far, axis=1, keepdims=True)
                summed = summed + jnp.dot(
                    w_far.astype(BF), v_all[0:past, cols], preferred_element_type=F32
                )
            owner = n - 1 - b if high else b
            o_all[owner * rows : (owner + 1) * rows, cols] = (summed / total).astype(BF)
    for k in range(n):
        outs[k][...] = o_all[place(rank ^ k), :]


def attend(n, high, rows, ids, pieces):
    wide = pieces[0].shape[1]
    chunks = 2 if high else 1
    pairs = n * (n + 1) // 2 + (n * n if high else 0)
    area = pairs * rows * rows * (wide // HD)
    return pl.pallas_call(
        functools.partial(attend_kernel, n, high, rows),
        out_shape=[jax.ShapeDtypeStruct((rows, wide), BF)] * n,
        in_specs=[sm()] + [vm()] * len(pieces),
        out_specs=[vm()] * n,
        scratch_shapes=[
            VMEM((n * rows, wide), BF),
            VMEM((chunks * n * rows, wide), BF),
            VMEM((chunks * n * rows, wide), BF),
            VMEM((n * rows, wide), BF),
        ],
        compiler_params=params(32),
        cost_estimate=cost(4 * area * HD, 8 * n * rows * wide * chunks, area),
        name="attend_high" if high else "attend_low",
    )(ids, *pieces)


def project_kernel(n, high, indices, slots_ref, ids_ref, base_ref, w_ref, *refs):
    count = len(indices)
    parts, outs, lhs = refs[:count], refs[count:-1], refs[-1]
    rank = ids_ref[0]
    me = ids_ref[1]
    rows, width = lhs.shape
    wide = width // n
    if base_ref.shape[0] == rows:
        total = base_ref[...]
    else:
        half = half_index(slots_ref, ids_ref, high)
        total = base_ref[pl.ds(pl.multiple_of(half * rows, rows), rows), :].astype(F32)
    for index, part in zip(indices, parts):
        for k in range(n):
            cols = pl.ds(pl.multiple_of((rank ^ k) * wide, wide), wide)
            lhs[:, cols] = part[k * rows : (k + 1) * rows, :]
        depth = pl.ds(pl.multiple_of((me ^ index) * width, width), width)
        total = total + jnp.dot(lhs[...], w_ref[depth, :], preferred_element_type=F32)
    outs[0][...] = total
    if len(outs) == 1:
        return
    outs[1][...] = total.astype(BF)
    squares = total * total
    lanes = squares[:, 0:HD]
    for g in range(1, squares.shape[1] // HD):
        lanes = lanes + squares[:, g * HD : (g + 1) * HD]
    outs[2][...] = jnp.sum(lanes.T, axis=0, keepdims=True)


def project(n, high, slots, ids, base, w_out, parts, indices, final):
    rows = parts[0].shape[0] // n
    width = w_out.shape[1]
    shapes = [jax.ShapeDtypeStruct((rows, width), F32)]
    if final:
        shapes.append(jax.ShapeDtypeStruct((rows, width), BF))
        shapes.append(jax.ShapeDtypeStruct((1, rows), F32))
    return pl.pallas_call(
        functools.partial(project_kernel, n, high, indices),
        out_shape=shapes,
        in_specs=[sm(), sm()] + [vm()] * (2 + len(parts)),
        out_specs=[vm()] * len(shapes),
        scratch_shapes=[VMEM((rows, width), BF)],
        compiler_params=params(20),
        cost_estimate=cost(2 * rows * width * width * len(parts), 2 * w_out.size * 1.5),
    )(slots, ids, base, w_out, *parts)


def normed_rows(res, sq_row, gain, model_width):
    rows, width = res.shape
    scale = lax.rsqrt(sq_row / model_width + EPS)
    column = jnp.broadcast_to(scale, (HD, rows)).T
    parts = [
        (res[:, g * HD : (g + 1) * HD] * column * gain[:, g * HD : (g + 1) * HD]).astype(BF)
        for g in range(width // HD)
    ]
    return jnp.concatenate(parts, axis=1)


def norm_kernel(model_width, res_ref, sq_ref, gain_ref, out_ref):
    out_ref[...] = normed_rows(res_ref[...], sq_ref[...], gain_ref[...], model_width)


def norm(model_width, res, sq, gain):
    return pl.pallas_call(
        functools.partial(norm_kernel, model_width),
        out_shape=jax.ShapeDtypeStruct(res.shape, BF),
        in_specs=[vm()] * 3,
        out_specs=vm(),
        compiler_params=params(8),
        cost_estimate=cost(4 * res.size, 6 * res.size),
    )(res, sq, gain)


def split(array):
    high = array.astype(jnp.bfloat16)
    low = (array - high.astype(np.float64)).astype(jnp.bfloat16)
    return high, low


def transform_tables(rows):
    size = 2 * rows
    freq = np.arange(rows)[:, None].astype(np.float64)
    time = np.arange(rows)[None, :].astype(np.float64)
    angle = 2 * np.pi * ((freq * time) % size) / size
    cosine = np.cos(angle)
    sine = -np.sin(angle)
    nyquist = np.where(np.arange(rows) % 2 == 0, 1.0, -1.0)
    sine[0] = nyquist
    forward = np.concatenate([cosine, sine], axis=0)
    late = 2 * np.pi * ((freq * (time + rows)) % size) / size
    back_cos = 2 * np.cos(late)
    back_cos[0] = 1.0
    back_sin = -2 * np.sin(late)
    back_sin[0] = np.where((np.arange(rows) + rows) % 2 == 0, 1.0, -1.0)
    backward = np.concatenate([back_cos, back_sin], axis=0).T / size
    return split(forward), split(backward)


def spectrum_kernel(filters_ref, len_ref, fh_ref, fl_ref, out_ref):
    taps = filters_ref.shape[1]
    lag = lax.broadcasted_iota(jnp.int32, filters_ref.shape, 1)
    used = jnp.where(lag < len_ref[...], filters_ref[...].astype(F32), 0.0).astype(BF)
    nt = (((1,), (1,)), ((), ()))
    fh = fh_ref[:, 0:taps]
    fl = fl_ref[:, 0:taps]
    out_ref[...] = lax.dot_general(fh, used, nt, preferred_element_type=F32) + lax.dot_general(
        fl, used, nt, preferred_element_type=F32
    )


def spectrum(filters, filter_len, forward):
    return pl.pallas_call(
        spectrum_kernel,
        out_shape=jax.ShapeDtypeStruct((forward[0].shape[0], filters.shape[0]), F32),
        in_specs=[vm()] * 4,
        out_specs=vm(),
        compiler_params=params(12),
        cost_estimate=cost(4 * forward[0].size * filters.shape[0], 8 * filters.size),
        name="spectrum",
    )(filters, filter_len.reshape(-1, 1), *forward)


def two(a_high, a_low, b):
    return jnp.dot(a_high, b, preferred_element_type=F32) + jnp.dot(
        a_low, b, preferred_element_type=F32
    )


def frequency_signs(rows):
    row_id = lax.broadcasted_iota(jnp.int32, (rows, 1), 0)
    return row_id == 0, jnp.where(row_id % 2 == 0, 1.0, -1.0)


def late_spectrum(own, fh, fl):
    rows = own.shape[0]
    first, sign = frequency_signs(rows)
    plain = two(fh, fl, own)
    return sign * plain[:rows], jnp.where(first, 1.0, sign) * plain[rows:]


def filtered(x_re, x_im, gh, gl, spec):
    rows = x_re.shape[0]
    first, _ = frequency_signs(rows)
    h_re, h_im = spec[:rows], spec[rows:]
    h_cross = jnp.where(first, 0.0, h_im)
    h_own = jnp.where(first, h_im, h_re)
    y = jnp.concatenate([x_re * h_re - x_im * h_cross, x_re * h_cross + x_im * h_own], axis=0)
    y_high = y.astype(BF)
    y_low = (y - y_high.astype(F32)).astype(BF)
    return two(gh, gl, y_high) + jnp.dot(gh, y_low, preferred_element_type=F32)


def conv_low_kernel(res_ref, own_ref, before_ref, spec_ref, skip_ref, fh, fl, gh, gl, out_ref):
    rows = res_ref.shape[0]
    own = own_ref[...]
    late_re, late_im = late_spectrum(own, fh[...], fl[...])
    early = two(fh[...], fl[...], before_ref[...])
    conv = filtered(early[:rows] + late_re, early[rows:] + late_im, gh[...], gl[...], spec_ref[...])
    out_ref[...] = (res_ref[...] + conv + skip_ref[...] * own.astype(F32)).astype(BF)


def conv_own_kernel(
    model_width, res_ref, sq_ref, spec_ref, gain_ref, skip_ref, fh, fl, gh, gl, out_ref
):
    own = normed_rows(res_ref[...], sq_ref[...], gain_ref[...], model_width)
    late_re, late_im = late_spectrum(own, fh[...], fl[...])
    conv = filtered(late_re, late_im, gh[...], gl[...], spec_ref[...])
    out_ref[...] = res_ref[...] + conv + skip_ref[...] * own.astype(F32)


def conv_high_kernel(
    n, model_width, slots_ref, ids_ref, part_ref, raw_ref, raw_sq_ref, low_ref, done_ref,
    spec_ref, gain_ref, fh, fl, gh, gl, out_ref,
):
    rows = part_ref.shape[0]
    last = ids_ref[0] == n - 1
    raw = normed_rows(raw_ref[...].astype(F32), raw_sq_ref[...], gain_ref[...], model_width)
    before = jnp.where(last, low_ref[...].astype(F32), raw.astype(F32)).astype(BF)
    early = two(fh[...], fl[...], before)
    conv = filtered(early[:rows], early[rows:], gh[...], gl[...], spec_ref[...])
    half = half_index(slots_ref, ids_ref, 1)
    out_ref[pl.ds(pl.multiple_of((1 - half) * rows, rows), rows), :] = done_ref[...]
    out_ref[pl.ds(pl.multiple_of(half * rows, rows), rows), :] = (part_ref[...] + conv).astype(BF)


def moved(block, axis, route):
    return lax.ppermute(block, axis, route)


def gather_mp(own, size):
    chips = size // 2
    pieces = [own]
    for k in range(1, chips - 1):
        pieces.append(moved(own, "mp", xor_route(size, 2 * k)))
    inner = [(i, i ^ (size - 2)) for i in range(2, size - 2)]
    direct = moved(own, "mp", inner)
    ends = [(2, 0), (3, 1), (size - 4, size - 2), (size - 3, size - 1)]
    relayed = moved(pieces[chips - 2], "mp", ends)
    pieces.append(direct + relayed)
    parts = []
    for piece in pieces:
        parts.append(piece)
        parts.append(moved(piece, "mp", xor_route(size, 1)))
    return parts


def total_mp(part, size):
    k = 1
    while k < size:
        part = part + moved(part, "mp", xor_route(size, k))
        k *= 2
    return part


def before_rows(block, distance):
    devices = range(lax.axis_size("seq"))
    return moved(block, "seq", [(i - distance, i) for i in devices if i - distance in devices])


def fast_device(
    incoming, queries, key_vecs, value_vecs, w_out, norm_gain, filters, filter_len, skip_gain, slot_map
):
    n = lax.axis_size("seq")
    mp_size = lax.axis_size("mp")
    rows, width = queries.shape[0] // 2, queries.shape[1]
    model_width = w_out.shape[0]
    ids = jnp.stack([lax.axis_index("seq"), lax.axis_index("mp")]).astype(jnp.int32)
    gain = norm_gain.reshape(1, -1)
    skip = skip_gain.reshape(1, -1)
    forward, backward = transform_tables(rows)
    forward = tuple(jnp.asarray(t) for t in forward)
    backward = tuple(jnp.asarray(t) for t in backward)

    def exchange(pieces):
        return [pieces[0]] + [moved(pieces[k], "seq", xor_route(n, k)) for k in range(1, n)]

    inputs = (queries, key_vecs, value_vecs)
    low = exchange(pack(n, 0, slot_map, ids, inputs))
    high = exchange(pack(n, 1, slot_map, ids, inputs))
    spec = spectrum(filters, filter_len, forward)

    att_low = exchange(attend(n, 0, rows, ids, low))
    parts_low = gather_mp(jnp.concatenate(att_low, axis=0), mp_size)
    att_high = exchange(attend(n, 1, rows, ids, low + high))
    parts_high = gather_mp(jnp.concatenate(att_high, axis=0), mp_size)

    every = tuple(range(mp_size))
    res_low, _, sq_low = project(n, 0, slot_map, ids, incoming, w_out, parts_low, every, True)
    norm_low = norm(model_width, res_low, total_mp(sq_low, mp_size), gain)
    before_low = before_rows(norm_low, 1)
    transforms = forward + backward
    done_low = pl.pallas_call(
        conv_low_kernel,
        out_shape=jax.ShapeDtypeStruct((rows, width), BF),
        in_specs=[vm()] * 9,
        out_specs=vm(),
        compiler_params=params(20),
        cost_estimate=cost(14 * rows * rows * width, 12 * rows * width),
        name="conv_low",
    )(res_low, norm_low, before_low, spec, skip, *transforms)

    most = mp_size - 2
    (base_high,) = project(
        n, 1, slot_map, ids, incoming, w_out, parts_high[:most], every[:most], False
    )
    res_high, raw_high, sq_high = project(
        n, 1, slot_map, ids, base_high, w_out, parts_high[most:], every[most:], True
    )
    raw_before = before_rows(raw_high, -1)
    sq_high = total_mp(sq_high, mp_size)
    sq_before = before_rows(sq_high, -1)
    part_high = pl.pallas_call(
        functools.partial(conv_own_kernel, model_width),
        out_shape=jax.ShapeDtypeStruct((rows, width), F32),
        in_specs=[vm()] * 9,
        out_specs=vm(),
        compiler_params=params(20),
        cost_estimate=cost(10 * rows * rows * width, 12 * rows * width),
        name="conv_own",
    )(res_high, sq_high, spec, gain, skip, *transforms)
    return pl.pallas_call(
        functools.partial(conv_high_kernel, n, model_width),
        out_shape=jax.ShapeDtypeStruct((2 * rows, width), BF),
        in_specs=[sm(), sm()] + [vm()] * 11,
        out_specs=vm(),
        compiler_params=params(20),
        cost_estimate=cost(10 * rows * rows * width, 12 * rows * width),
        name="conv_high",
    )(
        slot_map, ids, part_high, raw_before, sq_before, norm_low, done_low, spec, gain, *transforms
    )


def power_of_two(value):
    return value & (value - 1) == 0


def on_device(*arrays):
    n = lax.axis_size("seq")
    size = lax.axis_size("mp")
    queries, filters = arrays[1], arrays[6]
    rows = queries.shape[0] // 2
    heads = queries.shape[1] // HD
    fits = (
        heads % n == 0
        and power_of_two(n)
        and power_of_two(size)
        and size >= 8
        and rows % 256 == 0
        and filters.shape[1] <= rows
    )
    if not fits:
        return general_device(*arrays)
    return fast_device(*arrays)


def solution(mesh):
    placed = (
        P("seq", "mp"),
        P("seq", "mp"),
        P("seq", "mp"),
        P("seq", "mp"),
        P(None, "mp"),
        P("mp"),
        P("mp", None),
        P("mp"),
        P("mp"),
        P(),
    )
    return jax.shard_map(
        on_device, mesh=mesh, in_specs=placed, out_specs=P("seq", "mp"), check_vma=False
    )
```

```python
import functools

import jax
import jax.numpy as jnp
import numpy as np
from jax import lax
from jax.experimental import pallas as pl
from jax.experimental.pallas import tpu as pltpu
from jax.sharding import PartitionSpec as P


HD = 128
EPS = 1e-05
NEG = -1e30
LOG2E = 1.4426950408889634
BF = jnp.bfloat16
F32 = jnp.float32
VMEM = pltpu.VMEM
SMEM = pltpu.SMEM


def shifted(block, axis, distance):
    devices = range(lax.axis_size(axis))
    route = [(i - distance, i) for i in devices if i - distance in devices]
    return lax.ppermute(block, axis, route)


def block_update(running, query_heads, query_pos, key_part, value_part, key_pos):
    peak_now, total_now, accum_now = running
    key_count = key_part.shape[0]
    head_count = query_heads.shape[1]
    key_heads = key_part.reshape(key_count, head_count, HD)
    value_heads = value_part.reshape(key_count, head_count, HD)
    scores = jnp.einsum(
        "thd,shd->ths", query_heads, key_heads, preferred_element_type=F32
    ) * HD ** (-0.5)
    allowed = key_pos[None, None, :] <= query_pos[:, None, None]
    masked = jnp.where(allowed, scores, NEG)
    peak_next = jnp.maximum(peak_now, jnp.max(masked, axis=2))
    weights = jnp.where(allowed, jnp.exp(masked - peak_next[:, :, None]), 0.0)
    factor = jnp.exp(peak_now - peak_next)
    total_next = total_now * factor + jnp.sum(weights, axis=2)
    summed = jnp.einsum(
        "ths,shd->thd", weights.astype(BF), value_heads, preferred_element_type=F32
    )
    return (peak_next, total_next, accum_now * factor[:, :, None] + summed)


def attend_keys(running, query_heads, query_pos, key_part, value_part, key_pos, block_rows):
    block_count = key_part.shape[0] // block_rows

    def attend_advance(state, item):
        return block_update(state, query_heads, query_pos, *item), None

    stacked = (
        key_part.reshape(block_count, block_rows, -1),
        value_part.reshape(block_count, block_rows, -1),
        key_pos.reshape(block_count, block_rows),
    )
    running, _ = lax.scan(attend_advance, running, stacked)
    return running


def causal_window(extended, taps_lag):
    pair_count, twice, width = extended.shape
    length = twice // 2
    tap_count = taps_lag.shape[0]
    inner = int(np.gcd(tap_count, 16))

    def causal_advance(block, accum):
        base = block * inner
        window = lax.dynamic_slice_in_dim(
            extended, length - base - inner + 1, length + inner - 1, 1
        ).astype(F32)
        tap_block = lax.dynamic_slice_in_dim(taps_lag, base, inner, 0).astype(F32)
        for lag in range(inner):
            offset = inner - 1 - lag
            accum = accum + tap_block[lag][None, None, :] * window[:, offset : offset + length]
        return accum

    start = jnp.zeros((pair_count, length, width), F32)
    return lax.fori_loop(0, tap_count // inner, causal_advance, start)


def general_device(
    incoming, queries, key_vecs, value_vecs, w_out, norm_gain, filters, filter_len, skip_gain, slot_map
):
    tok_rows, local_width = queries.shape
    span_rows = tok_rows // 2
    head_count = local_width // HD
    model_width = w_out.shape[0]
    all_rows = slot_map.shape[0] * span_rows
    row_ids = jnp.arange(all_rows, dtype=jnp.int32)
    position = (
        jnp.repeat(slot_map, span_rows, total_repeat_length=all_rows) * span_rows
        + row_ids % span_rows
    )
    seq_rank = lax.axis_index("seq")
    seq_size = lax.axis_size("seq")
    own_pos = lax.dynamic_slice_in_dim(position, seq_rank * tok_rows, tok_rows)
    query_heads = queries.reshape(tok_rows, head_count, HD)
    keys_all = lax.all_gather(key_vecs, "seq", axis=0, tiled=True)
    values_all = lax.all_gather(value_vecs, "seq", axis=0, tiled=True)
    running = attend_keys(
        (
            jnp.full((tok_rows, head_count), NEG, F32),
            jnp.zeros((tok_rows, head_count), F32),
            jnp.zeros((tok_rows, head_count, HD), F32),
        ),
        query_heads,
        own_pos,
        keys_all,
        values_all,
        position,
        2 * tok_rows,
    )
    attention = (running[2] / running[1][:, :, None]).reshape(-1, local_width).astype(BF)
    projected = jnp.dot(
        lax.all_gather(attention, "mp", axis=1, tiled=True), w_out, preferred_element_type=F32
    )
    residual = incoming.astype(F32) + projected
    square_total = lax.psum(jnp.sum(residual * residual, axis=1), "mp")
    scale = lax.rsqrt(square_total / model_width + EPS)
    normed = (residual * scale[:, None] * norm_gain[None, :]).astype(BF)
    tap_count = filters.shape[1]
    taps = jnp.where(
        jnp.arange(tap_count, dtype=jnp.int32)[None, :] < filter_len[:, None],
        filters,
        jnp.zeros((), filters.dtype),
    )
    pair_ids = lax.dynamic_slice_in_dim(slot_map, 2 * seq_rank, 2)
    low_first = pair_ids[0] < pair_ids[1]
    slots = normed.reshape(2, span_rows, local_width)
    low_rows = jnp.where(low_first, slots[0], slots[1])
    high_rows = jnp.where(low_first, slots[1], slots[0])
    own_pair = jnp.stack([low_rows, high_rows])
    low_before = shifted(low_rows, "seq", 1)
    high_before = shifted(high_rows, "seq", -1)
    high_before = jnp.where(seq_rank == seq_size - 1, low_rows, high_before)
    before_pair = jnp.stack([low_before, high_before])
    conv_pair = causal_window(jnp.concatenate([before_pair, own_pair], axis=1), taps.T)
    conv_slots = jnp.where(low_first, conv_pair, conv_pair[::-1])
    conv_rows = conv_slots.reshape(tok_rows, local_width)
    layer_out = residual + conv_rows + skip_gain[None, :] * normed.astype(F32)
    return layer_out.astype(BF)


def params(megabytes=20):
    return pltpu.CompilerParams(vmem_limit_bytes=megabytes << 20)


def cost(flops, moved, exps=0):
    return pl.CostEstimate(flops=int(flops), bytes_accessed=int(moved), transcendentals=int(exps))


def vm():
    return pl.BlockSpec(memory_space=VMEM)


def sm():
    return pl.BlockSpec(memory_space=SMEM)


def xor_route(count, k):
    return [(i, i ^ k) for i in range(count)]


def half_index(slots_ref, ids_ref, high):
    rank = ids_ref[0]
    first_is_high = slots_ref[2 * rank] > slots_ref[2 * rank + 1]
    return jnp.where(first_is_high, 1 - high, high).astype(jnp.int32)


def pack_kernel(n, high, slots_ref, ids_ref, q_ref, k_ref, v_ref, *rest):
    outs, sem = rest[:n], rest[n]
    rank = ids_ref[0]
    rows = outs[0].shape[0] // 3
    wide = outs[0].shape[1]
    half = half_index(slots_ref, ids_ref, high)
    source_rows = pl.ds(pl.multiple_of(half * rows, rows), rows)
    copies = []
    for k in range(n):
        cols = pl.ds(pl.multiple_of((rank ^ k) * wide, wide), wide)
        for a, ref in enumerate((q_ref, k_ref, v_ref)):
            copy = pltpu.make_async_copy(
                ref.at[source_rows, cols],
                outs[k].at[a * rows : (a + 1) * rows, :],
                sem.at[k, a],
            )
            copy.start()
            copies.append(copy)
    for copy in copies:
        copy.wait()


def pack(n, high, slots, ids, arrays):
    rows, width = arrays[0].shape[0] // 2, arrays[0].shape[1]
    piece = jax.ShapeDtypeStruct((3 * rows, width // n), BF)
    return pl.pallas_call(
        functools.partial(pack_kernel, n, high),
        out_shape=[piece] * n,
        in_specs=[sm(), sm()] + [pl.BlockSpec(memory_space=pltpu.HBM)] * 3,
        out_specs=[vm()] * n,
        scratch_shapes=[pltpu.SemaphoreType.DMA((n, 3))],
        compiler_params=params(8),
        cost_estimate=cost(0, 12 * rows * width),
    )(slots, ids, *(pltpu.with_memory_space_constraint(x, pltpu.HBM) for x in arrays))


def attend_kernel(n, high, rows, ids_ref, *refs):
    chunks = 2 if high else 1
    ins = refs[: chunks * n]
    outs = refs[chunks * n : chunks * n + n]
    q_all, k_all, v_all, o_all = refs[chunks * n + n :]
    rank = ids_ref[0]
    wide = outs[0].shape[1]

    def place(block):
        return pl.ds(pl.multiple_of(block * rows, rows), rows)

    for c in range(chunks):
        for k in range(n):
            source = rank ^ k
            block = source if c == 0 else 2 * n - 1 - source
            piece = ins[c * n + k]
            if c == chunks - 1:
                q_all[place(block - c * n), :] = piece[0:rows, :]
            k_all[place(block), :] = piece[rows : 2 * rows, :]
            v_all[place(block), :] = piece[2 * rows : 3 * rows, :]
    base = n if high else 0
    row_id = lax.broadcasted_iota(jnp.int32, (rows, rows), 0)
    col_id = lax.broadcasted_iota(jnp.int32, (rows, rows), 1)
    causal = col_id <= row_id
    factor = HD ** (-0.5) * LOG2E
    nt = (((1,), (1,)), ((), ()))
    for b in range(n):
        past = (base + b) * rows
        for h in range(wide // HD):
            cols = slice(h * HD, (h + 1) * HD)
            q = q_all[b * rows : (b + 1) * rows, cols]
            near = lax.dot_general(
                q, k_all[past : past + rows, cols], nt, preferred_element_type=F32
            )
            near = jnp.where(causal, near, NEG)
            peak = jnp.max(near, axis=1, keepdims=True)
            if past:
                far = lax.dot_general(q, k_all[0:past, cols], nt, preferred_element_type=F32)
                peak = jnp.maximum(peak, jnp.max(far, axis=1, keepdims=True))
            w_near = jnp.exp2((near - peak) * factor)
            total = jnp.sum(w_near, axis=1, keepdims=True)
            summed = jnp.dot(
                w_near.astype(BF), v_all[past : past + rows, cols], preferred_element_type=F32
            )
            if past:
                w_far = jnp.exp2((far - peak) * factor)
                total = total + jnp.sum(w_far, axis=1, keepdims=True)
                summed = summed + jnp.dot(
                    w_far.astype(BF), v_all[0:past, cols], preferred_element_type=F32
                )
            owner = n - 1 - b if high else b
            o_all[owner * rows : (owner + 1) * rows, cols] = (summed / total).astype(BF)
    for k in range(n):
        outs[k][...] = o_all[place(rank ^ k), :]


def attend(n, high, rows, ids, pieces):
    wide = pieces[0].shape[1]
    chunks = 2 if high else 1
    pairs = n * (n + 1) // 2 + (n * n if high else 0)
    area = pairs * rows * rows * (wide // HD)
    return pl.pallas_call(
        functools.partial(attend_kernel, n, high, rows),
        out_shape=[jax.ShapeDtypeStruct((rows, wide), BF)] * n,
        in_specs=[sm()] + [vm()] * len(pieces),
        out_specs=[vm()] * n,
        scratch_shapes=[
            VMEM((n * rows, wide), BF),
            VMEM((chunks * n * rows, wide), BF),
            VMEM((chunks * n * rows, wide), BF),
            VMEM((n * rows, wide), BF),
        ],
        compiler_params=params(32),
        cost_estimate=cost(4 * area * HD, 8 * n * rows * wide * chunks, area),
        name="attend_high" if high else "attend_low",
    )(ids, *pieces)


def project_kernel(n, indices, slots_ref, ids_ref, base_ref, w_ref, *refs):
    count = len(indices)
    chunks, outs, lhs = (refs[:count], refs[count : 2 * count]), refs[2 * count : -1], refs[-1]
    rank = ids_ref[0]
    me = ids_ref[1]
    size, width = lhs.shape
    rows = size // 2
    wide = width // n
    if base_ref.dtype == F32:
        total = base_ref[...]
    else:
        halves = [half_index(slots_ref, ids_ref, high) * rows for high in range(2)]
        total = jnp.concatenate(
            [base_ref[pl.ds(pl.multiple_of(h, rows), rows), :] for h in halves], axis=0
        ).astype(F32)
    for j, index in enumerate(indices):
        for high in range(2):
            for k in range(n):
                cols = pl.ds(pl.multiple_of((rank ^ k) * wide, wide), wide)
                lhs[high * rows : (high + 1) * rows, cols] = chunks[high][j][
                    k * rows : (k + 1) * rows, :
                ]
        depth = pl.ds(pl.multiple_of((me ^ index) * width, width), width)
        total = total + jnp.dot(lhs[...], w_ref[depth, :], preferred_element_type=F32)
    outs[0][...] = total
    if len(outs) == 1:
        return
    for parity in range(2):

        @pl.when(rank % 2 == parity)
        def _():
            outs[1 + parity][...] = total[:rows].astype(BF)
            outs[2 - parity][...] = total[rows:].astype(BF)

    squares = total * total
    lanes = squares[:, 0:HD]
    for g in range(1, squares.shape[1] // HD):
        lanes = lanes + squares[:, g * HD : (g + 1) * HD]
    outs[3][...] = jnp.sum(lanes.T, axis=0, keepdims=True)


def project(n, slots, ids, base, w_out, low, high, indices, final):
    size, width = base.shape
    shapes = [jax.ShapeDtypeStruct((size, width), F32)]
    if final:
        shapes += [jax.ShapeDtypeStruct((size // 2, width), BF)] * 2
        shapes.append(jax.ShapeDtypeStruct((1, size), F32))
    return pl.pallas_call(
        functools.partial(project_kernel, n, indices),
        out_shape=shapes,
        in_specs=[sm(), sm()] + [vm()] * (2 + 2 * len(indices)),
        out_specs=[vm()] * len(shapes),
        scratch_shapes=[VMEM((size, width), BF)],
        compiler_params=params(20),
        cost_estimate=cost(2 * size * width * width * len(indices), 2 * w_out.size * 1.5),
    )(slots, ids, base, w_out, *low, *high)


def normed_rows(res, sq_row, gain, model_width):
    rows, width = res.shape
    scale = lax.rsqrt(sq_row / model_width + EPS)
    column = jnp.broadcast_to(scale, (HD, rows)).T
    parts = [
        (res[:, g * HD : (g + 1) * HD] * column * gain[:, g * HD : (g + 1) * HD]).astype(BF)
        for g in range(width // HD)
    ]
    return jnp.concatenate(parts, axis=1)


def split(array):
    high = array.astype(jnp.bfloat16)
    low = (array - high.astype(np.float64)).astype(jnp.bfloat16)
    return high, low


def transform_tables(rows):
    size = 2 * rows
    freq = np.arange(rows)[:, None].astype(np.float64)
    time = np.arange(rows)[None, :].astype(np.float64)
    angle = 2 * np.pi * ((freq * time) % size) / size
    cosine = np.cos(angle)
    sine = -np.sin(angle)
    nyquist = np.where(np.arange(rows) % 2 == 0, 1.0, -1.0)
    sine[0] = nyquist
    forward = np.concatenate([cosine, sine], axis=0)
    late = 2 * np.pi * ((freq * (time + rows)) % size) / size
    back_cos = 2 * np.cos(late)
    back_cos[0] = 1.0
    back_sin = -2 * np.sin(late)
    back_sin[0] = np.where((np.arange(rows) + rows) % 2 == 0, 1.0, -1.0)
    backward = np.concatenate([back_cos, back_sin], axis=0).T / size
    return split(forward), split(backward)


def spectrum_kernel(filters_ref, len_ref, fh_ref, fl_ref, out_ref):
    taps = filters_ref.shape[1]
    lag = lax.broadcasted_iota(jnp.int32, filters_ref.shape, 1)
    used = jnp.where(lag < len_ref[...], filters_ref[...].astype(F32), 0.0).astype(BF)
    nt = (((1,), (1,)), ((), ()))
    fh = fh_ref[:, 0:taps]
    fl = fl_ref[:, 0:taps]
    out_ref[...] = lax.dot_general(fh, used, nt, preferred_element_type=F32) + lax.dot_general(
        fl, used, nt, preferred_element_type=F32
    )


def spectrum(filters, filter_len, forward):
    return pl.pallas_call(
        spectrum_kernel,
        out_shape=jax.ShapeDtypeStruct((forward[0].shape[0], filters.shape[0]), F32),
        in_specs=[vm()] * 4,
        out_specs=vm(),
        compiler_params=params(12),
        cost_estimate=cost(4 * forward[0].size * filters.shape[0], 8 * filters.size),
        name="spectrum",
    )(filters, filter_len.reshape(-1, 1), *forward)


def two(a_high, a_low, b):
    return jnp.dot(a_high, b, preferred_element_type=F32) + jnp.dot(
        a_low, b, preferred_element_type=F32
    )


def frequency_signs(rows):
    row_id = lax.broadcasted_iota(jnp.int32, (rows, 1), 0)
    return row_id == 0, jnp.where(row_id % 2 == 0, 1.0, -1.0)


def late_spectrum(own, fh, fl):
    rows = own.shape[0]
    first, sign = frequency_signs(rows)
    plain = two(fh, fl, own)
    return sign * plain[:rows], jnp.where(first, 1.0, sign) * plain[rows:]


def filtered_spectrum(x_re, x_im, spec):
    rows = x_re.shape[0]
    first, _ = frequency_signs(rows)
    h_re, h_im = spec[:rows], spec[rows:]
    h_cross = jnp.where(first, 0.0, h_im)
    h_own = jnp.where(first, h_im, h_re)
    return jnp.concatenate([x_re * h_re - x_im * h_cross, x_re * h_cross + x_im * h_own], axis=0)


def filtered(x_re, x_im, gh, gl, spec):
    y = filtered_spectrum(x_re, x_im, spec)
    y_high = y.astype(BF)
    y_low = (y - y_high.astype(F32)).astype(BF)
    return two(gh, gl, y_high) + jnp.dot(gh, y_low, preferred_element_type=F32)


def conv_own_kernel(
    model_width, res_ref, sq_ref, spec_ref, gain_ref, skip_ref, fh, fl, gh, gl, out_ref, low_ref
):
    rows = spec_ref.shape[0] // 2
    for high in range(2):
        part = slice(high * rows, (high + 1) * rows)
        res = res_ref[part, :]
        own = normed_rows(res, sq_ref[:, part], gain_ref[...], model_width)
        if not high:
            low_ref[...] = own
        late_re, late_im = late_spectrum(own, fh[...], fl[...])
        conv = filtered(late_re, late_im, gh[...], gl[...], spec_ref[...])
        out_ref[part, :] = res + conv + skip_ref[...] * own.astype(F32)


def conv_last_kernel(
    n, model_width, slots_ref, ids_ref, part_ref, low_ref, raw_a, raw_b, sq_a, sq_b,
    spec_ref, gain_ref, fh, gh, out_ref,
):
    rows = low_ref.shape[0]
    rank = ids_ref[0]
    odd = rank % 2 == 1
    gain = gain_ref[...]
    for high in range(2):
        from_a = odd != (high == 1)
        raw = jnp.where(from_a, raw_a[...].astype(F32), raw_b[...].astype(F32))
        part = slice(high * rows, (high + 1) * rows)
        squares = jnp.where(from_a, sq_a[:, part], sq_b[:, part])
        before = normed_rows(raw, squares, gain, model_width)
        if high:
            last = rank == n - 1
            before = jnp.where(last, low_ref[...].astype(F32), before.astype(F32)).astype(BF)
        early = jnp.dot(fh[...], before, preferred_element_type=F32)
        y = filtered_spectrum(early[:rows], early[rows:], spec_ref[...]).astype(BF)
        conv = jnp.dot(gh[...], y, preferred_element_type=F32)
        half = half_index(slots_ref, ids_ref, high)
        out_ref[pl.ds(pl.multiple_of(half * rows, rows), rows), :] = (part_ref[part, :] + conv).astype(
            BF
        )


def relayed_piece(own, near, size):
    inner = [(i, i ^ (size - 2)) for i in range(2, size - 2)]
    direct = lax.ppermute(own, "mp", inner)
    ends = [(2, 0), (3, 1), (size - 4, size - 2), (size - 3, size - 1)]
    return direct + lax.ppermute(near, "mp", ends)


def gather_mp(own, size, relay):
    chips = size // 2
    pieces = [own]
    for k in range(1, chips):
        if relay and k == chips - 1:
            pieces.append(relayed_piece(own, pieces[k - 1], size))
        else:
            pieces.append(lax.ppermute(own, "mp", xor_route(size, 2 * k)))
    parts = []
    for piece in pieces:
        parts.append(piece)
        parts.append(lax.ppermute(piece, "mp", xor_route(size, 1)))
    return parts


def total_mp(part, size):
    k = 1
    while k < size:
        part = part + lax.ppermute(part, "mp", xor_route(size, k))
        k *= 2
    return part


def swapped(block, offset):
    n = lax.axis_size("seq")
    route = []
    for i in range(offset, n - 1, 2):
        route += [(i, i + 1), (i + 1, i)]
    return lax.ppermute(block, "seq", route)


def fast_device(
    incoming, queries, key_vecs, value_vecs, w_out, norm_gain, filters, filter_len, skip_gain, slot_map
):
    n = lax.axis_size("seq")
    mp_size = lax.axis_size("mp")
    rows, width = queries.shape[0] // 2, queries.shape[1]
    model_width = w_out.shape[0]
    ids = jnp.stack([lax.axis_index("seq"), lax.axis_index("mp")]).astype(jnp.int32)
    gain = norm_gain.reshape(1, -1)
    skip = skip_gain.reshape(1, -1)
    forward, backward = transform_tables(rows)
    forward = tuple(jnp.asarray(t) for t in forward)
    backward = tuple(jnp.asarray(t) for t in backward)

    def exchange(pieces):
        return [pieces[0]] + [lax.ppermute(pieces[k], "seq", xor_route(n, k)) for k in range(1, n)]

    inputs = (queries, key_vecs, value_vecs)
    low = exchange(pack(n, 0, slot_map, ids, inputs))
    high = exchange(pack(n, 1, slot_map, ids, inputs))
    spec = spectrum(filters, filter_len, forward)

    att_low = exchange(attend(n, 0, rows, ids, low))
    parts_low = gather_mp(jnp.concatenate(att_low, axis=0), mp_size, True)
    att_high = exchange(attend(n, 1, rows, ids, low + high))
    parts_high = gather_mp(jnp.concatenate(att_high, axis=0), mp_size, False)

    most = mp_size // 2
    first, last = tuple(range(most)), tuple(range(most, mp_size))
    (base,) = project(
        n, slot_map, ids, incoming, w_out,
        parts_low[:most], parts_high[:most], first, False,
    )
    res, raw_a, raw_b, squares = project(
        n, slot_map, ids, base, w_out,
        parts_low[most:], parts_high[most:], last, True,
    )
    raw_a = swapped(raw_a, 0)
    raw_b = swapped(raw_b, 1)
    squares = total_mp(squares, mp_size)
    sq_a = swapped(squares, 0)
    sq_b = swapped(squares, 1)
    transforms = forward + backward
    part, norm_low = pl.pallas_call(
        functools.partial(conv_own_kernel, model_width),
        out_shape=[
            jax.ShapeDtypeStruct((2 * rows, width), F32),
            jax.ShapeDtypeStruct((rows, width), BF),
        ],
        in_specs=[vm()] * 9,
        out_specs=[vm()] * 2,
        compiler_params=params(20),
        cost_estimate=cost(20 * rows * rows * width, 24 * rows * width),
        name="conv_own",
    )(res, squares, spec, gain, skip, *transforms)
    return pl.pallas_call(
        functools.partial(conv_last_kernel, n, model_width),
        out_shape=jax.ShapeDtypeStruct((2 * rows, width), BF),
        in_specs=[sm(), sm()] + [vm()] * 10,
        out_specs=vm(),
        compiler_params=params(20),
        cost_estimate=cost(20 * rows * rows * width, 24 * rows * width),
        name="conv_last",
    )(
        slot_map, ids, part, norm_low, raw_a, raw_b, sq_a, sq_b, spec, gain, forward[0], backward[0]
    )


def power_of_two(value):
    return value & (value - 1) == 0


def on_device(*arrays):
    n = lax.axis_size("seq")
    size = lax.axis_size("mp")
    queries, filters = arrays[1], arrays[6]
    rows = queries.shape[0] // 2
    heads = queries.shape[1] // HD
    fits = (
        heads % n == 0
        and power_of_two(n)
        and power_of_two(size)
        and n % 2 == 0
        and size >= 8
        and rows % 256 == 0
        and filters.shape[1] <= rows
    )
    if not fits:
        return general_device(*arrays)
    return fast_device(*arrays)


def solution(mesh):
    placed = (
        P("seq", "mp"),
        P("seq", "mp"),
        P("seq", "mp"),
        P("seq", "mp"),
        P(None, "mp"),
        P("mp"),
        P("mp", None),
        P("mp"),
        P("mp"),
        P(),
    )
    return jax.shard_map(
        on_device, mesh=mesh, in_specs=placed, out_specs=P("seq", "mp"), check_vma=False
    )
```

```python
import functools

import jax
import jax.numpy as jnp
import numpy as np
from jax import lax
from jax.experimental import pallas as pl
from jax.experimental.pallas import tpu as pltpu
from jax.sharding import PartitionSpec as P


HD = 128
EPS = 1e-05
NEG = -1e30
LOG2E = 1.4426950408889634
BF = jnp.bfloat16
F32 = jnp.float32
VMEM = pltpu.VMEM
SMEM = pltpu.SMEM


def shifted(block, axis, distance):
    devices = range(lax.axis_size(axis))
    route = [(i - distance, i) for i in devices if i - distance in devices]
    return lax.ppermute(block, axis, route)


def block_update(running, query_heads, query_pos, key_part, value_part, key_pos):
    peak_now, total_now, accum_now = running
    key_count = key_part.shape[0]
    head_count = query_heads.shape[1]
    key_heads = key_part.reshape(key_count, head_count, HD)
    value_heads = value_part.reshape(key_count, head_count, HD)
    scores = jnp.einsum(
        "thd,shd->ths", query_heads, key_heads, preferred_element_type=F32
    ) * HD ** (-0.5)
    allowed = key_pos[None, None, :] <= query_pos[:, None, None]
    masked = jnp.where(allowed, scores, NEG)
    peak_next = jnp.maximum(peak_now, jnp.max(masked, axis=2))
    weights = jnp.where(allowed, jnp.exp(masked - peak_next[:, :, None]), 0.0)
    factor = jnp.exp(peak_now - peak_next)
    total_next = total_now * factor + jnp.sum(weights, axis=2)
    summed = jnp.einsum(
        "ths,shd->thd", weights.astype(BF), value_heads, preferred_element_type=F32
    )
    return (peak_next, total_next, accum_now * factor[:, :, None] + summed)


def attend_keys(running, query_heads, query_pos, key_part, value_part, key_pos, block_rows):
    block_count = key_part.shape[0] // block_rows

    def attend_advance(state, item):
        return block_update(state, query_heads, query_pos, *item), None

    stacked = (
        key_part.reshape(block_count, block_rows, -1),
        value_part.reshape(block_count, block_rows, -1),
        key_pos.reshape(block_count, block_rows),
    )
    running, _ = lax.scan(attend_advance, running, stacked)
    return running


def causal_window(extended, taps_lag):
    pair_count, twice, width = extended.shape
    length = twice // 2
    tap_count = taps_lag.shape[0]
    inner = int(np.gcd(tap_count, 16))

    def causal_advance(block, accum):
        base = block * inner
        window = lax.dynamic_slice_in_dim(
            extended, length - base - inner + 1, length + inner - 1, 1
        ).astype(F32)
        tap_block = lax.dynamic_slice_in_dim(taps_lag, base, inner, 0).astype(F32)
        for lag in range(inner):
            offset = inner - 1 - lag
            accum = accum + tap_block[lag][None, None, :] * window[:, offset : offset + length]
        return accum

    start = jnp.zeros((pair_count, length, width), F32)
    return lax.fori_loop(0, tap_count // inner, causal_advance, start)


def general_device(
    incoming, queries, key_vecs, value_vecs, w_out, norm_gain, filters, filter_len, skip_gain, slot_map
):
    tok_rows, local_width = queries.shape
    span_rows = tok_rows // 2
    head_count = local_width // HD
    model_width = w_out.shape[0]
    all_rows = slot_map.shape[0] * span_rows
    row_ids = jnp.arange(all_rows, dtype=jnp.int32)
    position = (
        jnp.repeat(slot_map, span_rows, total_repeat_length=all_rows) * span_rows
        + row_ids % span_rows
    )
    seq_rank = lax.axis_index("seq")
    seq_size = lax.axis_size("seq")
    own_pos = lax.dynamic_slice_in_dim(position, seq_rank * tok_rows, tok_rows)
    query_heads = queries.reshape(tok_rows, head_count, HD)
    keys_all = lax.all_gather(key_vecs, "seq", axis=0, tiled=True)
    values_all = lax.all_gather(value_vecs, "seq", axis=0, tiled=True)
    running = attend_keys(
        (
            jnp.full((tok_rows, head_count), NEG, F32),
            jnp.zeros((tok_rows, head_count), F32),
            jnp.zeros((tok_rows, head_count, HD), F32),
        ),
        query_heads,
        own_pos,
        keys_all,
        values_all,
        position,
        2 * tok_rows,
    )
    attention = (running[2] / running[1][:, :, None]).reshape(-1, local_width).astype(BF)
    projected = jnp.dot(
        lax.all_gather(attention, "mp", axis=1, tiled=True), w_out, preferred_element_type=F32
    )
    residual = incoming.astype(F32) + projected
    square_total = lax.psum(jnp.sum(residual * residual, axis=1), "mp")
    scale = lax.rsqrt(square_total / model_width + EPS)
    normed = (residual * scale[:, None] * norm_gain[None, :]).astype(BF)
    tap_count = filters.shape[1]
    taps = jnp.where(
        jnp.arange(tap_count, dtype=jnp.int32)[None, :] < filter_len[:, None],
        filters,
        jnp.zeros((), filters.dtype),
    )
    pair_ids = lax.dynamic_slice_in_dim(slot_map, 2 * seq_rank, 2)
    low_first = pair_ids[0] < pair_ids[1]
    slots = normed.reshape(2, span_rows, local_width)
    low_rows = jnp.where(low_first, slots[0], slots[1])
    high_rows = jnp.where(low_first, slots[1], slots[0])
    own_pair = jnp.stack([low_rows, high_rows])
    low_before = shifted(low_rows, "seq", 1)
    high_before = shifted(high_rows, "seq", -1)
    high_before = jnp.where(seq_rank == seq_size - 1, low_rows, high_before)
    before_pair = jnp.stack([low_before, high_before])
    conv_pair = causal_window(jnp.concatenate([before_pair, own_pair], axis=1), taps.T)
    conv_slots = jnp.where(low_first, conv_pair, conv_pair[::-1])
    conv_rows = conv_slots.reshape(tok_rows, local_width)
    layer_out = residual + conv_rows + skip_gain[None, :] * normed.astype(F32)
    return layer_out.astype(BF)


def params(megabytes=20):
    return pltpu.CompilerParams(vmem_limit_bytes=megabytes << 20)


def cost(flops, moved, exps=0):
    return pl.CostEstimate(flops=int(flops), bytes_accessed=int(moved), transcendentals=int(exps))


def vm():
    return pl.BlockSpec(memory_space=VMEM)


def sm():
    return pl.BlockSpec(memory_space=SMEM)


def xor_route(count, k):
    return [(i, i ^ k) for i in range(count)]


def half_index(slots_ref, ids_ref, high):
    rank = ids_ref[0]
    first_is_high = slots_ref[2 * rank] > slots_ref[2 * rank + 1]
    return jnp.where(first_is_high, 1 - high, high).astype(jnp.int32)


def pack_kernel(n, high, slots_ref, ids_ref, q_ref, k_ref, v_ref, *rest):
    outs, sem = rest[:n], rest[n]
    rank = ids_ref[0]
    rows = outs[0].shape[0] // 3
    wide = outs[0].shape[1]
    half = half_index(slots_ref, ids_ref, high)
    source_rows = pl.ds(pl.multiple_of(half * rows, rows), rows)
    copies = []
    for k in range(n):
        cols = pl.ds(pl.multiple_of((rank ^ k) * wide, wide), wide)
        for a, ref in enumerate((q_ref, k_ref, v_ref)):
            copy = pltpu.make_async_copy(
                ref.at[source_rows, cols],
                outs[k].at[a * rows : (a + 1) * rows, :],
                sem.at[k, a],
            )
            copy.start()
            copies.append(copy)
    for copy in copies:
        copy.wait()


def in_hbm(array):
    return pltpu.with_memory_space_constraint(array, pltpu.HBM)


def pack(n, high, slots, ids, arrays):
    rows, width = arrays[0].shape[0] // 2, arrays[0].shape[1]
    piece = jax.ShapeDtypeStruct((3 * rows, width // n), BF)
    return pl.pallas_call(
        functools.partial(pack_kernel, n, high),
        out_shape=[piece] * n,
        in_specs=[sm(), sm()] + [pl.BlockSpec(memory_space=pltpu.HBM)] * 3,
        out_specs=[vm()] * n,
        scratch_shapes=[pltpu.SemaphoreType.DMA((n, 3))],
        compiler_params=params(8),
        cost_estimate=cost(0, 12 * rows * width),
    )(in_hbm(slots), ids, *(in_hbm(x) for x in arrays))


def attend_kernel(n, high, rows, ids_ref, *refs):
    chunks = 2 if high else 1
    ins = refs[: chunks * n]
    outs = refs[chunks * n : chunks * n + n]
    q_all, k_all, v_all, o_all = refs[chunks * n + n :]
    rank = ids_ref[0]
    wide = outs[0].shape[1]

    def place(block):
        return pl.ds(pl.multiple_of(block * rows, rows), rows)

    for c in range(chunks):
        for k in range(n):
            source = rank ^ k
            block = source if c == 0 else 2 * n - 1 - source
            piece = ins[c * n + k]
            if c == chunks - 1:
                q_all[place(block - c * n), :] = piece[0:rows, :]
            k_all[place(block), :] = piece[rows : 2 * rows, :]
            v_all[place(block), :] = piece[2 * rows : 3 * rows, :]
    base = n if high else 0
    row_id = lax.broadcasted_iota(jnp.int32, (rows, rows), 0)
    col_id = lax.broadcasted_iota(jnp.int32, (rows, rows), 1)
    causal = col_id <= row_id
    factor = HD ** (-0.5) * LOG2E
    nt = (((1,), (1,)), ((), ()))
    for b in range(n):
        past = (base + b) * rows
        for h in range(wide // HD):
            cols = slice(h * HD, (h + 1) * HD)
            q = q_all[b * rows : (b + 1) * rows, cols]
            near = lax.dot_general(
                q, k_all[past : past + rows, cols], nt, preferred_element_type=F32
            )
            near = jnp.where(causal, near, NEG)
            peak = jnp.max(near, axis=1, keepdims=True)
            if past:
                far = lax.dot_general(q, k_all[0:past, cols], nt, preferred_element_type=F32)
                peak = jnp.maximum(peak, jnp.max(far, axis=1, keepdims=True))
            w_near = jnp.exp2((near - peak) * factor)
            total = jnp.sum(w_near, axis=1, keepdims=True)
            summed = jnp.dot(
                w_near.astype(BF), v_all[past : past + rows, cols], preferred_element_type=F32
            )
            if past:
                w_far = jnp.exp2((far - peak) * factor)
                total = total + jnp.sum(w_far, axis=1, keepdims=True)
                summed = summed + jnp.dot(
                    w_far.astype(BF), v_all[0:past, cols], preferred_element_type=F32
                )
            owner = n - 1 - b if high else b
            o_all[owner * rows : (owner + 1) * rows, cols] = (summed / total).astype(BF)
    for k in range(n):
        outs[k][...] = o_all[place(rank ^ k), :]


def attend(n, high, rows, ids, pieces):
    wide = pieces[0].shape[1]
    chunks = 2 if high else 1
    pairs = n * (n + 1) // 2 + (n * n if high else 0)
    area = pairs * rows * rows * (wide // HD)
    return pl.pallas_call(
        functools.partial(attend_kernel, n, high, rows),
        out_shape=[jax.ShapeDtypeStruct((rows, wide), BF)] * n,
        in_specs=[sm()] + [vm()] * len(pieces),
        out_specs=[vm()] * n,
        scratch_shapes=[
            VMEM((n * rows, wide), BF),
            VMEM((chunks * n * rows, wide), BF),
            VMEM((chunks * n * rows, wide), BF),
            VMEM((n * rows, wide), BF),
        ],
        compiler_params=params(32),
        cost_estimate=cost(4 * area * HD, 8 * n * rows * wide * chunks, area),
        name="attend_high" if high else "attend_low",
    )(ids, *pieces)


def project_kernel(n, high, indices, has_low, slots_ref, ids_ref, base_ref, w_ref, *refs):
    count = len(indices)
    parts, outs, lhs = refs[:count], refs[count + has_low : -1], refs[-1]
    rank = ids_ref[0]
    me = ids_ref[1]
    rows, width = lhs.shape
    wide = width // n
    if base_ref.dtype == F32:
        total = base_ref[...]
    else:
        half = half_index(slots_ref, ids_ref, high)
        total = base_ref[pl.ds(pl.multiple_of(half * rows, rows), rows), :].astype(F32)
    for index, part in zip(indices, parts):
        for k in range(n):
            cols = pl.ds(pl.multiple_of((rank ^ k) * wide, wide), wide)
            lhs[:, cols] = part[k * rows : (k + 1) * rows, :]
        depth = pl.ds(pl.multiple_of((me ^ index) * width, width), width)
        total = total + jnp.dot(lhs[...], w_ref[depth, :], preferred_element_type=F32)
    outs[0][...] = total
    if len(outs) == 1:
        return
    outs[1][...] = total.astype(BF)
    squares = total * total
    lanes = squares[:, 0:HD]
    for g in range(1, squares.shape[1] // HD):
        lanes = lanes + squares[:, g * HD : (g + 1) * HD]
    if has_low:
        outs[2][:, 0:rows] = refs[count][...]
        outs[2][:, rows : 2 * rows] = jnp.sum(lanes.T, axis=0, keepdims=True)
    else:
        outs[2][...] = jnp.sum(lanes.T, axis=0, keepdims=True)


def project(n, high, slots, ids, base, w_out, parts, indices, final, low_squares=()):
    rows, width = parts[0].shape[0] // n, w_out.shape[1]
    shapes = [jax.ShapeDtypeStruct((rows, width), F32)]
    extra = list(low_squares)
    if final:
        shapes.append(jax.ShapeDtypeStruct((rows, width), BF))
        shapes.append(jax.ShapeDtypeStruct((1, rows * (1 + len(extra))), F32))
    return pl.pallas_call(
        functools.partial(project_kernel, n, high, indices, len(extra)),
        out_shape=shapes,
        in_specs=[sm(), sm()] + [vm()] * (2 + len(parts) + len(extra)),
        out_specs=[vm()] * len(shapes),
        scratch_shapes=[VMEM((rows, width), BF)],
        compiler_params=params(20),
        cost_estimate=cost(2 * rows * width * width * len(parts), 2 * w_out.size * 1.5),
    )(slots, ids, base, w_out, *parts, *extra)


def normed_rows(res, sq_row, gain, model_width):
    rows, width = res.shape
    scale = lax.rsqrt(sq_row / model_width + EPS)
    column = jnp.broadcast_to(scale, (HD, rows)).T
    parts = [
        (res[:, g * HD : (g + 1) * HD] * column * gain[:, g * HD : (g + 1) * HD]).astype(BF)
        for g in range(width // HD)
    ]
    return jnp.concatenate(parts, axis=1)


def split(array):
    high = array.astype(jnp.bfloat16)
    low = (array - high.astype(np.float64)).astype(jnp.bfloat16)
    return high, low


def transform_tables(rows):
    size = 2 * rows
    freq = np.arange(rows)[:, None].astype(np.float64)
    time = np.arange(rows)[None, :].astype(np.float64)
    angle = 2 * np.pi * ((freq * time) % size) / size
    cosine = np.cos(angle)
    sine = -np.sin(angle)
    nyquist = np.where(np.arange(rows) % 2 == 0, 1.0, -1.0)
    sine[0] = nyquist
    forward = np.concatenate([cosine, sine], axis=0)
    late = 2 * np.pi * ((freq * (time + rows)) % size) / size
    back_cos = 2 * np.cos(late)
    back_cos[0] = 1.0
    back_sin = -2 * np.sin(late)
    back_sin[0] = np.where((np.arange(rows) + rows) % 2 == 0, 1.0, -1.0)
    backward = np.concatenate([back_cos, back_sin], axis=0).T / size
    return split(forward), split(backward)


def spectrum_kernel(filters_ref, len_ref, fh_ref, fl_ref, out_ref):
    taps = filters_ref.shape[1]
    lag = lax.broadcasted_iota(jnp.int32, filters_ref.shape, 1)
    used = jnp.where(lag < len_ref[...], filters_ref[...].astype(F32), 0.0).astype(BF)
    nt = (((1,), (1,)), ((), ()))
    fh = fh_ref[:, 0:taps]
    fl = fl_ref[:, 0:taps]
    out_ref[...] = lax.dot_general(fh, used, nt, preferred_element_type=F32) + lax.dot_general(
        fl, used, nt, preferred_element_type=F32
    )


def spectrum(filters, filter_len, forward):
    return pl.pallas_call(
        spectrum_kernel,
        out_shape=jax.ShapeDtypeStruct((forward[0].shape[0], filters.shape[0]), F32),
        in_specs=[vm()] * 4,
        out_specs=vm(),
        compiler_params=params(12),
        cost_estimate=cost(4 * forward[0].size * filters.shape[0], 8 * filters.size),
        name="spectrum",
    )(filters, filter_len.reshape(-1, 1), *forward)


def two(a_high, a_low, b):
    return jnp.dot(a_high, b, preferred_element_type=F32) + jnp.dot(
        a_low, b, preferred_element_type=F32
    )


def frequency_signs(rows):
    row_id = lax.broadcasted_iota(jnp.int32, (rows, 1), 0)
    return row_id == 0, jnp.where(row_id % 2 == 0, 1.0, -1.0)


def late_spectrum(own, fh, fl):
    rows = own.shape[0]
    first, sign = frequency_signs(rows)
    plain = two(fh, fl, own)
    return sign * plain[:rows], jnp.where(first, 1.0, sign) * plain[rows:]


def filtered_spectrum(x_re, x_im, spec):
    rows = x_re.shape[0]
    first, _ = frequency_signs(rows)
    h_re, h_im = spec[:rows], spec[rows:]
    h_cross = jnp.where(first, 0.0, h_im)
    h_own = jnp.where(first, h_im, h_re)
    return jnp.concatenate([x_re * h_re - x_im * h_cross, x_re * h_cross + x_im * h_own], axis=0)


def filtered(x_re, x_im, gh, gl, spec):
    y = filtered_spectrum(x_re, x_im, spec)
    y_high = y.astype(BF)
    y_low = (y - y_high.astype(F32)).astype(BF)
    return two(gh, gl, y_high) + jnp.dot(gh, y_low, preferred_element_type=F32)


def conv_own_kernel(
    model_width, res_low, res_high, sq_ref, spec_ref, gain_ref, skip_ref, fh, fl, gh, gl,
    out_ref, low_ref,
):
    rows = spec_ref.shape[0] // 2
    for high, res_ref in enumerate((res_low, res_high)):
        part = slice(high * rows, (high + 1) * rows)
        res = res_ref[...]
        own = normed_rows(res, sq_ref[:, part], gain_ref[...], model_width)
        if not high:
            low_ref[...] = own
        late_re, late_im = late_spectrum(own, fh[...], fl[...])
        conv = filtered(late_re, late_im, gh[...], gl[...], spec_ref[...])
        out_ref[part, :] = res + conv + skip_ref[...] * own.astype(F32)


def conv_last_kernel(
    n, model_width, slots_ref, ids_ref, part_ref, low_ref, raw_low, raw_high, sq_a, sq_b,
    spec_ref, gain_ref, fh, gh, out_ref,
):
    rows = low_ref.shape[0]
    rank = ids_ref[0]
    odd = rank % 2 == 1
    for high, raw_ref in enumerate((raw_low, raw_high)):
        part = slice(high * rows, (high + 1) * rows)
        squares = jnp.where(odd != (high == 1), sq_a[:, part], sq_b[:, part])
        before = normed_rows(raw_ref[...].astype(F32), squares, gain_ref[...], model_width)
        before = before.astype(F32)
        if high:
            before = jnp.where(rank == n - 1, low_ref[...].astype(F32), before).astype(BF)
        else:
            before = jnp.where(rank == 0, 0.0, before).astype(BF)
        early = jnp.dot(fh[...], before, preferred_element_type=F32)
        y = filtered_spectrum(early[:rows], early[rows:], spec_ref[...]).astype(BF)
        conv = jnp.dot(gh[...], y, preferred_element_type=F32)
        half = half_index(slots_ref, ids_ref, high)
        out_ref[pl.ds(pl.multiple_of(half * rows, rows), rows), :] = (part_ref[part, :] + conv).astype(
            BF
        )


def relayed_piece(own, near, size):
    inner = [(i, i ^ (size - 2)) for i in range(2, size - 2)]
    direct = lax.ppermute(own, "mp", inner)
    ends = [(2, 0), (3, 1), (size - 4, size - 2), (size - 3, size - 1)]
    return direct + lax.ppermute(near, "mp", ends)


def gather_mp(own, size, relay):
    chips = size // 2
    pieces = [own]
    for k in range(1, chips):
        if relay and k == chips - 1:
            pieces.append(relayed_piece(own, pieces[k - 1], size))
        else:
            pieces.append(lax.ppermute(own, "mp", xor_route(size, 2 * k)))
    parts = []
    for piece in pieces:
        parts.append(piece)
        parts.append(lax.ppermute(piece, "mp", xor_route(size, 1)))
    return parts


def total_mp(part, size):
    k = 1
    while k < size:
        part = part + lax.ppermute(part, "mp", xor_route(size, k))
        k *= 2
    return part


def ring(n, step):
    return [(i, (i + step) % n) for i in range(n)]


def pairs(n, offset):
    route = []
    for i in range(offset, n, 2):
        route += [(i, (i + 1) % n), ((i + 1) % n, i)]
    return route


def fast_device(
    incoming, queries, key_vecs, value_vecs, w_out, norm_gain, filters, filter_len, skip_gain, slot_map
):
    n = lax.axis_size("seq")
    mp_size = lax.axis_size("mp")
    rows, width = queries.shape[0] // 2, queries.shape[1]
    model_width = w_out.shape[0]
    ids = jnp.stack([lax.axis_index("seq"), lax.axis_index("mp")]).astype(jnp.int32)
    gain = norm_gain.reshape(1, -1)
    skip = skip_gain.reshape(1, -1)
    forward, backward = transform_tables(rows)
    forward = tuple(jnp.asarray(t) for t in forward)
    backward = tuple(jnp.asarray(t) for t in backward)

    def exchange(pieces):
        return [pieces[0]] + [lax.ppermute(pieces[k], "seq", xor_route(n, k)) for k in range(1, n)]

    inputs = (queries, key_vecs, value_vecs)
    low = exchange(pack(n, 0, slot_map, ids, inputs))
    high = exchange(pack(n, 1, slot_map, ids, inputs))
    spec = spectrum(filters, filter_len, forward)

    att_low = exchange(attend(n, 0, rows, ids, low))
    parts_low = gather_mp(jnp.concatenate(att_low, axis=0), mp_size, True)
    att_high = exchange(attend(n, 1, rows, ids, low + high))
    parts_high = gather_mp(jnp.concatenate(att_high, axis=0), mp_size, False)

    most = mp_size // 2
    every = tuple(range(mp_size))
    res_low, raw_low, sq_low = project(n, 0, slot_map, ids, incoming, w_out, parts_low, every, True)
    raw_low = lax.ppermute(raw_low, "seq", ring(n, 1))
    (base,) = project(
        n, 1, slot_map, ids, incoming, w_out,
        parts_high[:most], every[:most], False,
    )
    res_high, raw_high, squares = project(
        n, 1, slot_map, ids, base, w_out,
        parts_high[most:], every[most:], True, (sq_low,),
    )
    raw_high = lax.ppermute(raw_high, "seq", ring(n, -1))
    squares = total_mp(squares, mp_size)
    sq_a = lax.ppermute(squares, "seq", pairs(n, 0))
    sq_b = lax.ppermute(squares, "seq", pairs(n, 1))
    transforms = forward + backward
    part, norm_low = pl.pallas_call(
        functools.partial(conv_own_kernel, model_width),
        out_shape=[
            jax.ShapeDtypeStruct((2 * rows, width), F32),
            jax.ShapeDtypeStruct((rows, width), BF),
        ],
        in_specs=[vm()] * 10,
        out_specs=[vm()] * 2,
        compiler_params=params(20),
        cost_estimate=cost(20 * rows * rows * width, 24 * rows * width),
        name="conv_own",
    )(res_low, res_high, squares, spec, gain, skip, *transforms)
    return pl.pallas_call(
        functools.partial(conv_last_kernel, n, model_width),
        out_shape=jax.ShapeDtypeStruct((2 * rows, width), BF),
        in_specs=[sm(), sm()] + [vm()] * 10,
        out_specs=vm(),
        compiler_params=params(20),
        cost_estimate=cost(20 * rows * rows * width, 24 * rows * width),
        name="conv_last",
    )(
        slot_map, ids, part, norm_low, raw_low, raw_high, sq_a, sq_b, spec, gain, forward[0], backward[0]
    )


def power_of_two(value):
    return value & (value - 1) == 0


def on_device(*arrays):
    n = lax.axis_size("seq")
    size = lax.axis_size("mp")
    queries, filters = arrays[1], arrays[6]
    rows = queries.shape[0] // 2
    heads = queries.shape[1] // HD
    fits = (
        heads % n == 0
        and power_of_two(n)
        and power_of_two(size)
        and n % 2 == 0
        and size >= 8
        and rows % 256 == 0
        and filters.shape[1] <= rows
    )
    if not fits:
        return general_device(*arrays)
    return fast_device(*arrays)


def solution(mesh):
    placed = (
        P("seq", "mp"),
        P("seq", "mp"),
        P("seq", "mp"),
        P("seq", "mp"),
        P(None, "mp"),
        P("mp"),
        P("mp", None),
        P("mp"),
        P("mp"),
        P(),
    )
    return jax.shard_map(
        on_device, mesh=mesh, in_specs=placed, out_specs=P("seq", "mp"), check_vma=False
    )
```

```python
import functools

import jax
import jax.numpy as jnp
import numpy as np
from jax import lax
from jax.experimental import pallas as pl
from jax.experimental.pallas import tpu as pltpu
from jax.sharding import PartitionSpec as P


HD = 128
EPS = 1e-05
NEG = -1e30
LOG2E = 1.4426950408889634
BF = jnp.bfloat16
F32 = jnp.float32
VMEM = pltpu.VMEM
SMEM = pltpu.SMEM


def shifted(block, axis, distance):
    devices = range(lax.axis_size(axis))
    route = [(i - distance, i) for i in devices if i - distance in devices]
    return lax.ppermute(block, axis, route)


def block_update(running, query_heads, query_pos, key_part, value_part, key_pos):
    peak_now, total_now, accum_now = running
    key_count = key_part.shape[0]
    head_count = query_heads.shape[1]
    key_heads = key_part.reshape(key_count, head_count, HD)
    value_heads = value_part.reshape(key_count, head_count, HD)
    scores = jnp.einsum(
        "thd,shd->ths", query_heads, key_heads, preferred_element_type=F32
    ) * HD ** (-0.5)
    allowed = key_pos[None, None, :] <= query_pos[:, None, None]
    masked = jnp.where(allowed, scores, NEG)
    peak_next = jnp.maximum(peak_now, jnp.max(masked, axis=2))
    weights = jnp.where(allowed, jnp.exp(masked - peak_next[:, :, None]), 0.0)
    factor = jnp.exp(peak_now - peak_next)
    total_next = total_now * factor + jnp.sum(weights, axis=2)
    summed = jnp.einsum(
        "ths,shd->thd", weights.astype(BF), value_heads, preferred_element_type=F32
    )
    return (peak_next, total_next, accum_now * factor[:, :, None] + summed)


def attend_keys(running, query_heads, query_pos, key_part, value_part, key_pos, block_rows):
    block_count = key_part.shape[0] // block_rows

    def attend_advance(state, item):
        return block_update(state, query_heads, query_pos, *item), None

    stacked = (
        key_part.reshape(block_count, block_rows, -1),
        value_part.reshape(block_count, block_rows, -1),
        key_pos.reshape(block_count, block_rows),
    )
    running, _ = lax.scan(attend_advance, running, stacked)
    return running


def causal_window(extended, taps_lag):
    pair_count, twice, width = extended.shape
    length = twice // 2
    tap_count = taps_lag.shape[0]
    inner = int(np.gcd(tap_count, 16))

    def causal_advance(block, accum):
        base = block * inner
        window = lax.dynamic_slice_in_dim(
            extended, length - base - inner + 1, length + inner - 1, 1
        ).astype(F32)
        tap_block = lax.dynamic_slice_in_dim(taps_lag, base, inner, 0).astype(F32)
        for lag in range(inner):
            offset = inner - 1 - lag
            accum = accum + tap_block[lag][None, None, :] * window[:, offset : offset + length]
        return accum

    start = jnp.zeros((pair_count, length, width), F32)
    return lax.fori_loop(0, tap_count // inner, causal_advance, start)


def general_device(
    incoming, queries, key_vecs, value_vecs, w_out, norm_gain, filters, filter_len, skip_gain, slot_map
):
    tok_rows, local_width = queries.shape
    span_rows = tok_rows // 2
    head_count = local_width // HD
    model_width = w_out.shape[0]
    all_rows = slot_map.shape[0] * span_rows
    row_ids = jnp.arange(all_rows, dtype=jnp.int32)
    position = (
        jnp.repeat(slot_map, span_rows, total_repeat_length=all_rows) * span_rows
        + row_ids % span_rows
    )
    seq_rank = lax.axis_index("seq")
    seq_size = lax.axis_size("seq")
    own_pos = lax.dynamic_slice_in_dim(position, seq_rank * tok_rows, tok_rows)
    query_heads = queries.reshape(tok_rows, head_count, HD)
    keys_all = lax.all_gather(key_vecs, "seq", axis=0, tiled=True)
    values_all = lax.all_gather(value_vecs, "seq", axis=0, tiled=True)
    running = attend_keys(
        (
            jnp.full((tok_rows, head_count), NEG, F32),
            jnp.zeros((tok_rows, head_count), F32),
            jnp.zeros((tok_rows, head_count, HD), F32),
        ),
        query_heads,
        own_pos,
        keys_all,
        values_all,
        position,
        2 * tok_rows,
    )
    attention = (running[2] / running[1][:, :, None]).reshape(-1, local_width).astype(BF)
    projected = jnp.dot(
        lax.all_gather(attention, "mp", axis=1, tiled=True), w_out, preferred_element_type=F32
    )
    residual = incoming.astype(F32) + projected
    square_total = lax.psum(jnp.sum(residual * residual, axis=1), "mp")
    scale = lax.rsqrt(square_total / model_width + EPS)
    normed = (residual * scale[:, None] * norm_gain[None, :]).astype(BF)
    tap_count = filters.shape[1]
    taps = jnp.where(
        jnp.arange(tap_count, dtype=jnp.int32)[None, :] < filter_len[:, None],
        filters,
        jnp.zeros((), filters.dtype),
    )
    pair_ids = lax.dynamic_slice_in_dim(slot_map, 2 * seq_rank, 2)
    low_first = pair_ids[0] < pair_ids[1]
    slots = normed.reshape(2, span_rows, local_width)
    low_rows = jnp.where(low_first, slots[0], slots[1])
    high_rows = jnp.where(low_first, slots[1], slots[0])
    own_pair = jnp.stack([low_rows, high_rows])
    low_before = shifted(low_rows, "seq", 1)
    high_before = shifted(high_rows, "seq", -1)
    high_before = jnp.where(seq_rank == seq_size - 1, low_rows, high_before)
    before_pair = jnp.stack([low_before, high_before])
    conv_pair = causal_window(jnp.concatenate([before_pair, own_pair], axis=1), taps.T)
    conv_slots = jnp.where(low_first, conv_pair, conv_pair[::-1])
    conv_rows = conv_slots.reshape(tok_rows, local_width)
    layer_out = residual + conv_rows + skip_gain[None, :] * normed.astype(F32)
    return layer_out.astype(BF)


def params(megabytes=20):
    return pltpu.CompilerParams(vmem_limit_bytes=megabytes << 20)


def cost(flops, moved, exps=0):
    return pl.CostEstimate(flops=int(flops), bytes_accessed=int(moved), transcendentals=int(exps))


def vm():
    return pl.BlockSpec(memory_space=VMEM)


def sm():
    return pl.BlockSpec(memory_space=SMEM)


def xor_route(count, k):
    return [(i, i ^ k) for i in range(count)]


def half_index(slots_ref, ids_ref, high):
    rank = ids_ref[0]
    first_is_high = slots_ref[2 * rank] > slots_ref[2 * rank + 1]
    return jnp.where(first_is_high, 1 - high, high).astype(jnp.int32)


def pack_kernel(n, high, slots_ref, ids_ref, q_ref, k_ref, v_ref, *rest):
    outs, sem = rest[:n], rest[n]
    rank = ids_ref[0]
    rows = outs[0].shape[0] // 3
    wide = outs[0].shape[1]
    half = half_index(slots_ref, ids_ref, high)
    source_rows = pl.ds(pl.multiple_of(half * rows, rows), rows)
    copies = []
    for k in range(n):
        cols = pl.ds(pl.multiple_of((rank ^ k) * wide, wide), wide)
        for a, ref in enumerate((q_ref, k_ref, v_ref)):
            copy = pltpu.make_async_copy(
                ref.at[source_rows, cols],
                outs[k].at[a * rows : (a + 1) * rows, :],
                sem.at[k, a],
            )
            copy.start()
            copies.append(copy)
    for copy in copies:
        copy.wait()


def in_hbm(array):
    return pltpu.with_memory_space_constraint(array, pltpu.HBM)


def pack(n, high, slots, ids, arrays):
    rows, width = arrays[0].shape[0] // 2, arrays[0].shape[1]
    piece = jax.ShapeDtypeStruct((3 * rows, width // n), BF)
    return pl.pallas_call(
        functools.partial(pack_kernel, n, high),
        out_shape=[piece] * n,
        in_specs=[sm(), sm()] + [pl.BlockSpec(memory_space=pltpu.HBM)] * 3,
        out_specs=[vm()] * n,
        scratch_shapes=[pltpu.SemaphoreType.DMA((n, 3))],
        compiler_params=params(8),
        cost_estimate=cost(0, 12 * rows * width),
    )(in_hbm(slots), ids, *(in_hbm(x) for x in arrays))


def attend_kernel(n, high, rows, ids_ref, *refs):
    chunks = 2 if high else 1
    ins = refs[: chunks * n]
    outs = refs[chunks * n : chunks * n + n]
    q_all, k_all, v_all, o_all = refs[chunks * n + n :]
    rank = ids_ref[0]
    wide = outs[0].shape[1]

    def place(block):
        return pl.ds(pl.multiple_of(block * rows, rows), rows)

    for c in range(chunks):
        for k in range(n):
            source = rank ^ k
            block = source if c == 0 else 2 * n - 1 - source
            piece = ins[c * n + k]
            if c == chunks - 1:
                q_all[place(block - c * n), :] = piece[0:rows, :]
            k_all[place(block), :] = piece[rows : 2 * rows, :]
            v_all[place(block), :] = piece[2 * rows : 3 * rows, :]
    base = n if high else 0
    row_id = lax.broadcasted_iota(jnp.int32, (rows, rows), 0)
    col_id = lax.broadcasted_iota(jnp.int32, (rows, rows), 1)
    causal = col_id <= row_id
    factor = HD ** (-0.5) * LOG2E
    nt = (((1,), (1,)), ((), ()))
    for b in range(n):
        past = (base + b) * rows
        for h in range(wide // HD):
            cols = slice(h * HD, (h + 1) * HD)
            q = q_all[b * rows : (b + 1) * rows, cols]
            near = lax.dot_general(
                q, k_all[past : past + rows, cols], nt, preferred_element_type=F32
            )
            near = jnp.where(causal, near, NEG)
            peak = jnp.max(near, axis=1, keepdims=True)
            if past:
                far = lax.dot_general(q, k_all[0:past, cols], nt, preferred_element_type=F32)
                peak = jnp.maximum(peak, jnp.max(far, axis=1, keepdims=True))
            w_near = jnp.exp2((near - peak) * factor)
            total = jnp.sum(w_near, axis=1, keepdims=True)
            summed = jnp.dot(
                w_near.astype(BF), v_all[past : past + rows, cols], preferred_element_type=F32
            )
            if past:
                w_far = jnp.exp2((far - peak) * factor)
                total = total + jnp.sum(w_far, axis=1, keepdims=True)
                summed = summed + jnp.dot(
                    w_far.astype(BF), v_all[0:past, cols], preferred_element_type=F32
                )
            owner = n - 1 - b if high else b
            o_all[owner * rows : (owner + 1) * rows, cols] = (summed / total).astype(BF)
    for k in range(n):
        outs[k][...] = o_all[place(rank ^ k), :]


def attend(n, high, rows, ids, pieces):
    wide = pieces[0].shape[1]
    chunks = 2 if high else 1
    pairs = n * (n + 1) // 2 + (n * n if high else 0)
    area = pairs * rows * rows * (wide // HD)
    return pl.pallas_call(
        functools.partial(attend_kernel, n, high, rows),
        out_shape=[jax.ShapeDtypeStruct((rows, wide), BF)] * n,
        in_specs=[sm()] + [vm()] * len(pieces),
        out_specs=[vm()] * n,
        scratch_shapes=[
            VMEM((n * rows, wide), BF),
            VMEM((chunks * n * rows, wide), BF),
            VMEM((chunks * n * rows, wide), BF),
            VMEM((n * rows, wide), BF),
        ],
        compiler_params=params(32),
        cost_estimate=cost(4 * area * HD, 8 * n * rows * wide * chunks, area),
        name="attend_high" if high else "attend_low",
    )(ids, *pieces)


def project_kernel(n, high, indices, has_low, slots_ref, ids_ref, base_ref, w_ref, *refs):
    count = len(indices)
    parts, outs, lhs = refs[:count], refs[count + has_low : -1], refs[-1]
    rank = ids_ref[0]
    me = ids_ref[1]
    rows, width = lhs.shape
    wide = width // n
    if base_ref.dtype == F32:
        total = base_ref[...]
    else:
        half = half_index(slots_ref, ids_ref, high)
        total = base_ref[pl.ds(pl.multiple_of(half * rows, rows), rows), :].astype(F32)
    for index, part in zip(indices, parts):
        for k in range(n):
            cols = pl.ds(pl.multiple_of((rank ^ k) * wide, wide), wide)
            lhs[:, cols] = part[k * rows : (k + 1) * rows, :]
        depth = pl.ds(pl.multiple_of((me ^ index) * width, width), width)
        total = total + jnp.dot(lhs[...], w_ref[depth, :], preferred_element_type=F32)
    outs[0][...] = total
    if len(outs) == 1:
        return
    outs[1][...] = total.astype(BF)
    squares = total * total
    lanes = squares[:, 0:HD]
    for g in range(1, squares.shape[1] // HD):
        lanes = lanes + squares[:, g * HD : (g + 1) * HD]
    if has_low:
        outs[2][:, 0:rows] = refs[count][...]
        outs[2][:, rows : 2 * rows] = jnp.sum(lanes.T, axis=0, keepdims=True)
    else:
        outs[2][...] = jnp.sum(lanes.T, axis=0, keepdims=True)


def project(n, high, slots, ids, base, w_out, parts, indices, final, low_squares=()):
    rows, width = parts[0].shape[0] // n, w_out.shape[1]
    shapes = [jax.ShapeDtypeStruct((rows, width), F32)]
    extra = list(low_squares)
    if final:
        shapes.append(jax.ShapeDtypeStruct((rows, width), BF))
        shapes.append(jax.ShapeDtypeStruct((1, rows * (1 + len(extra))), F32))
    return pl.pallas_call(
        functools.partial(project_kernel, n, high, indices, len(extra)),
        out_shape=shapes,
        in_specs=[sm(), sm()] + [vm()] * (2 + len(parts) + len(extra)),
        out_specs=[vm()] * len(shapes),
        scratch_shapes=[VMEM((rows, width), BF)],
        compiler_params=params(20),
        cost_estimate=cost(2 * rows * width * width * len(parts), 2 * w_out.size * 1.5),
    )(slots, ids, base, w_out, *parts, *extra)


def normed_rows(res, sq_row, gain, model_width):
    rows, width = res.shape
    scale = lax.rsqrt(sq_row / model_width + EPS)
    column = jnp.broadcast_to(scale, (HD, rows)).T
    parts = [
        (res[:, g * HD : (g + 1) * HD] * column * gain[:, g * HD : (g + 1) * HD]).astype(BF)
        for g in range(width // HD)
    ]
    return jnp.concatenate(parts, axis=1)


def split(array):
    high = array.astype(jnp.bfloat16)
    low = (array - high.astype(np.float64)).astype(jnp.bfloat16)
    return high, low


def transform_tables(rows):
    size = 2 * rows
    freq = np.arange(rows)[:, None].astype(np.float64)
    time = np.arange(rows)[None, :].astype(np.float64)
    angle = 2 * np.pi * ((freq * time) % size) / size
    cosine = np.cos(angle)
    sine = -np.sin(angle)
    nyquist = np.where(np.arange(rows) % 2 == 0, 1.0, -1.0)
    sine[0] = nyquist
    forward = np.concatenate([cosine, sine], axis=0)
    late = 2 * np.pi * ((freq * (time + rows)) % size) / size
    back_cos = 2 * np.cos(late)
    back_cos[0] = 1.0
    back_sin = -2 * np.sin(late)
    back_sin[0] = np.where((np.arange(rows) + rows) % 2 == 0, 1.0, -1.0)
    backward = np.concatenate([back_cos, back_sin], axis=0).T / size
    return split(forward), split(backward)


def spectrum_kernel(filters_ref, len_ref, fh_ref, fl_ref, out_ref):
    taps = filters_ref.shape[1]
    lag = lax.broadcasted_iota(jnp.int32, filters_ref.shape, 1)
    used = jnp.where(lag < len_ref[...], filters_ref[...].astype(F32), 0.0).astype(BF)
    nt = (((1,), (1,)), ((), ()))
    fh = fh_ref[:, 0:taps]
    fl = fl_ref[:, 0:taps]
    out_ref[...] = lax.dot_general(fh, used, nt, preferred_element_type=F32) + lax.dot_general(
        fl, used, nt, preferred_element_type=F32
    )


def spectrum(filters, filter_len, forward):
    return pl.pallas_call(
        spectrum_kernel,
        out_shape=jax.ShapeDtypeStruct((forward[0].shape[0], filters.shape[0]), F32),
        in_specs=[vm()] * 4,
        out_specs=vm(),
        compiler_params=params(12),
        cost_estimate=cost(4 * forward[0].size * filters.shape[0], 8 * filters.size),
        name="spectrum",
    )(filters, filter_len.reshape(-1, 1), *forward)


def two(a_high, a_low, b):
    return jnp.dot(a_high, b, preferred_element_type=F32) + jnp.dot(
        a_low, b, preferred_element_type=F32
    )


def frequency_signs(rows):
    row_id = lax.broadcasted_iota(jnp.int32, (rows, 1), 0)
    return row_id == 0, jnp.where(row_id % 2 == 0, 1.0, -1.0)


def late_spectrum(own, fh, fl):
    rows = own.shape[0]
    first, sign = frequency_signs(rows)
    plain = two(fh, fl, own)
    return sign * plain[:rows], jnp.where(first, 1.0, sign) * plain[rows:]


def filtered_spectrum(x_re, x_im, spec):
    rows = x_re.shape[0]
    first, _ = frequency_signs(rows)
    h_re, h_im = spec[:rows], spec[rows:]
    h_cross = jnp.where(first, 0.0, h_im)
    h_own = jnp.where(first, h_im, h_re)
    return jnp.concatenate([x_re * h_re - x_im * h_cross, x_re * h_cross + x_im * h_own], axis=0)


def filtered(x_re, x_im, gh, gl, spec):
    y = filtered_spectrum(x_re, x_im, spec)
    y_high = y.astype(BF)
    y_low = (y - y_high.astype(F32)).astype(BF)
    return two(gh, gl, y_high) + jnp.dot(gh, y_low, preferred_element_type=F32)


def conv_own_kernel(
    model_width, res_low, res_high, sq_ref, spec_ref, gain_ref, skip_ref, fh, fl, gh, gl,
    out_ref, low_ref,
):
    rows = spec_ref.shape[0] // 2
    for high, res_ref in enumerate((res_low, res_high)):
        part = slice(high * rows, (high + 1) * rows)
        res = res_ref[...]
        own = normed_rows(res, sq_ref[:, part], gain_ref[...], model_width)
        if not high:
            low_ref[...] = own
        late_re, late_im = late_spectrum(own, fh[...], fl[...])
        conv = filtered(late_re, late_im, gh[...], gl[...], spec_ref[...])
        out_ref[part, :] = res + conv + skip_ref[...] * own.astype(F32)


def conv_last_kernel(
    n, model_width, slots_ref, ids_ref, part_ref, low_ref, raw_low, raw_high, sq_a, sq_b,
    spec_ref, gain_ref, fh, gh, out_ref,
):
    rows = low_ref.shape[0]
    rank = ids_ref[0]
    odd = rank % 2 == 1
    for high, raw_ref in enumerate((raw_low, raw_high)):
        part = slice(high * rows, (high + 1) * rows)
        squares = jnp.where(odd != (high == 1), sq_a[:, part], sq_b[:, part])
        before = normed_rows(raw_ref[...].astype(F32), squares, gain_ref[...], model_width)
        before = before.astype(F32)
        if high:
            before = jnp.where(rank == n - 1, low_ref[...].astype(F32), before).astype(BF)
        else:
            before = jnp.where(rank == 0, 0.0, before).astype(BF)
        early = jnp.dot(fh[...], before, preferred_element_type=F32)
        y = filtered_spectrum(early[:rows], early[rows:], spec_ref[...]).astype(BF)
        conv = jnp.dot(gh[...], y, preferred_element_type=F32)
        half = half_index(slots_ref, ids_ref, high)
        out_ref[pl.ds(pl.multiple_of(half * rows, rows), rows), :] = (part_ref[part, :] + conv).astype(
            BF
        )


def relayed_piece(own, near, size):
    inner = [(i, i ^ (size - 2)) for i in range(2, size - 2)]
    direct = lax.ppermute(own, "mp", inner)
    ends = [(2, 0), (3, 1), (size - 4, size - 2), (size - 3, size - 1)]
    return direct + lax.ppermute(near, "mp", ends)


def gather_mp(own, size, relay):
    chips = size // 2
    pieces = [own]
    for k in range(1, chips):
        if relay and k == chips - 1:
            pieces.append(relayed_piece(own, pieces[k - 1], size))
        else:
            pieces.append(lax.ppermute(own, "mp", xor_route(size, 2 * k)))
    return pieces


def with_sibling(pieces, size):
    parts = []
    for piece in pieces:
        parts.append(piece)
        parts.append(lax.ppermute(piece, "mp", xor_route(size, 1)))
    return parts


def total_mp(part, size):
    k = 1
    while k < size:
        part = part + lax.ppermute(part, "mp", xor_route(size, k))
        k *= 2
    return part


def ring(n, step):
    return [(i, (i + step) % n) for i in range(n)]


def pairs(n, offset):
    route = []
    for i in range(offset, n, 2):
        route += [(i, (i + 1) % n), ((i + 1) % n, i)]
    return route


def fast_device(
    incoming, queries, key_vecs, value_vecs, w_out, norm_gain, filters, filter_len, skip_gain, slot_map
):
    n = lax.axis_size("seq")
    mp_size = lax.axis_size("mp")
    rows, width = queries.shape[0] // 2, queries.shape[1]
    model_width = w_out.shape[0]
    ids = jnp.stack([lax.axis_index("seq"), lax.axis_index("mp")]).astype(jnp.int32)
    gain = norm_gain.reshape(1, -1)
    skip = skip_gain.reshape(1, -1)
    forward, backward = transform_tables(rows)
    forward = tuple(jnp.asarray(t) for t in forward)
    backward = tuple(jnp.asarray(t) for t in backward)

    def exchange(pieces):
        return [pieces[0]] + [lax.ppermute(pieces[k], "seq", xor_route(n, k)) for k in range(1, n)]

    inputs = (queries, key_vecs, value_vecs)
    low = exchange(pack(n, 0, slot_map, ids, inputs))
    high = exchange(pack(n, 1, slot_map, ids, inputs))
    spec = spectrum(filters, filter_len, forward)

    att_low = exchange(attend(n, 0, rows, ids, low))
    early = gather_mp(att_low[0], mp_size, False)
    late = gather_mp(jnp.concatenate(att_low[1:], axis=0), mp_size, True)
    parts_low = with_sibling([jnp.concatenate(p, axis=0) for p in zip(early, late)], mp_size)
    att_high = exchange(attend(n, 1, rows, ids, low + high))
    early = gather_mp(att_high[0], mp_size, False)
    late = gather_mp(jnp.concatenate(att_high[1:], axis=0), mp_size, False)
    parts_high = with_sibling([jnp.concatenate(p, axis=0) for p in zip(early, late)], mp_size)

    most = mp_size // 2
    every = tuple(range(mp_size))
    res_low, raw_low, sq_low = project(n, 0, slot_map, ids, incoming, w_out, parts_low, every, True)
    raw_low = lax.ppermute(raw_low, "seq", ring(n, 1))
    (base,) = project(
        n, 1, slot_map, ids, incoming, w_out,
        parts_high[:most], every[:most], False,
    )
    res_high, raw_high, squares = project(
        n, 1, slot_map, ids, base, w_out,
        parts_high[most:], every[most:], True, (sq_low,),
    )
    raw_high = lax.ppermute(raw_high, "seq", ring(n, -1))
    squares = total_mp(squares, mp_size)
    sq_a = lax.ppermute(squares, "seq", pairs(n, 0))
    sq_b = lax.ppermute(squares, "seq", pairs(n, 1))
    transforms = forward + backward
    part, norm_low = pl.pallas_call(
        functools.partial(conv_own_kernel, model_width),
        out_shape=[
            jax.ShapeDtypeStruct((2 * rows, width), F32),
            jax.ShapeDtypeStruct((rows, width), BF),
        ],
        in_specs=[vm()] * 10,
        out_specs=[vm()] * 2,
        compiler_params=params(20),
        cost_estimate=cost(20 * rows * rows * width, 24 * rows * width),
        name="conv_own",
    )(res_low, res_high, squares, spec, gain, skip, *transforms)
    return pl.pallas_call(
        functools.partial(conv_last_kernel, n, model_width),
        out_shape=jax.ShapeDtypeStruct((2 * rows, width), BF),
        in_specs=[sm(), sm()] + [vm()] * 10,
        out_specs=vm(),
        compiler_params=params(20),
        cost_estimate=cost(20 * rows * rows * width, 24 * rows * width),
        name="conv_last",
    )(
        slot_map, ids, part, norm_low, raw_low, raw_high, sq_a, sq_b, spec, gain, forward[0], backward[0]
    )


def power_of_two(value):
    return value & (value - 1) == 0


def on_device(*arrays):
    n = lax.axis_size("seq")
    size = lax.axis_size("mp")
    queries, filters = arrays[1], arrays[6]
    rows = queries.shape[0] // 2
    heads = queries.shape[1] // HD
    fits = (
        heads % n == 0
        and power_of_two(n)
        and power_of_two(size)
        and n % 2 == 0
        and size >= 8
        and rows % 256 == 0
        and filters.shape[1] <= rows
    )
    if not fits:
        return general_device(*arrays)
    return fast_device(*arrays)


def solution(mesh):
    placed = (
        P("seq", "mp"),
        P("seq", "mp"),
        P("seq", "mp"),
        P("seq", "mp"),
        P(None, "mp"),
        P("mp"),
        P("mp", None),
        P("mp"),
        P("mp"),
        P(),
    )
    return jax.shard_map(
        on_device, mesh=mesh, in_specs=placed, out_specs=P("seq", "mp"), check_vma=False
    )
```

```python
import functools

import jax
import jax.numpy as jnp
import numpy as np
from jax import lax
from jax.experimental import pallas as pl
from jax.experimental.pallas import tpu as pltpu
from jax.sharding import PartitionSpec as P


HD = 128
EPS = 1e-05
NEG = -1e30
LOG2E = 1.4426950408889634
BF = jnp.bfloat16
F32 = jnp.float32
VMEM = pltpu.VMEM
SMEM = pltpu.SMEM


def shifted(block, axis, distance):
    devices = range(lax.axis_size(axis))
    route = [(i - distance, i) for i in devices if i - distance in devices]
    return lax.ppermute(block, axis, route)


def block_update(running, query_heads, query_pos, key_part, value_part, key_pos):
    peak_now, total_now, accum_now = running
    key_count = key_part.shape[0]
    head_count = query_heads.shape[1]
    key_heads = key_part.reshape(key_count, head_count, HD)
    value_heads = value_part.reshape(key_count, head_count, HD)
    scores = jnp.einsum(
        "thd,shd->ths", query_heads, key_heads, preferred_element_type=F32
    ) * HD ** (-0.5)
    allowed = key_pos[None, None, :] <= query_pos[:, None, None]
    masked = jnp.where(allowed, scores, NEG)
    peak_next = jnp.maximum(peak_now, jnp.max(masked, axis=2))
    weights = jnp.where(allowed, jnp.exp(masked - peak_next[:, :, None]), 0.0)
    factor = jnp.exp(peak_now - peak_next)
    total_next = total_now * factor + jnp.sum(weights, axis=2)
    summed = jnp.einsum(
        "ths,shd->thd", weights.astype(BF), value_heads, preferred_element_type=F32
    )
    return (peak_next, total_next, accum_now * factor[:, :, None] + summed)


def attend_keys(running, query_heads, query_pos, key_part, value_part, key_pos, block_rows):
    block_count = key_part.shape[0] // block_rows

    def attend_advance(state, item):
        return block_update(state, query_heads, query_pos, *item), None

    stacked = (
        key_part.reshape(block_count, block_rows, -1),
        value_part.reshape(block_count, block_rows, -1),
        key_pos.reshape(block_count, block_rows),
    )
    running, _ = lax.scan(attend_advance, running, stacked)
    return running


def causal_window(extended, taps_lag):
    pair_count, twice, width = extended.shape
    length = twice // 2
    tap_count = taps_lag.shape[0]
    inner = int(np.gcd(tap_count, 16))

    def causal_advance(block, accum):
        base = block * inner
        window = lax.dynamic_slice_in_dim(
            extended, length - base - inner + 1, length + inner - 1, 1
        ).astype(F32)
        tap_block = lax.dynamic_slice_in_dim(taps_lag, base, inner, 0).astype(F32)
        for lag in range(inner):
            offset = inner - 1 - lag
            accum = accum + tap_block[lag][None, None, :] * window[:, offset : offset + length]
        return accum

    start = jnp.zeros((pair_count, length, width), F32)
    return lax.fori_loop(0, tap_count // inner, causal_advance, start)


def general_device(
    incoming, queries, key_vecs, value_vecs, w_out, norm_gain, filters, filter_len, skip_gain, slot_map
):
    tok_rows, local_width = queries.shape
    span_rows = tok_rows // 2
    head_count = local_width // HD
    model_width = w_out.shape[0]
    all_rows = slot_map.shape[0] * span_rows
    row_ids = jnp.arange(all_rows, dtype=jnp.int32)
    position = (
        jnp.repeat(slot_map, span_rows, total_repeat_length=all_rows) * span_rows
        + row_ids % span_rows
    )
    seq_rank = lax.axis_index("seq")
    seq_size = lax.axis_size("seq")
    own_pos = lax.dynamic_slice_in_dim(position, seq_rank * tok_rows, tok_rows)
    query_heads = queries.reshape(tok_rows, head_count, HD)
    keys_all = lax.all_gather(key_vecs, "seq", axis=0, tiled=True)
    values_all = lax.all_gather(value_vecs, "seq", axis=0, tiled=True)
    running = attend_keys(
        (
            jnp.full((tok_rows, head_count), NEG, F32),
            jnp.zeros((tok_rows, head_count), F32),
            jnp.zeros((tok_rows, head_count, HD), F32),
        ),
        query_heads,
        own_pos,
        keys_all,
        values_all,
        position,
        2 * tok_rows,
    )
    attention = (running[2] / running[1][:, :, None]).reshape(-1, local_width).astype(BF)
    projected = jnp.dot(
        lax.all_gather(attention, "mp", axis=1, tiled=True), w_out, preferred_element_type=F32
    )
    residual = incoming.astype(F32) + projected
    square_total = lax.psum(jnp.sum(residual * residual, axis=1), "mp")
    scale = lax.rsqrt(square_total / model_width + EPS)
    normed = (residual * scale[:, None] * norm_gain[None, :]).astype(BF)
    tap_count = filters.shape[1]
    taps = jnp.where(
        jnp.arange(tap_count, dtype=jnp.int32)[None, :] < filter_len[:, None],
        filters,
        jnp.zeros((), filters.dtype),
    )
    pair_ids = lax.dynamic_slice_in_dim(slot_map, 2 * seq_rank, 2)
    low_first = pair_ids[0] < pair_ids[1]
    slots = normed.reshape(2, span_rows, local_width)
    low_rows = jnp.where(low_first, slots[0], slots[1])
    high_rows = jnp.where(low_first, slots[1], slots[0])
    own_pair = jnp.stack([low_rows, high_rows])
    low_before = shifted(low_rows, "seq", 1)
    high_before = shifted(high_rows, "seq", -1)
    high_before = jnp.where(seq_rank == seq_size - 1, low_rows, high_before)
    before_pair = jnp.stack([low_before, high_before])
    conv_pair = causal_window(jnp.concatenate([before_pair, own_pair], axis=1), taps.T)
    conv_slots = jnp.where(low_first, conv_pair, conv_pair[::-1])
    conv_rows = conv_slots.reshape(tok_rows, local_width)
    layer_out = residual + conv_rows + skip_gain[None, :] * normed.astype(F32)
    return layer_out.astype(BF)


def params(megabytes=20):
    return pltpu.CompilerParams(vmem_limit_bytes=megabytes << 20)


def cost(flops, moved, exps=0):
    return pl.CostEstimate(flops=int(flops), bytes_accessed=int(moved), transcendentals=int(exps))


def vm():
    return pl.BlockSpec(memory_space=VMEM)


def sm():
    return pl.BlockSpec(memory_space=SMEM)


def xor_route(count, k):
    return [(i, i ^ k) for i in range(count)]


def half_index(slots_ref, ids_ref, high):
    rank = ids_ref[0]
    first_is_high = slots_ref[2 * rank] > slots_ref[2 * rank + 1]
    return jnp.where(first_is_high, 1 - high, high).astype(jnp.int32)


def pack_kernel(n, high, slots_ref, ids_ref, q_ref, k_ref, v_ref, *rest):
    outs, sem = rest[:n], rest[n]
    rank = ids_ref[0]
    rows = outs[0].shape[0] // 3
    wide = outs[0].shape[1]
    half = half_index(slots_ref, ids_ref, high)
    source_rows = pl.ds(pl.multiple_of(half * rows, rows), rows)
    copies = []
    for k in range(n):
        cols = pl.ds(pl.multiple_of((rank ^ k) * wide, wide), wide)
        for a, ref in enumerate((q_ref, k_ref, v_ref)):
            copy = pltpu.make_async_copy(
                ref.at[source_rows, cols],
                outs[k].at[a * rows : (a + 1) * rows, :],
                sem.at[k, a],
            )
            copy.start()
            copies.append(copy)
    for copy in copies:
        copy.wait()


def in_hbm(array):
    return pltpu.with_memory_space_constraint(array, pltpu.HBM)


def pack(n, high, slots, ids, arrays):
    rows, width = arrays[0].shape[0] // 2, arrays[0].shape[1]
    piece = jax.ShapeDtypeStruct((3 * rows, width // n), BF)
    return pl.pallas_call(
        functools.partial(pack_kernel, n, high),
        out_shape=[piece] * n,
        in_specs=[sm(), sm()] + [pl.BlockSpec(memory_space=pltpu.HBM)] * 3,
        out_specs=[vm()] * n,
        scratch_shapes=[pltpu.SemaphoreType.DMA((n, 3))],
        compiler_params=params(8),
        cost_estimate=cost(0, 12 * rows * width),
    )(in_hbm(slots), ids, *(in_hbm(x) for x in arrays))


def attend_kernel(n, high, rows, ids_ref, *refs):
    chunks = 2 if high else 1
    ins = refs[: chunks * n]
    outs = refs[chunks * n : chunks * n + n]
    q_all, k_all, v_all, o_all = refs[chunks * n + n :]
    rank = ids_ref[0]
    wide = outs[0].shape[1]

    def place(block):
        return pl.ds(pl.multiple_of(block * rows, rows), rows)

    for c in range(chunks):
        for k in range(n):
            source = rank ^ k
            block = source if c == 0 else 2 * n - 1 - source
            piece = ins[c * n + k]
            if c == chunks - 1:
                q_all[place(block - c * n), :] = piece[0:rows, :]
            k_all[place(block), :] = piece[rows : 2 * rows, :]
            v_all[place(block), :] = piece[2 * rows : 3 * rows, :]
    base = n if high else 0
    row_id = lax.broadcasted_iota(jnp.int32, (rows, rows), 0)
    col_id = lax.broadcasted_iota(jnp.int32, (rows, rows), 1)
    causal = col_id <= row_id
    factor = HD ** (-0.5) * LOG2E
    nt = (((1,), (1,)), ((), ()))
    for b in range(n):
        past = (base + b) * rows
        for h in range(wide // HD):
            cols = slice(h * HD, (h + 1) * HD)
            q = q_all[b * rows : (b + 1) * rows, cols]
            near = lax.dot_general(
                q, k_all[past : past + rows, cols], nt, preferred_element_type=F32
            )
            near = jnp.where(causal, near, NEG)
            peak = jnp.max(near, axis=1, keepdims=True)
            if past:
                far = lax.dot_general(q, k_all[0:past, cols], nt, preferred_element_type=F32)
                peak = jnp.maximum(peak, jnp.max(far, axis=1, keepdims=True))
            w_near = jnp.exp2((near - peak) * factor)
            total = jnp.sum(w_near, axis=1, keepdims=True)
            summed = jnp.dot(
                w_near.astype(BF), v_all[past : past + rows, cols], preferred_element_type=F32
            )
            if past:
                w_far = jnp.exp2((far - peak) * factor)
                total = total + jnp.sum(w_far, axis=1, keepdims=True)
                summed = summed + jnp.dot(
                    w_far.astype(BF), v_all[0:past, cols], preferred_element_type=F32
                )
            owner = n - 1 - b if high else b
            o_all[owner * rows : (owner + 1) * rows, cols] = (summed / total).astype(BF)
    for k in range(n):
        outs[k][...] = o_all[place(rank ^ k), :]


def attend(n, high, rows, ids, pieces):
    wide = pieces[0].shape[1]
    chunks = 2 if high else 1
    pairs = n * (n + 1) // 2 + (n * n if high else 0)
    area = pairs * rows * rows * (wide // HD)
    return pl.pallas_call(
        functools.partial(attend_kernel, n, high, rows),
        out_shape=[jax.ShapeDtypeStruct((rows, wide), BF)] * n,
        in_specs=[sm()] + [vm()] * len(pieces),
        out_specs=[vm()] * n,
        scratch_shapes=[
            VMEM((n * rows, wide), BF),
            VMEM((chunks * n * rows, wide), BF),
            VMEM((chunks * n * rows, wide), BF),
            VMEM((n * rows, wide), BF),
        ],
        compiler_params=params(32),
        cost_estimate=cost(4 * area * HD, 8 * n * rows * wide * chunks, area),
        name="attend_high" if high else "attend_low",
    )(ids, *pieces)


def project_kernel(n, high, indices, has_low, slots_ref, ids_ref, base_ref, w_ref, *refs):
    count = len(indices)
    parts, outs, lhs = refs[:count], refs[count + has_low : -1], refs[-1]
    rank = ids_ref[0]
    me = ids_ref[1]
    rows, width = lhs.shape
    wide = width // n
    if base_ref.dtype == F32:
        total = base_ref[...]
    else:
        half = half_index(slots_ref, ids_ref, high)
        total = base_ref[pl.ds(pl.multiple_of(half * rows, rows), rows), :].astype(F32)
    for index, part in zip(indices, parts):
        for k in range(n):
            cols = pl.ds(pl.multiple_of((rank ^ k) * wide, wide), wide)
            lhs[:, cols] = part[k * rows : (k + 1) * rows, :]
        depth = pl.ds(pl.multiple_of((me ^ index) * width, width), width)
        total = total + jnp.dot(lhs[...], w_ref[depth, :], preferred_element_type=F32)
    outs[0][...] = total
    if len(outs) == 1:
        return
    outs[1][...] = total.astype(BF)
    squares = total * total
    lanes = squares[:, 0:HD]
    for g in range(1, squares.shape[1] // HD):
        lanes = lanes + squares[:, g * HD : (g + 1) * HD]
    if has_low:
        outs[2][:, 0:rows] = refs[count][...]
        outs[2][:, rows : 2 * rows] = jnp.sum(lanes.T, axis=0, keepdims=True)
    else:
        outs[2][...] = jnp.sum(lanes.T, axis=0, keepdims=True)


def project(n, high, slots, ids, base, w_out, parts, indices, final, low_squares=()):
    rows, width = parts[0].shape[0] // n, w_out.shape[1]
    shapes = [jax.ShapeDtypeStruct((rows, width), F32)]
    extra = list(low_squares)
    if final:
        shapes.append(jax.ShapeDtypeStruct((rows, width), BF))
        shapes.append(jax.ShapeDtypeStruct((1, rows * (1 + len(extra))), F32))
    return pl.pallas_call(
        functools.partial(project_kernel, n, high, indices, len(extra)),
        out_shape=shapes,
        in_specs=[sm(), sm()] + [vm()] * (2 + len(parts) + len(extra)),
        out_specs=[vm()] * len(shapes),
        scratch_shapes=[VMEM((rows, width), BF)],
        compiler_params=params(20),
        cost_estimate=cost(2 * rows * width * width * len(parts), 2 * w_out.size * 1.5),
    )(slots, ids, base, w_out, *parts, *extra)


def normed_rows(res, sq_row, gain, model_width):
    rows, width = res.shape
    scale = lax.rsqrt(sq_row / model_width + EPS)
    column = jnp.broadcast_to(scale, (HD, rows)).T
    parts = [
        (res[:, g * HD : (g + 1) * HD] * column * gain[:, g * HD : (g + 1) * HD]).astype(BF)
        for g in range(width // HD)
    ]
    return jnp.concatenate(parts, axis=1)


def split(array):
    high = array.astype(jnp.bfloat16)
    low = (array - high.astype(np.float64)).astype(jnp.bfloat16)
    return high, low


def transform_tables(rows):
    size = 2 * rows
    freq = np.arange(rows)[:, None].astype(np.float64)
    time = np.arange(rows)[None, :].astype(np.float64)
    angle = 2 * np.pi * ((freq * time) % size) / size
    cosine = np.cos(angle)
    sine = -np.sin(angle)
    nyquist = np.where(np.arange(rows) % 2 == 0, 1.0, -1.0)
    sine[0] = nyquist
    forward = np.concatenate([cosine, sine], axis=0)
    late = 2 * np.pi * ((freq * (time + rows)) % size) / size
    back_cos = 2 * np.cos(late)
    back_cos[0] = 1.0
    back_sin = -2 * np.sin(late)
    back_sin[0] = np.where((np.arange(rows) + rows) % 2 == 0, 1.0, -1.0)
    backward = np.concatenate([back_cos, back_sin], axis=0).T / size
    return split(forward), split(backward)


def spectrum_kernel(filters_ref, len_ref, fh_ref, fl_ref, out_ref):
    taps = filters_ref.shape[1]
    lag = lax.broadcasted_iota(jnp.int32, filters_ref.shape, 1)
    used = jnp.where(lag < len_ref[...], filters_ref[...].astype(F32), 0.0).astype(BF)
    nt = (((1,), (1,)), ((), ()))
    fh = fh_ref[:, 0:taps]
    fl = fl_ref[:, 0:taps]
    out_ref[...] = lax.dot_general(fh, used, nt, preferred_element_type=F32) + lax.dot_general(
        fl, used, nt, preferred_element_type=F32
    )


def spectrum(filters, filter_len, forward):
    return pl.pallas_call(
        spectrum_kernel,
        out_shape=jax.ShapeDtypeStruct((forward[0].shape[0], filters.shape[0]), F32),
        in_specs=[vm()] * 4,
        out_specs=vm(),
        compiler_params=params(12),
        cost_estimate=cost(4 * forward[0].size * filters.shape[0], 8 * filters.size),
        name="spectrum",
    )(filters, filter_len.reshape(-1, 1), *forward)


def two(a_high, a_low, b):
    return jnp.dot(a_high, b, preferred_element_type=F32) + jnp.dot(
        a_low, b, preferred_element_type=F32
    )


def frequency_signs(rows):
    row_id = lax.broadcasted_iota(jnp.int32, (rows, 1), 0)
    return row_id == 0, jnp.where(row_id % 2 == 0, 1.0, -1.0)


def late_spectrum(own, fh, fl):
    rows = own.shape[0]
    first, sign = frequency_signs(rows)
    plain = two(fh, fl, own)
    return sign * plain[:rows], jnp.where(first, 1.0, sign) * plain[rows:]


def filtered_spectrum(x_re, x_im, spec):
    rows = x_re.shape[0]
    first, _ = frequency_signs(rows)
    h_re, h_im = spec[:rows], spec[rows:]
    h_cross = jnp.where(first, 0.0, h_im)
    h_own = jnp.where(first, h_im, h_re)
    return jnp.concatenate([x_re * h_re - x_im * h_cross, x_re * h_cross + x_im * h_own], axis=0)


def filtered(x_re, x_im, gh, gl, spec):
    y = filtered_spectrum(x_re, x_im, spec)
    y_high = y.astype(BF)
    y_low = (y - y_high.astype(F32)).astype(BF)
    return two(gh, gl, y_high) + jnp.dot(gh, y_low, preferred_element_type=F32)


def conv_own_kernel(
    model_width, res_low, res_high, sq_ref, spec_ref, gain_ref, skip_ref, fh, fl, gh, gl,
    out_ref, low_ref,
):
    rows = spec_ref.shape[0] // 2
    for high, res_ref in enumerate((res_low, res_high)):
        part = slice(high * rows, (high + 1) * rows)
        res = res_ref[...]
        own = normed_rows(res, sq_ref[:, part], gain_ref[...], model_width)
        if not high:
            low_ref[...] = own
        late_re, late_im = late_spectrum(own, fh[...], fl[...])
        conv = filtered(late_re, late_im, gh[...], gl[...], spec_ref[...])
        out_ref[part, :] = res + conv + skip_ref[...] * own.astype(F32)


def conv_last_kernel(
    n, model_width, slots_ref, ids_ref, part_ref, low_ref, raw_low, raw_high, sq_a, sq_b,
    spec_ref, gain_ref, fh, gh, out_ref,
):
    rows = low_ref.shape[0]
    rank = ids_ref[0]
    odd = rank % 2 == 1
    for high, raw_ref in enumerate((raw_low, raw_high)):
        part = slice(high * rows, (high + 1) * rows)
        squares = jnp.where(odd != (high == 1), sq_a[:, part], sq_b[:, part])
        before = normed_rows(raw_ref[...].astype(F32), squares, gain_ref[...], model_width)
        before = before.astype(F32)
        if high:
            before = jnp.where(rank == n - 1, low_ref[...].astype(F32), before).astype(BF)
        else:
            before = jnp.where(rank == 0, 0.0, before).astype(BF)
        early = jnp.dot(fh[...], before, preferred_element_type=F32)
        y = filtered_spectrum(early[:rows], early[rows:], spec_ref[...]).astype(BF)
        conv = jnp.dot(gh[...], y, preferred_element_type=F32)
        half = half_index(slots_ref, ids_ref, high)
        out_ref[pl.ds(pl.multiple_of(half * rows, rows), rows), :] = (part_ref[part, :] + conv).astype(
            BF
        )


def relayed_piece(own, near, size):
    inner = [(i, i ^ (size - 2)) for i in range(2, size - 2)]
    direct = lax.ppermute(own, "mp", inner)
    ends = [(2, 0), (3, 1), (size - 4, size - 2), (size - 3, size - 1)]
    return direct + lax.ppermute(near, "mp", ends)


def gather_mp(own, size, relay):
    chips = size // 2
    pieces = [own]
    for k in range(1, chips):
        if relay and k == chips - 1:
            pieces.append(relayed_piece(own, pieces[k - 1], size))
        else:
            pieces.append(lax.ppermute(own, "mp", xor_route(size, 2 * k)))
    return pieces


def with_sibling(pieces, size):
    parts = []
    for piece in pieces:
        parts.append(piece)
        parts.append(lax.ppermute(piece, "mp", xor_route(size, 1)))
    return parts


def total_mp(part, size):
    k = 1
    while k < size:
        part = part + lax.ppermute(part, "mp", xor_route(size, k))
        k *= 2
    return part


def ring(n, step):
    return [(i, (i + step) % n) for i in range(n)]


def pairs(n, offset):
    route = []
    for i in range(offset, n, 2):
        route += [(i, (i + 1) % n), ((i + 1) % n, i)]
    return route


def fast_device(
    incoming, queries, key_vecs, value_vecs, w_out, norm_gain, filters, filter_len, skip_gain, slot_map
):
    n = lax.axis_size("seq")
    mp_size = lax.axis_size("mp")
    rows, width = queries.shape[0] // 2, queries.shape[1]
    model_width = w_out.shape[0]
    ids = jnp.stack([lax.axis_index("seq"), lax.axis_index("mp")]).astype(jnp.int32)
    gain = norm_gain.reshape(1, -1)
    skip = skip_gain.reshape(1, -1)
    forward, backward = transform_tables(rows)
    forward = tuple(jnp.asarray(t) for t in forward)
    backward = tuple(jnp.asarray(t) for t in backward)

    def exchange(pieces):
        return [pieces[0]] + [lax.ppermute(pieces[k], "seq", xor_route(n, k)) for k in range(1, n)]

    inputs = (queries, key_vecs, value_vecs)
    low = exchange(pack(n, 0, slot_map, ids, inputs))
    high = exchange(pack(n, 1, slot_map, ids, inputs))
    spec = spectrum(filters, filter_len, forward)

    att_low = exchange(attend(n, 0, rows, ids, low))
    early = gather_mp(att_low[0], mp_size, False)
    late = gather_mp(jnp.concatenate(att_low[1:], axis=0), mp_size, True)
    parts_low = with_sibling([jnp.concatenate(p, axis=0) for p in zip(early, late)], mp_size)
    att_high = exchange(attend(n, 1, rows, ids, low + high))
    middle = n // 2
    own_a = jnp.concatenate(att_high[:middle], axis=0)
    own_b = jnp.concatenate(att_high[middle:], axis=0)
    early = gather_mp(own_a, mp_size, True)
    late = gather_mp(own_b, mp_size, False)
    parts_high = with_sibling([jnp.concatenate(p, axis=0) for p in zip(early, late)], mp_size)

    most = mp_size // 2
    every = tuple(range(mp_size))
    res_low, raw_low, sq_low = project(n, 0, slot_map, ids, incoming, w_out, parts_low, every, True)
    raw_low = lax.ppermute(raw_low, "seq", ring(n, 1))
    (base,) = project(
        n, 1, slot_map, ids, incoming, w_out,
        parts_high[:most], every[:most], False,
    )
    res_high, raw_high, squares = project(
        n, 1, slot_map, ids, base, w_out,
        parts_high[most:], every[most:], True, (sq_low,),
    )
    raw_high = lax.ppermute(raw_high, "seq", ring(n, -1))
    squares = total_mp(squares, mp_size)
    sq_a = lax.ppermute(squares, "seq", pairs(n, 0))
    sq_b = lax.ppermute(squares, "seq", pairs(n, 1))
    transforms = forward + backward
    part, norm_low = pl.pallas_call(
        functools.partial(conv_own_kernel, model_width),
        out_shape=[
            jax.ShapeDtypeStruct((2 * rows, width), F32),
            jax.ShapeDtypeStruct((rows, width), BF),
        ],
        in_specs=[vm()] * 10,
        out_specs=[vm()] * 2,
        compiler_params=params(20),
        cost_estimate=cost(20 * rows * rows * width, 24 * rows * width),
        name="conv_own",
    )(res_low, res_high, squares, spec, gain, skip, *transforms)
    return pl.pallas_call(
        functools.partial(conv_last_kernel, n, model_width),
        out_shape=jax.ShapeDtypeStruct((2 * rows, width), BF),
        in_specs=[sm(), sm()] + [vm()] * 10,
        out_specs=vm(),
        compiler_params=params(20),
        cost_estimate=cost(20 * rows * rows * width, 24 * rows * width),
        name="conv_last",
    )(
        slot_map, ids, part, norm_low, raw_low, raw_high, sq_a, sq_b, spec, gain, forward[0], backward[0]
    )


def power_of_two(value):
    return value & (value - 1) == 0


def on_device(*arrays):
    n = lax.axis_size("seq")
    size = lax.axis_size("mp")
    queries, filters = arrays[1], arrays[6]
    rows = queries.shape[0] // 2
    heads = queries.shape[1] // HD
    fits = (
        heads % n == 0
        and power_of_two(n)
        and power_of_two(size)
        and n % 2 == 0
        and size >= 8
        and rows % 256 == 0
        and filters.shape[1] <= rows
    )
    if not fits:
        return general_device(*arrays)
    return fast_device(*arrays)


def solution(mesh):
    placed = (
        P("seq", "mp"),
        P("seq", "mp"),
        P("seq", "mp"),
        P("seq", "mp"),
        P(None, "mp"),
        P("mp"),
        P("mp", None),
        P("mp"),
        P("mp"),
        P(),
    )
    return jax.shard_map(
        on_device, mesh=mesh, in_specs=placed, out_specs=P("seq", "mp"), check_vma=False
    )
```
